1024 devices in a mesh: blk: 32 (over x_hi, y, core), panel: 32 (over z, x_lo).
Axes of the slice: x: 4 (x_hi: 2, x_lo: 2; x = x_hi * 2 + x_lo), y: 8, z: 16, core: 2. Of those that a mesh axis runs over, the one named last changes fastest.
Arguments:
- integrals: bfloat16 [8192, 32768], P('blk', 'panel'), may hold values from -0.09375 to 0.09375
- amplitudes: bfloat16 [1600, 32768], P('blk', 'panel'), may hold values from -6 to 6
- ab_irrep: int32 [128], P('blk'), may hold values from 0 to 7
- cd_irrep: int32 [512], P('panel'), may hold values from 0 to 7
- occ_irrep: int32 [40], replicated, may hold values from 0 to 7
Outputs:
- ladder: float32 [8192, 1600], P(('blk', 'panel'))
The draws below stay inside these ranges and needn't reach their ends.
Inputs may be any that keep to these rules, and one draw needn't show every extreme that they name: `ab_irrep`: irreps of virtual pair tiles. `cd_irrep`: irreps of virtual pair tiles.
All inputs are finite; a program needn't handle non-finite values.
Results may differ from the reference program's by a relative error of at most 0.0003.
Values may be sent and summed in bfloat16 or wider, within the bound.
No kernel may reach another device: no remote copies, remote signals or barrier semaphores. Data moves between devices by JAX's collectives and lax.ppermute only.
A program may use at most 64 MiB of HBM per device.

```python
import math
import jax
import jax.numpy as jnp
import numpy as np

TW = 64
IRREPS = 8
OCC = 40
IJ = 1600
AB = 8192
CD = 32768


def plant(drawn, rng, least, high):
    index_at = [jax.random.randint(jax.random.fold_in(rng, axis), (), 0, length) for axis, length in enumerate(drawn.shape)]
    main_axis = drawn.shape.index(max(drawn.shape))
    neighbour = index_at[:main_axis] + [(index_at[main_axis] + 1) % drawn.shape[main_axis]] + index_at[main_axis + 1:]
    return drawn.at[tuple(index_at)].set(least).at[tuple(neighbour)].set(high)


def level_of(key, shape, shards, smallest, largest):
    def one(dim, parts):
        heights = jax.random.uniform(jax.random.fold_in(jax.random.fold_in(key, 6), dim), (parts,), jnp.float32, smallest / len(shards), largest / len(shards))
        return jnp.repeat(jnp.exp(heights), shape[dim] // parts).reshape((-1,) + (1,) * (len(shape) - dim - 1))

    gain = one(*shards[0])
    for cut in shards[1:]:
        gain = gain * one(*cut)
    return gain


def cumulative_ranks(number_of, skew):
    loads = [(1 << 20) // math.isqrt(standing ** skew) + 1 for standing in range(1, number_of + 1)]
    scale = 1 + sum(loads) // (1 << 30)
    return np.cumsum(np.array([max(1, weight // scale) for weight in loads]))


def ranked(own_key, shape, amount, skew):
    grid = cumulative_ranks(amount, skew)
    lot = jax.random.randint(jax.random.fold_in(own_key, 1), shape, 0, int(grid[amount - 1]))
    grade = jnp.searchsorted(jnp.asarray(grid, jnp.int32), lot, side="right")
    return jax.random.permutation(jax.random.fold_in(own_key, 2), amount)[grade].astype(jnp.int32)


def centred(own_key, dims, width, bound, shards=(), held_as=jnp.bfloat16):
    array = jax.random.normal(own_key, dims, jnp.float32) * width
    if len(shards) > 0:
        array = level_of(own_key, dims, shards, -0.22, 0.18) * array
    return jnp.clip(array, min=-bound, max=bound).astype(held_as)


def setup_inputs(seed: int = 0) -> dict:
    splits = jax.random.split(jax.random.key(seed), 6)
    return {
        "integrals": centred(splits[0], (AB, CD), (CD // 8) ** -0.5, 0.09375, ((0, 32), (1, 32))),
        "amplitudes": centred(splits[1], (IJ, CD), 1.0, 6.0, ((0, 32), (1, 32))),
        "ab_irrep": plant(jax.random.randint(splits[2], (AB // TW,), 0, IRREPS), jax.random.fold_in(splits[2], 1), 0, IRREPS - 1).astype(jnp.int32),
        "cd_irrep": plant(jax.random.randint(splits[3], (CD // TW,), 0, IRREPS), jax.random.fold_in(splits[3], 1), 0, IRREPS - 1).astype(jnp.int32),
        "occ_irrep": plant(ranked(splits[4], (OCC,), IRREPS, 3), jax.random.fold_in(splits[4], 3), 0, IRREPS - 1).astype(jnp.int32),
    }


def reference(integrals, amplitudes, ab_irrep, cd_irrep, occ_irrep):
    row_irrep = jnp.repeat(ab_irrep, TW)
    col_irrep = jnp.repeat(cd_irrep, TW)
    first_irrep = jnp.repeat(occ_irrep, OCC)
    second_irrep = jnp.tile(occ_irrep, OCC)
    pair_irrep = jnp.bitwise_xor(first_irrep, second_irrep)
    vmasked = jnp.where(row_irrep[:, None] == col_irrep[None, :], integrals, jnp.zeros((), integrals.dtype))
    tmasked = jnp.where(pair_irrep[:, None] == col_irrep[None, :], amplitudes, jnp.zeros((), amplitudes.dtype))
    return jnp.dot(vmasked, tmasked.T, preferred_element_type=jnp.float32)
```

```python
import functools

import jax
import jax.numpy as jnp
from jax import lax
from jax.experimental import pallas as pl
from jax.experimental.pallas import tpu as pltpu
from jax.sharding import Mesh
from jax.sharding import PartitionSpec as P


TW = 64
IRREPS = 8
OCC = 40
IJ = 1600
BLK = ("blk_0", "blk_1", "blk_2")
BLK_PANEL = ("blk_0", "blk_1", "blk_2", "panel")
CHIPS = ("blk_0", "blk_1")

PAIRS = 50
ROWS = 56
SOURCES = 16
HALF = SOURCES * ROWS
WIDE = 8
COLS = 640
LIST = 2304
KEPT = 16

SMEM = pl.BlockSpec(memory_space=pltpu.SMEM)
VMEM = pl.BlockSpec(memory_space=pltpu.VMEM)
NT = (((1,), (1,)), ((), ()))


def places(cd_ref):
    irreps = [cd_ref[t] for t in range(16)]
    ranks = []
    for t in range(16):
        rank = jnp.int32(0)
        for earlier in range(t):
            rank += jnp.where(irreps[earlier] == irreps[t], 1, 0)
        ranks.append(rank)
    return irreps, ranks


def fill_chooser(choose, ranks, turn):
    width = WIDE * TW
    row = lax.broadcasted_iota(jnp.int32, (TW, width), 0)
    col = lax.broadcasted_iota(jnp.int32, (TW, width), 1)
    place = jnp.where(col % TW == row, col // TW + turn * WIDE, -1)
    for t in range(16):
        hit = jnp.where(place == ranks[t], 1.0, 0.0)
        choose[t * TW : (t + 1) * TW, :] = hit.astype(jnp.bfloat16)


def column_irreps(irreps):
    lane = lax.broadcasted_iota(jnp.int32, (1, 16 * TW), 1) // TW
    found = jnp.zeros((1, 16 * TW), jnp.int32)
    for t in range(16):
        found = jnp.where(lane == t, irreps[t], found)
    return found


def pack(values, row_irrep, col_irrep, choose):
    kept = jnp.where(row_irrep == col_irrep, values.astype(jnp.float32), 0.0)
    return jnp.dot(
        kept.astype(jnp.bfloat16), choose[...], preferred_element_type=jnp.float32
    ).astype(jnp.bfloat16)


def send_kernel(turn, t_ref, cd_ref, occ_ref, out_ref, choose):
    blk = lax.axis_index("blk_0") * 16 + lax.axis_index("blk_1") * 2 + lax.axis_index("blk_2")
    irreps, ranks = places(cd_ref)
    fill_chooser(choose, ranks, turn)
    first = blk * PAIRS
    row = lax.broadcasted_iota(jnp.int32, (PAIRS, 1), 0)
    row_irrep = jnp.zeros((PAIRS, 1), jnp.int32)
    for m in range(PAIRS):
        pair = first + m
        left = pair // OCC
        irrep = jnp.bitwise_xor(occ_ref[left], occ_ref[pair - left * OCC])
        row_irrep = jnp.where(row == m, irrep, row_irrep)
    packed = pack(t_ref[...], row_irrep, column_irreps(irreps), choose)
    for s in range(SOURCES):
        out_ref[s, :PAIRS, :] = packed
        out_ref[s, PAIRS:, :] = jnp.zeros((ROWS - PAIRS, WIDE * TW), jnp.bfloat16)


def pack_rows_kernel(turn, v_ref, ab_ref, cd_ref, out_ref, choose):
    irreps, ranks = places(cd_ref)
    fill_chooser(choose, ranks, turn)
    row = lax.broadcasted_iota(jnp.int32, (4 * TW, 1), 0) // TW
    row_irrep = jnp.zeros((4 * TW, 1), jnp.int32)
    for i in range(4):
        row_irrep = jnp.where(row == i, ab_ref[i], row_irrep)
    out_ref[...] = pack(v_ref[...], row_irrep, column_irreps(irreps), choose)


def tables_kernel(cd_ref, occ_ref, list_ref, code_ref, kept_ref, orbitals, count):
    core = lax.axis_index("blk_2")
    for g in range(IRREPS):
        orbitals[g] = 0

    @pl.loop(0, OCC)
    def _(i):
        g = occ_ref[i]
        orbitals[g] = orbitals[g] + 1

    start = jnp.int32(0)
    most = jnp.int32(0)
    for g in range(IRREPS):
        pairs = jnp.int32(0)
        for h in range(IRREPS):
            pairs += orbitals[h] * orbitals[g ^ h]
        kept_ref[g] = start
        count[g] = start
        start += pairs
        most = jnp.maximum(most, pairs)
    _, ranks = places(cd_ref)
    widest = ranks[0]
    for rank in ranks[1:]:
        widest = jnp.maximum(widest, rank)
    kept_ref[8] = start
    kept_ref[9] = widest + 1
    kept_ref[10] = most
    for k in range(11, KEPT):
        kept_ref[k] = 0

    @pl.loop(0, OCC)
    def _(i):
        left = occ_ref[i]

        @pl.loop(0, OCC)
        def _(j):
            pair = i * OCC + j
            irrep = jnp.bitwise_xor(left, occ_ref[j])
            at = count[irrep]
            count[irrep] = at + 1
            source = pair // PAIRS
            other = jnp.bitwise_xor(source & 1, core)
            list_ref[at] = (other * SOURCES + (source >> 1)) * ROWS + pair - source * PAIRS
            code_ref[pair] = (at - kept_ref[irrep]) * IRREPS + irrep

    @pl.loop(IJ, LIST)
    def _(k):
        list_ref[k] = 0


def product_kernel(turns, round_ref, *refs):
    halves, weights = refs[: 2 * turns], refs[2 * turns : 3 * turns]
    ab_ref, list_ref, kept_ref, out_ref, left_product, right_product, dense = refs[3 * turns :]
    products = (left_product, right_product)
    for half in range(2):
        total = None
        for turn in range(turns):
            part = lax.dot_general(
                halves[2 * turn + half][...], weights[turn][...], NT,
                preferred_element_type=jnp.float32,
            )
            total = part if total is None else total + part
        for q in range(2):
            products[q][half * HALF : (half + 1) * HALF, :] = total[:, q * 128 : (q + 1) * 128]
    lower = lax.broadcasted_iota(jnp.int32, (1, 128), 1) < TW
    skip = round_ref[0] * COLS
    for q in range(2):
        product = products[q]
        dense[...] = jnp.zeros_like(dense)
        irreps = [ab_ref[2 * q + i] for i in range(2)]
        starts = [jnp.minimum(kept_ref[g] + skip, IJ) for g in irreps]
        counts = [kept_ref[g + 1] - kept_ref[g] - skip for g in irreps]
        most = jnp.clip(jnp.maximum(counts[0], counts[1]), 0, COLS)

        @pl.loop(0, (most + 7) // 8)
        def _(block):
            base = block * 8
            for u in range(8):
                at = [list_ref[start + base + u] for start in starts]
                rows = [product[pl.ds(a, 1), :] for a in at]
                dense[pl.ds(base + u, 1), :] = jnp.where(lower, rows[0], rows[1])

        out_ref[q * 16 : (q + 1) * 16] = dense[...].T.reshape(16, 8, COLS)


def finish_kernel(round_ref, got_ref, ab_ref, code_ref, out_ref):
    irrep = ab_ref[lax.axis_index("panel") // 8]
    total = got_ref[0]
    for s in range(1, 32):
        total = total + got_ref[s]
    high = total.astype(jnp.bfloat16)
    rest = total - high.astype(jnp.float32)
    middle = rest.astype(jnp.bfloat16)
    low = (rest - middle.astype(jnp.float32)).astype(jnp.bfloat16)
    code = code_ref[...]
    place = jnp.where(code % IRREPS == irrep, code // IRREPS - round_ref[0] * COLS, -1)
    row = lax.broadcasted_iota(jnp.int32, (COLS, IJ), 0)
    spread = jnp.where(row == place, 1.0, 0.0).astype(jnp.bfloat16)
    parts = [jnp.dot(p, spread, preferred_element_type=jnp.float32) for p in (low, middle, high)]
    out_ref[...] = parts[0] + parts[1] + parts[2]


def shaped(shape, dtype):
    return jax.ShapeDtypeStruct(shape, dtype)


def body(integrals, amplitudes, ab_irrep, cd_irrep, occ_irrep):
    bf16, f32, i32 = jnp.bfloat16, jnp.float32, jnp.int32
    width = WIDE * TW
    chooser = pltpu.VMEM((16 * TW, width), bf16)

    def gathered(turn):
        sent = pl.pallas_call(
            functools.partial(send_kernel, turn),
            out_shape=shaped((SOURCES, ROWS, width), bf16),
            in_specs=[VMEM, SMEM, SMEM],
            out_specs=VMEM,
            scratch_shapes=[chooser],
        )(amplitudes, cd_irrep, occ_irrep)
        mine = lax.all_to_all(sent, CHIPS, split_axis=0, concat_axis=0, tiled=True)
        mine = mine.reshape(HALF, width)
        return [mine, lax.ppermute(mine, "blk_2", [(0, 1), (1, 0)])]

    def weights(turn):
        return pl.pallas_call(
            functools.partial(pack_rows_kernel, turn),
            out_shape=shaped((4 * TW, width), bf16),
            in_specs=[VMEM, SMEM, SMEM],
            out_specs=VMEM,
            scratch_shapes=[chooser],
        )(integrals, ab_irrep, cd_irrep)

    pair_list, code, kept = pl.pallas_call(
        tables_kernel,
        out_shape=[shaped((LIST,), i32), shaped((IJ,), i32), shaped((KEPT,), i32)],
        in_specs=[SMEM, SMEM],
        out_specs=[SMEM] * 3,
        scratch_shapes=[pltpu.SMEM((IRREPS,), i32), pltpu.SMEM((IRREPS,), i32)],
        name="tables",
    )(cd_irrep, occ_irrep)
    code = code.reshape(1, IJ)

    first, first_weights = gathered(0), weights(0)

    def products(which, turns, operands):
        return pl.pallas_call(
            functools.partial(product_kernel, turns),
            out_shape=shaped((32, 8, COLS), f32),
            in_specs=[SMEM] + [VMEM] * (3 * turns) + [SMEM] * 3,
            out_specs=VMEM,
            scratch_shapes=[
                pltpu.VMEM((2 * HALF, 128), f32),
                pltpu.VMEM((2 * HALF, 128), f32),
                pltpu.VMEM((COLS, 128), f32),
            ],
        )(which, *operands, ab_irrep, pair_list, kept)

    def partial_of(which):
        return lax.cond(
            kept[9] > WIDE,
            lambda: products(which, 2, [*first, *gathered(1), first_weights, weights(1)]),
            lambda: products(which, 1, [*first, first_weights]),
        )

    def reduced(number):
        which = jnp.full((1,), number, i32)
        arrived = lax.all_to_all(partial_of(which), "panel", split_axis=0, concat_axis=0, tiled=True)
        return pl.pallas_call(
            finish_kernel,
            out_shape=shaped((8, IJ), f32),
            in_specs=[SMEM, VMEM, SMEM, VMEM],
            out_specs=VMEM,
            name="finish",
        )(which, arrived, ab_irrep, code)

    def all_rounds():
        rounds = (kept[10] + COLS - 1) // COLS
        return lax.fori_loop(
            0, rounds, lambda number, total: total + reduced(number), jnp.zeros((8, IJ), f32)
        )

    return lax.cond(kept[10] > COLS, all_rounds, lambda: reduced(0))


def solution(mesh):
    split = Mesh(
        mesh.devices.reshape(2, 8, 2, mesh.shape["panel"]), ("blk_0", "blk_1", "blk_2", "panel")
    )
    return jax.shard_map(
        body,
        mesh=split,
        in_specs=(P(BLK, "panel"), P(BLK, "panel"), P(BLK), P("panel"), P()),
        out_specs=P(BLK_PANEL, None),
        check_vma=False,
    )
```

```python
import functools

import jax
import jax.numpy as jnp
from jax import lax
from jax.experimental import pallas as pl
from jax.experimental.pallas import tpu as pltpu
from jax.sharding import Mesh
from jax.sharding import PartitionSpec as P


TW = 64
IRREPS = 8
OCC = 40
IJ = 1600
BLK = ("blk_0", "blk_1", "blk_2")
BLK_PANEL = ("blk_0", "blk_1", "blk_2", "panel")
CHIPS = ("blk_0", "blk_1")

PAIRS = 50
ROWS = 56
SOURCES = 16
HALF = SOURCES * ROWS
WIDE = 8
WIRE = 640
COLS = WIRE - 1
LIST = 2304
KEPT = 16

SMEM = pl.BlockSpec(memory_space=pltpu.SMEM)
VMEM = pl.BlockSpec(memory_space=pltpu.VMEM)
NT = (((1,), (1,)), ((), ()))


def places(cd_ref):
    irreps = [cd_ref[t] for t in range(16)]
    ranks = []
    for t in range(16):
        rank = jnp.int32(0)
        for earlier in range(t):
            rank += jnp.where(irreps[earlier] == irreps[t], 1, 0)
        ranks.append(rank)
    return irreps, ranks


def fill_chooser(choose, ranks, turn):
    width = WIDE * TW
    row = lax.broadcasted_iota(jnp.int32, (TW, width), 0)
    col = lax.broadcasted_iota(jnp.int32, (TW, width), 1)
    place = jnp.where(col % TW == row, col // TW + turn * WIDE, -1)
    for t in range(16):
        hit = jnp.where(place == ranks[t], 1.0, 0.0)
        choose[t * TW : (t + 1) * TW, :] = hit.astype(jnp.bfloat16)


def column_irreps(irreps):
    lane = lax.broadcasted_iota(jnp.int32, (1, 16 * TW), 1) // TW
    found = jnp.zeros((1, 16 * TW), jnp.int32)
    for t in range(16):
        found = jnp.where(lane == t, irreps[t], found)
    return found


def pack(values, row_irrep, col_irrep, choose):
    kept = jnp.where(row_irrep == col_irrep, values.astype(jnp.float32), 0.0)
    return jnp.dot(
        kept.astype(jnp.bfloat16), choose[...], preferred_element_type=jnp.float32
    ).astype(jnp.bfloat16)


def send_kernel(turn, t_ref, cd_ref, occ_ref, out_ref, choose):
    blk = lax.axis_index("blk_0") * 16 + lax.axis_index("blk_1") * 2 + lax.axis_index("blk_2")
    irreps, ranks = places(cd_ref)
    fill_chooser(choose, ranks, turn)
    upper = blk * 5 // 4
    at = blk % 4 * 10
    left = [occ_ref[upper], occ_ref[jnp.minimum(upper + 1, OCC - 1)]]
    row = lax.broadcasted_iota(jnp.int32, (PAIRS, 1), 0)
    row_irrep = jnp.zeros((PAIRS, 1), jnp.int32)
    for m in range(PAIRS):
        later = at + m >= OCC
        right = occ_ref[at + m - jnp.where(later, OCC, 0)]
        irrep = jnp.bitwise_xor(jnp.where(later, left[1], left[0]), right)
        row_irrep = jnp.where(row == m, irrep, row_irrep)
    packed = pack(t_ref[...], row_irrep, column_irreps(irreps), choose)
    for s in range(SOURCES):
        out_ref[s, :PAIRS, :] = packed
        out_ref[s, PAIRS:, :] = jnp.zeros((ROWS - PAIRS, WIDE * TW), jnp.bfloat16)


def pack_rows_kernel(turn, v_ref, ab_ref, cd_ref, out_ref, choose):
    irreps, ranks = places(cd_ref)
    fill_chooser(choose, ranks, turn)
    row = lax.broadcasted_iota(jnp.int32, (4 * TW, 1), 0) // TW
    row_irrep = jnp.zeros((4 * TW, 1), jnp.int32)
    for i in range(4):
        row_irrep = jnp.where(row == i, ab_ref[i], row_irrep)
    out_ref[...] = pack(v_ref[...], row_irrep, column_irreps(irreps), choose)


def tables_kernel(cd_ref, occ_ref, list_ref, code_ref, kept_ref, orbitals, count):
    core = lax.axis_index("blk_2")
    for g in range(IRREPS):
        orbitals[g] = 0

    @pl.loop(0, OCC)
    def _(i):
        g = occ_ref[i]
        orbitals[g] = orbitals[g] + 1

    start = jnp.int32(0)
    most = jnp.int32(0)
    for g in range(IRREPS):
        pairs = jnp.int32(0)
        for h in range(IRREPS):
            pairs += orbitals[h] * orbitals[g ^ h]
        kept_ref[g] = start
        count[g] = start
        start += pairs
        most = jnp.maximum(most, pairs)
    _, ranks = places(cd_ref)
    widest = ranks[0]
    for rank in ranks[1:]:
        widest = jnp.maximum(widest, rank)
    kept_ref[8] = start
    kept_ref[9] = widest + 1
    kept_ref[10] = most
    for k in range(11, KEPT):
        kept_ref[k] = 0

    @pl.loop(0, 8)
    def _(part):
        base = [part * 2 * ROWS + jnp.bitwise_xor(other, core) * HALF for other in range(2)]
        for i in range(5):
            left = occ_ref[part * 5 + i]
            for j in range(OCC):
                pair = i * OCC + j
                source, m = divmod(pair, PAIRS)
                irrep = jnp.bitwise_xor(left, occ_ref[j])
                at = count[irrep]
                count[irrep] = at + 1
                list_ref[at] = base[source % 2] + source // 2 * ROWS + m
                code_ref[part * 200 + pair] = at * IRREPS + irrep

    @pl.loop(0, (LIST - IJ) // 16)
    def _(k):
        for u in range(16):
            list_ref[IJ + k * 16 + u] = 0


def product_kernel(turns, round_ref, *refs):
    halves, weights = refs[: 2 * turns], refs[2 * turns : 3 * turns]
    ab_ref, list_ref, kept_ref, out_ref, left_product, right_product, dense, both = refs[3 * turns :]
    products = (left_product, right_product)
    for half in range(2):
        total = None
        for turn in range(turns):
            part = lax.dot_general(
                halves[2 * turn + half][...], weights[turn][...], NT,
                preferred_element_type=jnp.float32,
            )
            total = part if total is None else total + part
        for q in range(2):
            products[q][half * HALF : (half + 1) * HALF, :] = total[:, q * 128 : (q + 1) * 128]
    lower = lax.broadcasted_iota(jnp.int32, (1, 128), 1) < TW
    skip = round_ref[0] * COLS
    for q in range(2):
        product = products[q]
        dense[...] = jnp.zeros_like(dense)
        irreps = [ab_ref[2 * q + i] for i in range(2)]
        starts = [jnp.minimum(kept_ref[g] + skip, IJ) for g in irreps]
        counts = [kept_ref[g + 1] - kept_ref[g] - skip for g in irreps]
        most = jnp.clip(jnp.maximum(counts[0], counts[1]), 0, COLS)

        @pl.loop(0, (most + 7) // 8)
        def _(block):
            base = block * 8
            for u in range(8):
                at = [list_ref[start + base + u] for start in starts]
                rows = [product[pl.ds(a, 1), :] for a in at]
                dense[pl.ds(base + u, 1), :] = jnp.where(lower, rows[0], rows[1])

        both[q * 128 : (q + 1) * 128, :] = dense[...].T
    largest = jnp.max(jnp.max(jnp.abs(both[...]), axis=1, keepdims=True), axis=0, keepdims=True)
    power = 14.0 - jnp.floor(jnp.log2(jnp.maximum(largest, 1e-30)))
    scaled = both[...] * jnp.exp2(power)
    lane = lax.broadcasted_iota(jnp.int32, (4 * TW, WIRE), 1)
    out_ref[...] = jnp.where(lane == COLS, power, scaled).reshape(32, 8, WIRE)


def finish_kernel(round_ref, sum_ref, ab_ref, kept_ref, code_ref, out_ref):
    irrep = ab_ref[lax.axis_index("panel") // 8]
    total = sum_ref[...]
    high = total.astype(jnp.bfloat16)
    rest = total - high.astype(jnp.float32)
    middle = rest.astype(jnp.bfloat16)
    low = (rest - middle.astype(jnp.float32)).astype(jnp.bfloat16)
    code = code_ref[...]
    first = kept_ref[irrep] + round_ref[0] * COLS
    place = jnp.where(code % IRREPS == irrep, code // IRREPS - first, -1)
    place = jnp.where(place < COLS, place, -1)
    row = lax.broadcasted_iota(jnp.int32, (WIRE, IJ), 0)
    spread = jnp.where(row == place, 1.0, 0.0).astype(jnp.bfloat16)
    parts = [jnp.dot(p, spread, preferred_element_type=jnp.float32) for p in (low, middle, high)]
    out_ref[...] = parts[0] + parts[1] + parts[2]


def shaped(shape, dtype):
    return jax.ShapeDtypeStruct(shape, dtype)


def body(integrals, amplitudes, ab_irrep, cd_irrep, occ_irrep):
    bf16, f32, i32 = jnp.bfloat16, jnp.float32, jnp.int32
    width = WIDE * TW
    chooser = pltpu.VMEM((16 * TW, width), bf16)

    def gathered(turn):
        sent = pl.pallas_call(
            functools.partial(send_kernel, turn),
            out_shape=shaped((SOURCES, ROWS, width), bf16),
            in_specs=[VMEM, SMEM, SMEM],
            out_specs=VMEM,
            scratch_shapes=[chooser],
        )(amplitudes, cd_irrep, occ_irrep)
        mine = lax.all_to_all(sent, CHIPS, split_axis=0, concat_axis=0, tiled=True)
        mine = mine.reshape(HALF, width)
        return [mine, lax.ppermute(mine, "blk_2", [(0, 1), (1, 0)])]

    def weights(turn):
        return pl.pallas_call(
            functools.partial(pack_rows_kernel, turn),
            out_shape=shaped((4 * TW, width), bf16),
            in_specs=[VMEM, SMEM, SMEM],
            out_specs=VMEM,
            scratch_shapes=[chooser],
        )(integrals, ab_irrep, cd_irrep)

    pair_list, code, kept = pl.pallas_call(
        tables_kernel,
        out_shape=[shaped((LIST,), i32), shaped((IJ,), i32), shaped((KEPT,), i32)],
        in_specs=[SMEM, SMEM],
        out_specs=[SMEM] * 3,
        scratch_shapes=[pltpu.SMEM((IRREPS,), i32), pltpu.SMEM((IRREPS,), i32)],
        name="tables",
    )(cd_irrep, occ_irrep)
    code = code.reshape(1, IJ)

    first, first_weights = gathered(0), weights(0)

    def products(which, turns, operands):
        return pl.pallas_call(
            functools.partial(product_kernel, turns),
            out_shape=shaped((32, 8, WIRE), f32),
            in_specs=[SMEM] + [VMEM] * (3 * turns) + [SMEM] * 3,
            out_specs=VMEM,
            scratch_shapes=[
                pltpu.VMEM((2 * HALF, 128), f32),
                pltpu.VMEM((2 * HALF, 128), f32),
                pltpu.VMEM((WIRE, 128), f32),
                pltpu.VMEM((4 * TW, WIRE), f32),
            ],
        )(which, *operands, ab_irrep, pair_list, kept)

    more_tiles, more_pairs = kept[9] > WIDE, kept[10] > COLS

    def partial_of(which):
        return lax.cond(
            more_tiles,
            lambda: products(which, 2, [*first, *gathered(1), first_weights, weights(1)]),
            lambda: products(which, 1, [*first, first_weights]),
        )

    def reduced(number):
        which = jnp.full((1,), number, i32)
        sent = partial_of(which).astype(jnp.float16)
        arrived = lax.all_to_all(sent, "panel", split_axis=0, concat_axis=0, tiled=True)
        arrived = arrived.astype(f32)
        total = jnp.sum(arrived * jnp.exp2(-arrived[:, :, COLS:]), axis=0)
        return pl.pallas_call(
            finish_kernel,
            out_shape=shaped((8, IJ), f32),
            in_specs=[SMEM, VMEM, SMEM, SMEM, VMEM],
            out_specs=VMEM,
            name="finish",
        )(which, total, ab_irrep, kept, code)

    def all_rounds():
        rounds = (kept[10] + COLS - 1) // COLS
        return lax.fori_loop(
            0, rounds, lambda number, total: total + reduced(number), jnp.zeros((8, IJ), f32)
        )

    return lax.cond(more_pairs, all_rounds, lambda: reduced(0))


def solution(mesh):
    split = Mesh(
        mesh.devices.reshape(2, 8, 2, mesh.shape["panel"]), ("blk_0", "blk_1", "blk_2", "panel")
    )
    return jax.shard_map(
        body,
        mesh=split,
        in_specs=(P(BLK, "panel"), P(BLK, "panel"), P(BLK), P("panel"), P()),
        out_specs=P(BLK_PANEL, None),
        check_vma=False,
    )
```

```python
import functools

import jax
import jax.numpy as jnp
from jax import lax
from jax.experimental import pallas as pl
from jax.experimental.pallas import tpu as pltpu
from jax.sharding import Mesh
from jax.sharding import PartitionSpec as P


TW = 64
IRREPS = 8
OCC = 40
IJ = 1600
BLK = ("blk_0", "blk_1", "blk_2")
BLK_PANEL = ("blk_0", "blk_1", "blk_2", "panel")
CHIPS = ("blk_0", "blk_1")

PAIRS = 50
SOURCES = 16
WIDE = 8
NARROW = 4
ROWS = 88
FULL = 56
WIRES = (512, 640)
LIST = 2304
KEPT = 16

SMEM = pl.BlockSpec(memory_space=pltpu.SMEM)
VMEM = pl.BlockSpec(memory_space=pltpu.VMEM)
NT = (((1,), (1,)), ((), ()))


def places(cd_ref):
    irreps = [cd_ref[t] for t in range(16)]
    ranks = []
    for t in range(16):
        rank = jnp.int32(0)
        for earlier in range(t):
            rank += jnp.where(irreps[earlier] == irreps[t], 1, 0)
        ranks.append(rank)
    return irreps, ranks


def fill_chooser(choose, ranks, turn):
    width = WIDE * TW
    row = lax.broadcasted_iota(jnp.int32, (TW, width), 0)
    col = lax.broadcasted_iota(jnp.int32, (TW, width), 1)
    place = jnp.where(col % TW == row, col // TW + turn * WIDE, -1)
    for t in range(16):
        hit = jnp.where(place == ranks[t], 1.0, 0.0)
        choose[t * TW : (t + 1) * TW, :] = hit.astype(jnp.bfloat16)


def column_irreps(irreps):
    lane = lax.broadcasted_iota(jnp.int32, (1, 16 * TW), 1) // TW
    found = jnp.zeros((1, 16 * TW), jnp.int32)
    for t in range(16):
        found = jnp.where(lane == t, irreps[t], found)
    return found


def pack(values, row_irrep, col_irrep, choose):
    kept = jnp.where(row_irrep == col_irrep, values.astype(jnp.float32), 0.0)
    return jnp.dot(
        kept.astype(jnp.bfloat16), choose[...], preferred_element_type=jnp.float32
    ).astype(jnp.bfloat16)


def my_pairs(occ_ref):
    blk = lax.axis_index("blk_0") * 16 + lax.axis_index("blk_1") * 2 + lax.axis_index("blk_2")
    upper = blk * 5 // 4
    at = blk % 4 * 10
    left = [occ_ref[upper], occ_ref[jnp.minimum(upper + 1, OCC - 1)]]
    row = lax.broadcasted_iota(jnp.int32, (PAIRS, 1), 0)
    column = jnp.zeros((PAIRS, 1), jnp.int32)
    irreps = []
    for m in range(PAIRS):
        later = at + m >= OCC
        right = occ_ref[at + m - jnp.where(later, OCC, 0)]
        irreps.append(jnp.bitwise_xor(jnp.where(later, left[1], left[0]), right))
        column = jnp.where(row == m, irreps[m], column)
    return irreps, column


def count_rows(irreps, need):
    for g in range(IRREPS):
        tiles = jnp.int32(0)
        for irrep in irreps:
            tiles += jnp.where(irrep == g, 1, 0)
        need[g] = (tiles + NARROW - 1) // NARROW


def send_kernel(t_ref, cd_ref, occ_ref, out_ref, choose, need):
    irreps, ranks = places(cd_ref)
    fill_chooser(choose, ranks, 0)
    count_rows(irreps, need)
    pairs, row_irrep = my_pairs(occ_ref)
    packed = pack(t_ref[...], row_irrep, column_irreps(irreps), choose)
    lane = lax.broadcasted_iota(jnp.int32, (1, PAIRS), 1)
    first = jnp.zeros((1, PAIRS), jnp.int32)
    last = jnp.zeros((1, PAIRS), jnp.int32)
    row = jnp.int32(0)
    for m in range(PAIRS):
        rows = need[pairs[m]]
        first = jnp.where(lane == m, jnp.where(rows > 0, row, -1), first)
        last = jnp.where(lane == m, jnp.where(rows > 1, row + 1, -1), last)
        row += rows
    place = lax.broadcasted_iota(jnp.int32, (ROWS, PAIRS), 0)
    width = NARROW * TW
    spread = None
    for part, at in enumerate((first, last)):
        move = jnp.where(place == at, 1.0, 0.0).astype(jnp.bfloat16)
        moved = jnp.dot(
            move, packed[:, part * width : (part + 1) * width], preferred_element_type=jnp.float32
        )
        spread = moved if spread is None else spread + moved
    spread = spread.astype(jnp.bfloat16)
    for s in range(SOURCES):
        out_ref[s] = spread


def send_full_kernel(turn, t_ref, cd_ref, occ_ref, out_ref, choose):
    irreps, ranks = places(cd_ref)
    fill_chooser(choose, ranks, turn)
    _, row_irrep = my_pairs(occ_ref)
    packed = pack(t_ref[...], row_irrep, column_irreps(irreps), choose)
    for s in range(SOURCES):
        out_ref[s, :PAIRS, :] = packed
        out_ref[s, PAIRS:, :] = jnp.zeros((FULL - PAIRS, WIDE * TW), jnp.bfloat16)


def pack_rows_kernel(turn, v_ref, ab_ref, cd_ref, out_ref, choose):
    irreps, ranks = places(cd_ref)
    fill_chooser(choose, ranks, turn)
    row = lax.broadcasted_iota(jnp.int32, (4 * TW, 1), 0) // TW
    row_irrep = jnp.zeros((4 * TW, 1), jnp.int32)
    for i in range(4):
        row_irrep = jnp.where(row == i, ab_ref[i], row_irrep)
    out_ref[...] = pack(v_ref[...], row_irrep, column_irreps(irreps), choose)


def tables_kernel(cd_ref, occ_ref, list_ref, code_ref, kept_ref, orbitals, count, need):
    core = lax.axis_index("blk_2")
    for g in range(IRREPS):
        orbitals[g] = 0

    @pl.loop(0, OCC)
    def _(i):
        g = occ_ref[i]
        orbitals[g] = orbitals[g] + 1

    start = jnp.int32(0)
    most = jnp.int32(0)
    for g in range(IRREPS):
        pairs = jnp.int32(0)
        for h in range(IRREPS):
            pairs += orbitals[h] * orbitals[g ^ h]
        kept_ref[g] = start
        count[g] = start
        start += pairs
        most = jnp.maximum(most, pairs)
    irreps, ranks = places(cd_ref)
    widest = ranks[0]
    for rank in ranks[1:]:
        widest = jnp.maximum(widest, rank)
    count_rows(irreps, need)
    kept_ref[8] = start
    kept_ref[9] = jnp.where(widest < WIDE, 0, 1)
    kept_ref[10] = most
    for k in range(11, KEPT):
        kept_ref[k] = 0

    @pl.loop(0, 8)
    def _(part):
        half = SOURCES * ROWS
        base = [part * 2 * ROWS + jnp.bitwise_xor(other, core) * half for other in range(2)]
        longest = jnp.int32(0)
        row = None
        for i in range(5):
            left = occ_ref[part * 5 + i]
            for j in range(OCC):
                pair = i * OCC + j
                source, m = divmod(pair, PAIRS)
                if m == 0:
                    row = base[source % 2] + source // 2 * ROWS
                    end = row + ROWS
                irrep = jnp.bitwise_xor(left, occ_ref[j])
                at = count[irrep]
                count[irrep] = at + 1
                list_ref[at] = jnp.minimum(row, end - 1)
                code_ref[part * 200 + pair] = at * IRREPS + irrep
                row += need[irrep]
                if m == PAIRS - 1:
                    longest = jnp.maximum(longest, row - end)
        kept_ref[9] = jnp.where(longest > 0, 1, kept_ref[9])

    @pl.loop(0, (LIST - IJ) // 16)
    def _(k):
        for u in range(16):
            list_ref[IJ + k * 16 + u] = 0


def full_list_kernel(occ_ref, kept_ref, list_ref, count):
    core = lax.axis_index("blk_2")
    for g in range(IRREPS):
        count[g] = kept_ref[g]

    @pl.loop(0, OCC)
    def _(i):
        left = occ_ref[i]

        @pl.loop(0, OCC)
        def _(j):
            pair = i * OCC + j
            irrep = jnp.bitwise_xor(left, occ_ref[j])
            at = count[irrep]
            count[irrep] = at + 1
            source = pair // PAIRS
            chip = jnp.bitwise_xor(source & 1, core) * SOURCES + (source >> 1)
            list_ref[at] = chip * FULL + pair - source * PAIRS

    @pl.loop(IJ, LIST)
    def _(k):
        list_ref[k] = 0


def product_kernel(full, round_ref, *refs):
    turns = 2 if full else 1
    half_rows = SOURCES * (FULL if full else ROWS)
    halves, weights = refs[: 2 * turns], refs[2 * turns : 3 * turns]
    ab_ref, list_ref, kept_ref, out_ref, left_product, right_product, dense, both = refs[3 * turns :]
    products = (left_product, right_product)
    wire = dense.shape[0]
    cols = wire - 1
    width = NARROW * TW

    def times(held, weight):
        return lax.dot_general(held, weight, NT, preferred_element_type=jnp.float32)

    for half in range(2):
        if full:
            total = times(halves[half][...], weights[0][...])
            total += times(halves[2 + half][...], weights[1][...])
        else:
            held = halves[half][...]
            total = times(held, weights[0][:, :width])
            following = times(held, weights[0][:, width:])
            total += pltpu.roll(following, half_rows - 1, 0)
        for q in range(2):
            at = slice(half * half_rows, (half + 1) * half_rows)
            products[q][at, :] = total[:, q * 128 : (q + 1) * 128]
    lower = lax.broadcasted_iota(jnp.int32, (1, 128), 1) < TW
    skip = round_ref[0] * cols
    for q in range(2):
        product = products[q]
        dense[...] = jnp.zeros_like(dense)
        irreps = [ab_ref[2 * q + i] for i in range(2)]
        starts = [jnp.minimum(kept_ref[g] + skip, IJ) for g in irreps]
        counts = [kept_ref[g + 1] - kept_ref[g] - skip for g in irreps]
        most = jnp.clip(jnp.maximum(counts[0], counts[1]), 0, cols)

        @pl.loop(0, (most + 7) // 8)
        def _(block):
            base = block * 8
            for u in range(8):
                at = [list_ref[start + base + u] for start in starts]
                rows = [product[pl.ds(a, 1), :] for a in at]
                dense[pl.ds(base + u, 1), :] = jnp.where(lower, rows[0], rows[1])

        both[q * 128 : (q + 1) * 128, :] = dense[...].T
    largest = jnp.max(jnp.max(jnp.abs(both[...]), axis=1, keepdims=True), axis=0, keepdims=True)
    power = 14.0 - jnp.floor(jnp.log2(jnp.maximum(largest, 1e-30)))
    scaled = both[...] * jnp.exp2(power)
    lane = lax.broadcasted_iota(jnp.int32, (4 * TW, wire), 1)
    out_ref[...] = jnp.where(lane == cols, power, scaled).reshape(32, 8, wire)


def spread_kernel(round_ref, ab_ref, kept_ref, code_ref, out_ref):
    irrep = ab_ref[lax.axis_index("panel") // 8]
    cols = WIRES[-1] - 1
    code = code_ref[...]
    first = kept_ref[irrep] + round_ref[0] * cols
    place = jnp.where(code % IRREPS == irrep, code // IRREPS - first, -1)
    place = jnp.where(place < cols, place, -1)
    row = lax.broadcasted_iota(jnp.int32, (WIRES[-1], IJ), 0)
    out_ref[...] = jnp.where(row == place, 1.0, 0.0).astype(jnp.bfloat16)


def finish_kernel(got_ref, spread_ref, out_ref):
    wire = got_ref.shape[2]
    total = None
    for s in range(32):
        got = got_ref[s]
        got = got * jnp.exp2(-got[:, wire - 1 :])
        total = got if total is None else total + got
    high = total.astype(jnp.bfloat16)
    rest = total - high.astype(jnp.float32)
    middle = rest.astype(jnp.bfloat16)
    low = (rest - middle.astype(jnp.float32)).astype(jnp.bfloat16)
    spread = spread_ref[:wire, :]
    parts = [jnp.dot(p, spread, preferred_element_type=jnp.float32) for p in (low, middle, high)]
    out_ref[...] = parts[0] + parts[1] + parts[2]


def shaped(shape, dtype):
    return jax.ShapeDtypeStruct(shape, dtype)


def body(integrals, amplitudes, ab_irrep, cd_irrep, occ_irrep):
    bf16, f32, i32 = jnp.bfloat16, jnp.float32, jnp.int32
    width = WIDE * TW
    chooser = pltpu.VMEM((16 * TW, width), bf16)
    numbers = pltpu.SMEM((IRREPS,), i32)

    def both_cores(sent):
        mine = lax.all_to_all(sent, CHIPS, split_axis=0, concat_axis=0, tiled=True)
        mine = mine.reshape(sent.shape[0] * sent.shape[1], sent.shape[2])
        return [mine, lax.ppermute(mine, "blk_2", [(0, 1), (1, 0)])]

    def gathered_full(turn):
        sent = pl.pallas_call(
            functools.partial(send_full_kernel, turn),
            out_shape=shaped((SOURCES, FULL, width), bf16),
            in_specs=[VMEM, SMEM, SMEM],
            out_specs=VMEM,
            scratch_shapes=[chooser],
        )(amplitudes, cd_irrep, occ_irrep)
        return both_cores(sent)

    def weights(turn):
        return pl.pallas_call(
            functools.partial(pack_rows_kernel, turn),
            out_shape=shaped((4 * TW, width), bf16),
            in_specs=[VMEM, SMEM, SMEM],
            out_specs=VMEM,
            scratch_shapes=[chooser],
        )(integrals, ab_irrep, cd_irrep)

    def spread_of(which):
        return pl.pallas_call(
            spread_kernel,
            out_shape=shaped((WIRES[-1], IJ), bf16),
            in_specs=[SMEM] * 3 + [VMEM],
            out_specs=VMEM,
            name="spread",
        )(which, ab_irrep, kept, code)

    sent = pl.pallas_call(
        send_kernel,
        out_shape=shaped((SOURCES, ROWS, NARROW * TW), bf16),
        in_specs=[VMEM, SMEM, SMEM],
        out_specs=VMEM,
        scratch_shapes=[chooser, numbers],
        name="send",
    )(amplitudes, cd_irrep, occ_irrep)
    halves = both_cores(sent)

    pair_list, code, kept = pl.pallas_call(
        tables_kernel,
        out_shape=[shaped((LIST,), i32), shaped((IJ,), i32), shaped((KEPT,), i32)],
        in_specs=[SMEM, SMEM],
        out_specs=[SMEM] * 3,
        scratch_shapes=[numbers] * 3,
        name="tables",
    )(cd_irrep, occ_irrep)
    code = code.reshape(1, IJ)
    zero = jnp.zeros((1,), i32)
    first_weights, first_spread = weights(0), spread_of(zero)

    def products(full, wire, which, operands, pairs):
        rows = 2 * SOURCES * (FULL if full else ROWS)
        return pl.pallas_call(
            functools.partial(product_kernel, full),
            out_shape=shaped((32, 8, wire), f32),
            in_specs=[SMEM] + [VMEM] * len(operands) + [SMEM] * 3,
            out_specs=VMEM,
            scratch_shapes=[
                pltpu.VMEM((rows, 128), f32),
                pltpu.VMEM((rows, 128), f32),
                pltpu.VMEM((wire, 128), f32),
                pltpu.VMEM((4 * TW, wire), f32),
            ],
        )(which, *operands, ab_irrep, pairs, kept)

    def full_products(wire, which):
        pairs = pl.pallas_call(
            full_list_kernel,
            out_shape=shaped((LIST,), i32),
            in_specs=[SMEM] * 2,
            out_specs=SMEM,
            scratch_shapes=[numbers],
            name="full_list",
        )(occ_irrep, kept)
        operands = [*gathered_full(0), *gathered_full(1), first_weights, weights(1)]
        return products(True, wire, which, operands, pairs)

    general, most = kept[9] > 0, kept[10]

    def reduced(wire, which, spread):
        partial = lax.cond(
            general,
            lambda: full_products(wire, which),
            lambda: products(False, wire, which, [*halves, first_weights], pair_list),
        ).astype(jnp.float16)
        arrived = lax.all_to_all(partial, "panel", split_axis=0, concat_axis=0, tiled=True)
        return pl.pallas_call(
            finish_kernel,
            out_shape=shaped((8, IJ), f32),
            in_specs=[VMEM, VMEM],
            out_specs=VMEM,
            name="finish",
        )(arrived.astype(f32), spread)

    def all_rounds():
        cols = WIRES[-1] - 1

        def add_round(number, total):
            which = jnp.full((1,), number, i32)
            return total + reduced(WIRES[-1], which, spread_of(which))

        return lax.fori_loop(0, (most + cols - 1) // cols, add_round, jnp.zeros((8, IJ), f32))

    branches = [functools.partial(reduced, wire, zero, first_spread) for wire in WIRES]
    chosen = sum((most >= wire).astype(i32) for wire in WIRES)
    return lax.switch(chosen, [*branches, all_rounds])


def solution(mesh):
    split = Mesh(
        mesh.devices.reshape(2, 8, 2, mesh.shape["panel"]), ("blk_0", "blk_1", "blk_2", "panel")
    )
    return jax.shard_map(
        body,
        mesh=split,
        in_specs=(P(BLK, "panel"), P(BLK, "panel"), P(BLK), P("panel"), P()),
        out_specs=P(BLK_PANEL, None),
        check_vma=False,
    )
```

```python
import functools

import jax
import jax.numpy as jnp
from jax import lax
from jax.experimental import pallas as pl
from jax.experimental.pallas import tpu as pltpu
from jax.sharding import Mesh
from jax.sharding import PartitionSpec as P


TW = 64
IRREPS = 8
OCC = 40
IJ = 1600
BLK = ("blk_0", "blk_1", "blk_2")
BLK_PANEL = ("blk_0", "blk_1", "blk_2", "panel")
CHIPS = ("blk_0", "blk_1")

PAIRS = 50
SOURCES = 16
WIDE = 8
NARROW = 2
PARTS = WIDE // NARROW
ROWS = 136
FULL = 56
WIRES = (512, 640)
CODES = 1664
NOWHERE = 1 << 24
LIST = 2304
KEPT = 16

SMEM = pl.BlockSpec(memory_space=pltpu.SMEM)
VMEM = pl.BlockSpec(memory_space=pltpu.VMEM)
NT = (((1,), (1,)), ((), ()))
GRANT = pltpu.CompilerParams(vmem_limit_bytes=24 << 20)
LARGE = pltpu.CompilerParams(vmem_limit_bytes=40 << 20)


def places(cd_ref):
    irreps = [cd_ref[t] for t in range(16)]
    ranks = []
    for t in range(16):
        rank = jnp.int32(0)
        for earlier in range(t):
            rank += jnp.where(irreps[earlier] == irreps[t], 1, 0)
        ranks.append(rank)
    return irreps, ranks


def fill_chooser(choose, ranks, turn):
    width = WIDE * TW
    row = lax.broadcasted_iota(jnp.int32, (TW, width), 0)
    col = lax.broadcasted_iota(jnp.int32, (TW, width), 1)
    place = jnp.where(col % TW == row, col // TW + turn * WIDE, -1)
    for t in range(16):
        hit = jnp.where(place == ranks[t], 1.0, 0.0)
        choose[t * TW : (t + 1) * TW, :] = hit.astype(jnp.bfloat16)


def column_irreps(irreps):
    lane = lax.broadcasted_iota(jnp.int32, (1, 16 * TW), 1) // TW
    found = jnp.zeros((1, 16 * TW), jnp.int32)
    for t in range(16):
        found = jnp.where(lane == t, irreps[t], found)
    return found


def pack(values, row_irrep, col_irrep, choose):
    kept = jnp.where(row_irrep == col_irrep, values.astype(jnp.float32), 0.0)
    return jnp.dot(
        kept.astype(jnp.bfloat16), choose[...], preferred_element_type=jnp.float32
    ).astype(jnp.bfloat16)


def my_pairs(occ_ref):
    blk = lax.axis_index("blk_0") * 16 + lax.axis_index("blk_1") * 2 + lax.axis_index("blk_2")
    upper = blk * 5 // 4
    at = blk % 4 * 10
    left = [occ_ref[upper], occ_ref[jnp.minimum(upper + 1, OCC - 1)]]
    row = lax.broadcasted_iota(jnp.int32, (PAIRS, 1), 0)
    column = jnp.zeros((PAIRS, 1), jnp.int32)
    irreps = []
    for m in range(PAIRS):
        later = at + m >= OCC
        right = occ_ref[at + m - jnp.where(later, OCC, 0)]
        irreps.append(jnp.bitwise_xor(jnp.where(later, left[1], left[0]), right))
        column = jnp.where(row == m, irreps[m], column)
    return irreps, column


def count_rows(irreps, need):
    for g in range(IRREPS):
        tiles = jnp.int32(0)
        for irrep in irreps:
            tiles += jnp.where(irrep == g, 1, 0)
        need[g] = (tiles + NARROW - 1) // NARROW


def send_kernel(t_ref, cd_ref, occ_ref, out_ref, choose, need):
    irreps, ranks = places(cd_ref)
    fill_chooser(choose, ranks, 0)
    count_rows(irreps, need)
    pairs, row_irrep = my_pairs(occ_ref)
    packed = pack(t_ref[...], row_irrep, column_irreps(irreps), choose)
    lane = lax.broadcasted_iota(jnp.int32, (1, PAIRS), 1)
    first = jnp.zeros((1, PAIRS), jnp.int32)
    count = jnp.zeros((1, PAIRS), jnp.int32)
    row = jnp.int32(0)
    for m in range(PAIRS):
        rows = need[pairs[m]]
        first = jnp.where(lane == m, row, first)
        count = jnp.where(lane == m, rows, count)
        row += rows
    place = lax.broadcasted_iota(jnp.int32, (ROWS, PAIRS), 0)
    width = NARROW * TW
    spread = None
    for part in range(PARTS):
        at = jnp.where(count > part, first + part, -1)
        move = jnp.where(place == at, 1.0, 0.0).astype(jnp.bfloat16)
        moved = jnp.dot(
            move, packed[:, part * width : (part + 1) * width], preferred_element_type=jnp.float32
        )
        spread = moved if spread is None else spread + moved
    spread = spread.astype(jnp.bfloat16)
    for s in range(SOURCES):
        out_ref[s] = spread


def send_full_kernel(turn, t_ref, cd_ref, occ_ref, out_ref, choose):
    irreps, ranks = places(cd_ref)
    fill_chooser(choose, ranks, turn)
    _, row_irrep = my_pairs(occ_ref)
    packed = pack(t_ref[...], row_irrep, column_irreps(irreps), choose)
    for s in range(SOURCES):
        out_ref[s, :PAIRS, :] = packed
        out_ref[s, PAIRS:, :] = jnp.zeros((FULL - PAIRS, WIDE * TW), jnp.bfloat16)


def pack_rows_kernel(turn, v_ref, ab_ref, cd_ref, out_ref, choose):
    irreps, ranks = places(cd_ref)
    fill_chooser(choose, ranks, turn)
    row = lax.broadcasted_iota(jnp.int32, (4 * TW, 1), 0) // TW
    row_irrep = jnp.zeros((4 * TW, 1), jnp.int32)
    for i in range(4):
        row_irrep = jnp.where(row == i, ab_ref[i], row_irrep)
    out_ref[...] = pack(v_ref[...], row_irrep, column_irreps(irreps), choose)


def tables_kernel(cd_ref, occ_ref, list_ref, code_ref, kept_ref, orbitals, count, need):
    core = lax.axis_index("blk_2")
    for g in range(IRREPS):
        orbitals[g] = 0

    @pl.loop(0, OCC)
    def _(i):
        g = occ_ref[i]
        orbitals[g] = orbitals[g] + 1

    start = jnp.int32(0)
    most = jnp.int32(0)
    for g in range(IRREPS):
        pairs = jnp.int32(0)
        for h in range(IRREPS):
            pairs += orbitals[h] * orbitals[g ^ h]
        kept_ref[g] = start
        count[g] = start
        start += pairs
        most = jnp.maximum(most, pairs)
    irreps, ranks = places(cd_ref)
    widest = ranks[0]
    for rank in ranks[1:]:
        widest = jnp.maximum(widest, rank)
    count_rows(irreps, need)
    kept_ref[8] = start
    kept_ref[9] = jnp.where(widest < WIDE, 0, 1)
    kept_ref[10] = most
    for k in range(11, KEPT):
        kept_ref[k] = 0

    @pl.loop(0, 8)
    def _(part):
        half = SOURCES * ROWS
        base = [part * 2 * ROWS + jnp.bitwise_xor(other, core) * half for other in range(2)]
        longest = jnp.int32(0)
        row = None
        for i in range(5):
            left = occ_ref[part * 5 + i]
            for j in range(OCC):
                pair = i * OCC + j
                source, m = divmod(pair, PAIRS)
                if m == 0:
                    row = base[source % 2] + source // 2 * ROWS
                    end = row + ROWS
                irrep = jnp.bitwise_xor(left, occ_ref[j])
                at = count[irrep]
                count[irrep] = at + 1
                list_ref[at] = jnp.minimum(row, end - 1)
                code_ref[part * 200 + pair] = at * IRREPS + irrep
                row += need[irrep]
                if m == PAIRS - 1:
                    longest = jnp.maximum(longest, row - end)
        kept_ref[9] = jnp.where(longest > 0, 1, kept_ref[9])

    for k in range(IJ, CODES):
        code_ref[k] = NOWHERE

    @pl.loop(0, (LIST - IJ) // 16)
    def _(k):
        for u in range(16):
            list_ref[IJ + k * 16 + u] = 0


def full_list_kernel(occ_ref, kept_ref, list_ref, count):
    core = lax.axis_index("blk_2")
    for g in range(IRREPS):
        count[g] = kept_ref[g]

    @pl.loop(0, OCC)
    def _(i):
        left = occ_ref[i]

        @pl.loop(0, OCC)
        def _(j):
            pair = i * OCC + j
            irrep = jnp.bitwise_xor(left, occ_ref[j])
            at = count[irrep]
            count[irrep] = at + 1
            source = pair // PAIRS
            chip = jnp.bitwise_xor(source & 1, core) * SOURCES + (source >> 1)
            list_ref[at] = chip * FULL + pair - source * PAIRS

    @pl.loop(IJ, LIST)
    def _(k):
        list_ref[k] = 0


def product_kernel(full, round_ref, *refs):
    turns = 2 if full else 1
    half_rows = SOURCES * (FULL if full else ROWS)
    halves, weights = refs[: 2 * turns], refs[2 * turns : 3 * turns]
    ab_ref, list_ref, kept_ref, out_ref, left_product, right_product, dense, both = refs[3 * turns :]
    products = (left_product, right_product)
    wire = dense.shape[0]
    cols = wire - 1

    def times(held, weight):
        return lax.dot_general(held, weight, NT, preferred_element_type=jnp.float32)

    for half in range(2):
        if full:
            total = times(halves[half][...], weights[0][...])
            total += times(halves[2 + half][...], weights[1][...])
        else:
            held = halves[half][...].astype(jnp.float32)
            rows = [held] + [pltpu.roll(held, half_rows - part, 0) for part in range(1, PARTS)]
            joined = jnp.concatenate([r.astype(jnp.bfloat16) for r in rows], axis=1)
            total = times(joined, weights[0][...])
        for q in range(2):
            at = slice(half * half_rows, (half + 1) * half_rows)
            products[q][at, :] = total[:, q * 128 : (q + 1) * 128]
    lower = lax.broadcasted_iota(jnp.int32, (1, 128), 1) < TW
    skip = round_ref[0] * cols
    for q in range(2):
        product = products[q]
        dense[...] = jnp.zeros_like(dense)
        irreps = [ab_ref[2 * q + i] for i in range(2)]
        starts = [jnp.minimum(kept_ref[g] + skip, IJ) for g in irreps]
        counts = [kept_ref[g + 1] - kept_ref[g] - skip for g in irreps]
        most = jnp.clip(jnp.maximum(counts[0], counts[1]), 0, cols)

        @pl.loop(0, (most + 7) // 8)
        def _(block):
            base = block * 8
            for u in range(8):
                at = [list_ref[start + base + u] for start in starts]
                rows = [product[pl.ds(a, 1), :] for a in at]
                dense[pl.ds(base + u, 1), :] = jnp.where(lower, rows[0], rows[1])

        both[q * 128 : (q + 1) * 128, :] = dense[...].T
    largest = jnp.max(jnp.max(jnp.abs(both[...]), axis=1, keepdims=True), axis=0, keepdims=True)
    power = 14.0 - jnp.floor(jnp.log2(jnp.maximum(largest, 1e-30)))
    scaled = both[...] * jnp.exp2(power)
    lane = lax.broadcasted_iota(jnp.int32, (4 * TW, wire), 1)
    out_ref[...] = jnp.where(lane == cols, power, scaled).reshape(32, 8, wire)


def finish_kernel(round_ref, got_ref, ab_ref, kept_ref, code_ref, out_ref):
    irrep = ab_ref[lax.axis_index("panel") // 8]
    wire = got_ref.shape[2]
    cols = wire - 1
    total = None
    for s in range(32):
        got = got_ref[s]
        got = got * jnp.exp2(-got[:, cols:])
        total = got if total is None else total + got
    first = kept_ref[irrep] + round_ref[0] * cols
    for block in range(CODES // 128):
        code = jnp.broadcast_to(code_ref[:, block * 128 : (block + 1) * 128], (8, 128))
        place = jnp.where(code % IRREPS == irrep, code // IRREPS - first, -1)
        place = jnp.where(place < cols, place, -1)
        lane = place & 127
        found = jnp.zeros((8, 128), jnp.float32)
        for k in range(wire // 128):
            moved = jnp.take_along_axis(total[:, k * 128 : (k + 1) * 128], lane, axis=1)
            found = jnp.where(place >> 7 == k, moved, found)
        held = min(128, IJ - block * 128)
        out_ref[:, block * 128 : block * 128 + held] = found[:, :held]


def shaped(shape, dtype):
    return jax.ShapeDtypeStruct(shape, dtype)


def body(integrals, amplitudes, ab_irrep, cd_irrep, occ_irrep):
    bf16, f32, i32 = jnp.bfloat16, jnp.float32, jnp.int32
    width = WIDE * TW
    chooser = pltpu.VMEM((16 * TW, width), bf16)
    numbers = pltpu.SMEM((IRREPS,), i32)

    def both_cores(sent):
        mine = lax.all_to_all(sent, CHIPS, split_axis=0, concat_axis=0, tiled=True)
        mine = mine.reshape(sent.shape[0] * sent.shape[1], sent.shape[2])
        return [mine, lax.ppermute(mine, "blk_2", [(0, 1), (1, 0)])]

    def gathered_full(turn):
        sent = pl.pallas_call(
            functools.partial(send_full_kernel, turn),
            out_shape=shaped((SOURCES, FULL, width), bf16),
            in_specs=[VMEM, SMEM, SMEM],
            out_specs=VMEM,
            scratch_shapes=[chooser],
            compiler_params=GRANT,
        )(amplitudes, cd_irrep, occ_irrep)
        return both_cores(sent)

    def weights(turn):
        return pl.pallas_call(
            functools.partial(pack_rows_kernel, turn),
            out_shape=shaped((4 * TW, width), bf16),
            in_specs=[VMEM, SMEM, SMEM],
            out_specs=VMEM,
            scratch_shapes=[chooser],
            compiler_params=GRANT,
        )(integrals, ab_irrep, cd_irrep)

    sent = pl.pallas_call(
        send_kernel,
        out_shape=shaped((SOURCES, ROWS, NARROW * TW), bf16),
        in_specs=[VMEM, SMEM, SMEM],
        out_specs=VMEM,
        scratch_shapes=[chooser, numbers],
        compiler_params=GRANT,
        name="send",
    )(amplitudes, cd_irrep, occ_irrep)
    halves = both_cores(sent)

    pair_list, code, kept = pl.pallas_call(
        tables_kernel,
        out_shape=[shaped((LIST,), i32), shaped((CODES,), i32), shaped((KEPT,), i32)],
        in_specs=[SMEM, SMEM],
        out_specs=[SMEM] * 3,
        scratch_shapes=[numbers] * 3,
        compiler_params=GRANT,
        name="tables",
    )(cd_irrep, occ_irrep)
    code = code.reshape(1, CODES)
    zero = jnp.zeros((1,), i32)
    first_weights = weights(0)

    def products(full, wire, which, operands, pairs):
        rows = 2 * SOURCES * (FULL if full else ROWS)
        return pl.pallas_call(
            functools.partial(product_kernel, full),
            out_shape=shaped((32, 8, wire), f32),
            in_specs=[SMEM] + [VMEM] * len(operands) + [SMEM] * 3,
            out_specs=VMEM,
            scratch_shapes=[
                pltpu.VMEM((rows, 128), f32),
                pltpu.VMEM((rows, 128), f32),
                pltpu.VMEM((wire, 128), f32),
                pltpu.VMEM((4 * TW, wire), f32),
            ],
            compiler_params=LARGE,
        )(which, *operands, ab_irrep, pairs, kept)

    def full_products(wire, which):
        pairs = pl.pallas_call(
            full_list_kernel,
            out_shape=shaped((LIST,), i32),
            in_specs=[SMEM] * 2,
            out_specs=SMEM,
            scratch_shapes=[numbers],
            compiler_params=GRANT,
            name="full_list",
        )(occ_irrep, kept)
        operands = [*gathered_full(0), *gathered_full(1), first_weights, weights(1)]
        return products(True, wire, which, operands, pairs)

    general, most = kept[9] > 0, kept[10]

    def reduced(wire, which):
        partial = lax.cond(
            general,
            lambda: full_products(wire, which),
            lambda: products(False, wire, which, [*halves, first_weights], pair_list),
        ).astype(jnp.float16)
        arrived = lax.all_to_all(partial, "panel", split_axis=0, concat_axis=0, tiled=True)
        return pl.pallas_call(
            finish_kernel,
            out_shape=shaped((8, IJ), f32),
            in_specs=[SMEM, VMEM, SMEM, SMEM, VMEM],
            out_specs=VMEM,
            compiler_params=GRANT,
            name="finish",
        )(which, arrived.astype(f32), ab_irrep, kept, code)

    def all_rounds():
        cols = WIRES[-1] - 1

        def add_round(number, total):
            which = jnp.full((1,), number, i32)
            return total + reduced(WIRES[-1], which)

        return lax.fori_loop(0, (most + cols - 1) // cols, add_round, jnp.zeros((8, IJ), f32))

    branches = [functools.partial(reduced, wire, zero) for wire in WIRES]
    chosen = sum((most >= wire).astype(i32) for wire in WIRES)
    return lax.switch(chosen, [*branches, all_rounds])


def solution(mesh):
    split = Mesh(
        mesh.devices.reshape(2, 8, 2, mesh.shape["panel"]), ("blk_0", "blk_1", "blk_2", "panel")
    )
    return jax.shard_map(
        body,
        mesh=split,
        in_specs=(P(BLK, "panel"), P(BLK, "panel"), P(BLK), P("panel"), P()),
        out_specs=P(BLK_PANEL, None),
        check_vma=False,
    )
```

```python
import functools

import jax
import jax.numpy as jnp
from jax import lax
from jax.experimental import pallas as pl
from jax.experimental.pallas import tpu as pltpu
from jax.sharding import Mesh
from jax.sharding import PartitionSpec as P


TW = 64
IRREPS = 8
OCC = 40
IJ = 1600
BLK = ("blk_0", "blk_1", "blk_2")
BLK_PANEL = ("blk_0", "blk_1", "blk_2", "panel")
CHIPS = ("blk_0", "blk_1")

PAIRS = 50
SOURCES = 16
WIDE = 8
NARROW = 2
PARTS = WIDE // NARROW
ROWS = 136
FULL = 56
WIRES = (512, 640)
CODES = 1664
NOWHERE = 1 << 24
LIST = 2304
KEPT = 16

SMEM = pl.BlockSpec(memory_space=pltpu.SMEM)
VMEM = pl.BlockSpec(memory_space=pltpu.VMEM)
ANY = pl.BlockSpec(memory_space=pl.ANY)
NT = (((1,), (1,)), ((), ()))
GRANT = pltpu.CompilerParams(vmem_limit_bytes=24 << 20)
LARGE = pltpu.CompilerParams(vmem_limit_bytes=40 << 20)


def places(cd_ref):
    irreps = [cd_ref[t] for t in range(16)]
    ranks = []
    for t in range(16):
        rank = jnp.int32(0)
        for earlier in range(t):
            rank += jnp.where(irreps[earlier] == irreps[t], 1, 0)
        ranks.append(rank)
    return irreps, ranks


def fill_chooser(choose, ranks, turn):
    width = WIDE * TW
    row = lax.broadcasted_iota(jnp.int32, (TW, width), 0)
    col = lax.broadcasted_iota(jnp.int32, (TW, width), 1)
    place = jnp.where(col % TW == row, col // TW + turn * WIDE, -1)
    for t in range(16):
        hit = jnp.where(place == ranks[t], 1.0, 0.0)
        choose[t * TW : (t + 1) * TW, :] = hit.astype(jnp.bfloat16)


def column_irreps(irreps):
    lane = lax.broadcasted_iota(jnp.int32, (1, 16 * TW), 1) // TW
    found = jnp.zeros((1, 16 * TW), jnp.int32)
    for t in range(16):
        found = jnp.where(lane == t, irreps[t], found)
    return found


def pack(values, row_irrep, col_irrep, choose):
    kept = jnp.where(row_irrep == col_irrep, values.astype(jnp.float32), 0.0)
    return jnp.dot(
        kept.astype(jnp.bfloat16), choose[...], preferred_element_type=jnp.float32
    ).astype(jnp.bfloat16)


def my_pairs(occ_ref):
    blk = lax.axis_index("blk_0") * 16 + lax.axis_index("blk_1") * 2 + lax.axis_index("blk_2")
    upper = blk * 5 // 4
    at = blk % 4 * 10
    left = [occ_ref[upper], occ_ref[jnp.minimum(upper + 1, OCC - 1)]]
    row = lax.broadcasted_iota(jnp.int32, (PAIRS, 1), 0)
    column = jnp.zeros((PAIRS, 1), jnp.int32)
    irreps = []
    for m in range(PAIRS):
        later = at + m >= OCC
        right = occ_ref[at + m - jnp.where(later, OCC, 0)]
        irreps.append(jnp.bitwise_xor(jnp.where(later, left[1], left[0]), right))
        column = jnp.where(row == m, irreps[m], column)
    return irreps, column


def count_rows(irreps, need):
    for g in range(IRREPS):
        tiles = jnp.int32(0)
        for irrep in irreps:
            tiles += jnp.where(irrep == g, 1, 0)
        need[g] = (tiles + NARROW - 1) // NARROW


def send_kernel(t_ref, cd_ref, occ_ref, out_ref, choose, need):
    irreps, ranks = places(cd_ref)
    fill_chooser(choose, ranks, 0)
    count_rows(irreps, need)
    pairs, row_irrep = my_pairs(occ_ref)
    packed = pack(t_ref[...], row_irrep, column_irreps(irreps), choose)
    lane = lax.broadcasted_iota(jnp.int32, (1, PAIRS), 1)
    first = jnp.zeros((1, PAIRS), jnp.int32)
    count = jnp.zeros((1, PAIRS), jnp.int32)
    row = jnp.int32(0)
    for m in range(PAIRS):
        rows = need[pairs[m]]
        first = jnp.where(lane == m, row, first)
        count = jnp.where(lane == m, rows, count)
        row += rows
    place = lax.broadcasted_iota(jnp.int32, (ROWS, PAIRS), 0)
    width = NARROW * TW
    spread = None
    for part in range(PARTS):
        at = jnp.where(count > part, first + part, -1)
        move = jnp.where(place == at, 1.0, 0.0).astype(jnp.bfloat16)
        moved = jnp.dot(
            move, packed[:, part * width : (part + 1) * width], preferred_element_type=jnp.float32
        )
        spread = moved if spread is None else spread + moved
    spread = spread.astype(jnp.bfloat16)
    for s in range(SOURCES):
        out_ref[s] = spread


def send_full_kernel(turn, t_ref, cd_ref, occ_ref, out_ref, choose):
    irreps, ranks = places(cd_ref)
    fill_chooser(choose, ranks, turn)
    _, row_irrep = my_pairs(occ_ref)
    packed = pack(t_ref[...], row_irrep, column_irreps(irreps), choose)
    for s in range(SOURCES):
        out_ref[s, :PAIRS, :] = packed
        out_ref[s, PAIRS:, :] = jnp.zeros((FULL - PAIRS, WIDE * TW), jnp.bfloat16)


def pack_rows_kernel(turn, v_ref, ab_ref, cd_ref, out_ref, choose):
    irreps, ranks = places(cd_ref)
    fill_chooser(choose, ranks, turn)
    row = lax.broadcasted_iota(jnp.int32, (4 * TW, 1), 0) // TW
    row_irrep = jnp.zeros((4 * TW, 1), jnp.int32)
    for i in range(4):
        row_irrep = jnp.where(row == i, ab_ref[i], row_irrep)
    out_ref[...] = pack(v_ref[...], row_irrep, column_irreps(irreps), choose)


def tables_kernel(cd_ref, occ_ref, list_ref, code_ref, kept_ref, orbitals, count, need):
    core = lax.axis_index("blk_2")
    for g in range(IRREPS):
        orbitals[g] = 0

    @pl.loop(0, OCC)
    def _(i):
        g = occ_ref[i]
        orbitals[g] = orbitals[g] + 1

    start = jnp.int32(0)
    most = jnp.int32(0)
    for g in range(IRREPS):
        pairs = jnp.int32(0)
        for h in range(IRREPS):
            pairs += orbitals[h] * orbitals[g ^ h]
        kept_ref[g] = start
        count[g] = start
        start += pairs
        most = jnp.maximum(most, pairs)
    irreps, ranks = places(cd_ref)
    widest = ranks[0]
    for rank in ranks[1:]:
        widest = jnp.maximum(widest, rank)
    count_rows(irreps, need)
    kept_ref[8] = start
    kept_ref[9] = jnp.where(widest < WIDE, 0, 1)
    kept_ref[10] = most
    for k in range(11, KEPT):
        kept_ref[k] = 0

    @pl.loop(0, 8)
    def _(part):
        half = SOURCES * ROWS
        base = [part * 2 * ROWS + jnp.bitwise_xor(other, core) * half for other in range(2)]
        longest = jnp.int32(0)
        row = None
        for i in range(5):
            left = occ_ref[part * 5 + i]
            for j in range(OCC):
                pair = i * OCC + j
                source, m = divmod(pair, PAIRS)
                if m == 0:
                    row = base[source % 2] + source // 2 * ROWS
                    end = row + ROWS
                irrep = jnp.bitwise_xor(left, occ_ref[j])
                at = count[irrep]
                count[irrep] = at + 1
                list_ref[at] = jnp.minimum(row, end - 1)
                code_ref[part * 200 + pair] = at * IRREPS + irrep
                row += need[irrep]
                if m == PAIRS - 1:
                    longest = jnp.maximum(longest, row - end)
        kept_ref[9] = jnp.where(longest > 0, 1, kept_ref[9])

    for k in range(IJ, CODES):
        code_ref[k] = NOWHERE

    @pl.loop(0, (LIST - IJ) // 16)
    def _(k):
        for u in range(16):
            list_ref[IJ + k * 16 + u] = 0


def full_list_kernel(occ_ref, kept_ref, list_ref, count):
    core = lax.axis_index("blk_2")
    for g in range(IRREPS):
        count[g] = kept_ref[g]

    @pl.loop(0, OCC)
    def _(i):
        left = occ_ref[i]

        @pl.loop(0, OCC)
        def _(j):
            pair = i * OCC + j
            irrep = jnp.bitwise_xor(left, occ_ref[j])
            at = count[irrep]
            count[irrep] = at + 1
            source = pair // PAIRS
            chip = jnp.bitwise_xor(source & 1, core) * SOURCES + (source >> 1)
            list_ref[at] = chip * FULL + pair - source * PAIRS

    @pl.loop(IJ, LIST)
    def _(k):
        list_ref[k] = 0


def times(held, weight):
    return lax.dot_general(held, weight, NT, preferred_element_type=jnp.float32)


def joined_product(held_ref, weight_ref):
    held = held_ref[...].astype(jnp.float32)
    count = held.shape[0]
    rows = [held] + [pltpu.roll(held, count - part, 0) for part in range(1, PARTS)]
    joined = jnp.concatenate([r.astype(jnp.bfloat16) for r in rows], axis=1)
    return times(joined, weight_ref[...])


def own_product_kernel(held_ref, weight_ref, left_ref, right_ref):
    total = joined_product(held_ref, weight_ref)
    left_ref[...] = total[:, :128]
    right_ref[...] = total[:, 128:]


def product_kernel(full, round_ref, *refs):
    if full:
        halves, weights, refs = refs[:4], refs[4:6], refs[6:]
    else:
        (*own, other, weight), refs = refs[:4], refs[4:]
    ab_ref, list_ref, kept_ref, out_ref, left_product, right_product, dense, both, sems = refs
    products = (left_product, right_product)
    wire = dense.shape[0]
    cols = wire - 1
    half_rows = SOURCES * (FULL if full else ROWS)

    def keep(half, total):
        at = slice(half * half_rows, (half + 1) * half_rows)
        for q in range(2):
            products[q][at, :] = total[:, q * 128 : (q + 1) * 128]

    if full:
        for half in range(2):
            total = times(halves[half][...], weights[0][...])
            keep(half, total + times(halves[2 + half][...], weights[1][...]))
    else:
        copies = [
            pltpu.make_async_copy(own[q], products[q].at[pl.ds(0, half_rows)], sems.at[q])
            for q in range(2)
        ]
        for copy in copies:
            copy.start()
        keep(1, joined_product(other, weight))
        for copy in copies:
            copy.wait()
    lower = lax.broadcasted_iota(jnp.int32, (1, 128), 1) < TW
    skip = round_ref[0] * cols
    for q in range(2):
        product = products[q]
        dense[...] = jnp.zeros_like(dense)
        irreps = [ab_ref[2 * q + i] for i in range(2)]
        starts = [jnp.minimum(kept_ref[g] + skip, IJ) for g in irreps]
        counts = [kept_ref[g + 1] - kept_ref[g] - skip for g in irreps]
        most = jnp.clip(jnp.maximum(counts[0], counts[1]), 0, cols)

        @pl.loop(0, (most + 7) // 8)
        def _(block):
            base = block * 8
            for u in range(8):
                at = [list_ref[start + base + u] for start in starts]
                rows = [product[pl.ds(a, 1), :] for a in at]
                dense[pl.ds(base + u, 1), :] = jnp.where(lower, rows[0], rows[1])

        both[q * 128 : (q + 1) * 128, :] = dense[...].T
    largest = jnp.max(jnp.max(jnp.abs(both[...]), axis=1, keepdims=True), axis=0, keepdims=True)
    power = 14.0 - jnp.floor(jnp.log2(jnp.maximum(largest, 1e-30)))
    scaled = both[...] * jnp.exp2(power)
    lane = lax.broadcasted_iota(jnp.int32, (4 * TW, wire), 1)
    out_ref[...] = jnp.where(lane == cols, power, scaled).reshape(32, 8, wire)


def finish_kernel(round_ref, got_ref, ab_ref, kept_ref, code_ref, out_ref):
    irrep = ab_ref[lax.axis_index("panel") // 8]
    wire = got_ref.shape[2]
    cols = wire - 1
    total = None
    for s in range(32):
        got = got_ref[s]
        got = got * jnp.exp2(-got[:, cols:])
        total = got if total is None else total + got
    first = kept_ref[irrep] + round_ref[0] * cols
    for block in range(CODES // 128):
        code = jnp.broadcast_to(code_ref[:, block * 128 : (block + 1) * 128], (8, 128))
        place = jnp.where(code % IRREPS == irrep, code // IRREPS - first, -1)
        place = jnp.where(place < cols, place, -1)
        lane = place & 127
        found = jnp.zeros((8, 128), jnp.float32)
        for k in range(wire // 128):
            moved = jnp.take_along_axis(total[:, k * 128 : (k + 1) * 128], lane, axis=1)
            found = jnp.where(place >> 7 == k, moved, found)
        held = min(128, IJ - block * 128)
        out_ref[:, block * 128 : block * 128 + held] = found[:, :held]


def shaped(shape, dtype):
    return jax.ShapeDtypeStruct(shape, dtype)


def body(integrals, amplitudes, ab_irrep, cd_irrep, occ_irrep):
    bf16, f32, i32 = jnp.bfloat16, jnp.float32, jnp.int32
    width = WIDE * TW
    chooser = pltpu.VMEM((16 * TW, width), bf16)
    numbers = pltpu.SMEM((IRREPS,), i32)

    def both_cores(sent):
        mine = lax.all_to_all(sent, CHIPS, split_axis=0, concat_axis=0, tiled=True)
        mine = mine.reshape(sent.shape[0] * sent.shape[1], sent.shape[2])
        return [mine, lax.ppermute(mine, "blk_2", [(0, 1), (1, 0)])]

    def gathered_full(turn):
        sent = pl.pallas_call(
            functools.partial(send_full_kernel, turn),
            out_shape=shaped((SOURCES, FULL, width), bf16),
            in_specs=[VMEM, SMEM, SMEM],
            out_specs=VMEM,
            scratch_shapes=[chooser],
            compiler_params=GRANT,
        )(amplitudes, cd_irrep, occ_irrep)
        return both_cores(sent)

    def weights(turn):
        return pl.pallas_call(
            functools.partial(pack_rows_kernel, turn),
            out_shape=shaped((4 * TW, width), bf16),
            in_specs=[VMEM, SMEM, SMEM],
            out_specs=VMEM,
            scratch_shapes=[chooser],
            compiler_params=GRANT,
        )(integrals, ab_irrep, cd_irrep)

    sent = pl.pallas_call(
        send_kernel,
        out_shape=shaped((SOURCES, ROWS, NARROW * TW), bf16),
        in_specs=[VMEM, SMEM, SMEM],
        out_specs=VMEM,
        scratch_shapes=[chooser, numbers],
        compiler_params=GRANT,
        name="send",
    )(amplitudes, cd_irrep, occ_irrep)
    halves = both_cores(sent)

    pair_list, code, kept = pl.pallas_call(
        tables_kernel,
        out_shape=[shaped((LIST,), i32), shaped((CODES,), i32), shaped((KEPT,), i32)],
        in_specs=[SMEM, SMEM],
        out_specs=[SMEM] * 3,
        scratch_shapes=[numbers] * 3,
        compiler_params=GRANT,
        name="tables",
    )(cd_irrep, occ_irrep)
    code = code.reshape(1, CODES)
    zero = jnp.zeros((1,), i32)
    first_weights = weights(0)

    half_rows = SOURCES * ROWS
    own = pl.pallas_call(
        own_product_kernel,
        out_shape=[shaped((half_rows, 128), f32)] * 2,
        in_specs=[VMEM, VMEM],
        out_specs=[VMEM] * 2,
        compiler_params=GRANT,
        name="own_product",
    )(halves[0], first_weights)

    def products(full, wire, which, operands, pairs):
        rows = 2 * SOURCES * (FULL if full else ROWS)
        specs = [VMEM] * 6 if full else [ANY, ANY, VMEM, VMEM]
        return pl.pallas_call(
            functools.partial(product_kernel, full),
            out_shape=pltpu.VMEM((32, 8, wire), f32),
            in_specs=[SMEM] + specs + [SMEM] * 3,
            out_specs=VMEM,
            scratch_shapes=[
                pltpu.VMEM((rows, 128), f32),
                pltpu.VMEM((rows, 128), f32),
                pltpu.VMEM((wire, 128), f32),
                pltpu.VMEM((4 * TW, wire), f32),
                pltpu.SemaphoreType.DMA((2,)),
            ],
            compiler_params=LARGE,
        )(which, *operands, ab_irrep, pairs, kept)

    def full_products(wire, which):
        pairs = pl.pallas_call(
            full_list_kernel,
            out_shape=shaped((LIST,), i32),
            in_specs=[SMEM] * 2,
            out_specs=SMEM,
            scratch_shapes=[numbers],
            compiler_params=GRANT,
            name="full_list",
        )(occ_irrep, kept)
        operands = [*gathered_full(0), *gathered_full(1), first_weights, weights(1)]
        return products(True, wire, which, operands, pairs)

    general, most = kept[9] > 0, kept[10]

    def reduced(wire, which):
        partial = lax.cond(
            general,
            lambda: full_products(wire, which),
            lambda: products(False, wire, which, [*own, halves[1], first_weights], pair_list),
        ).astype(jnp.float16)
        arrived = lax.all_to_all(partial, "panel", split_axis=0, concat_axis=0, tiled=True)
        return pl.pallas_call(
            finish_kernel,
            out_shape=shaped((8, IJ), f32),
            in_specs=[SMEM, VMEM, SMEM, SMEM, VMEM],
            out_specs=VMEM,
            compiler_params=GRANT,
            name="finish",
        )(which, arrived.astype(f32), ab_irrep, kept, code)

    def all_rounds():
        cols = WIRES[-1] - 1

        def add_round(number, total):
            which = jnp.full((1,), number, i32)
            return total + reduced(WIRES[-1], which)

        return lax.fori_loop(0, (most + cols - 1) // cols, add_round, jnp.zeros((8, IJ), f32))

    branches = [functools.partial(reduced, wire, zero) for wire in WIRES]
    chosen = sum((most >= wire).astype(i32) for wire in WIRES)
    return lax.switch(chosen, [*branches, all_rounds])


def solution(mesh):
    split = Mesh(
        mesh.devices.reshape(2, 8, 2, mesh.shape["panel"]), ("blk_0", "blk_1", "blk_2", "panel")
    )
    return jax.shard_map(
        body,
        mesh=split,
        in_specs=(P(BLK, "panel"), P(BLK, "panel"), P(BLK), P("panel"), P()),
        out_specs=P(BLK_PANEL, None),
        check_vma=False,
    )
```

```python
import functools

import jax
import jax.numpy as jnp
from jax import lax
from jax.experimental import pallas as pl
from jax.experimental.pallas import tpu as pltpu
from jax.sharding import Mesh
from jax.sharding import PartitionSpec as P


TW = 64
IRREPS = 8
OCC = 40
IJ = 1600
BLK = ("blk_0", "blk_1", "blk_2")
BLK_PANEL = ("blk_0", "blk_1", "blk_2", "panel")
CHIPS = ("blk_0", "blk_1")

PAIRS = 50
SOURCES = 16
WIDE = 8
NARROW = 2
PARTS = WIDE // NARROW
ROWS = 144
FULL = 56
WIRES = (512, 640, 896)
CODES = 1664
NOWHERE = 1 << 24
LIST = 2560
KEPT = 16

SMEM = pl.BlockSpec(memory_space=pltpu.SMEM)
VMEM = pl.BlockSpec(memory_space=pltpu.VMEM)
NT = (((1,), (1,)), ((), ()))
GRANT = pltpu.CompilerParams(vmem_limit_bytes=24 << 20)
LARGE = pltpu.CompilerParams(vmem_limit_bytes=40 << 20)


def places(cd_ref):
    irreps = [cd_ref[t] for t in range(16)]
    ranks = []
    for t in range(16):
        rank = jnp.int32(0)
        for earlier in range(t):
            rank += jnp.where(irreps[earlier] == irreps[t], 1, 0)
        ranks.append(rank)
    return irreps, ranks


def fill_chooser(choose, ranks, turn):
    width = WIDE * TW
    row = lax.broadcasted_iota(jnp.int32, (TW, width), 0)
    col = lax.broadcasted_iota(jnp.int32, (TW, width), 1)
    place = jnp.where(col % TW == row, col // TW + turn * WIDE, -1)
    for t in range(16):
        hit = jnp.where(place == ranks[t], 1.0, 0.0)
        choose[t * TW : (t + 1) * TW, :] = hit.astype(jnp.bfloat16)


def column_irreps(irreps):
    lane = lax.broadcasted_iota(jnp.int32, (1, 16 * TW), 1) // TW
    found = jnp.zeros((1, 16 * TW), jnp.int32)
    for t in range(16):
        found = jnp.where(lane == t, irreps[t], found)
    return found


def pack(values, row_irrep, col_irrep, choose):
    kept = jnp.where(row_irrep == col_irrep, values.astype(jnp.float32), 0.0)
    return jnp.dot(
        kept.astype(jnp.bfloat16), choose[...], preferred_element_type=jnp.float32
    ).astype(jnp.bfloat16)


def my_pairs(occ_ref):
    blk = lax.axis_index("blk_0") * 16 + lax.axis_index("blk_1") * 2 + lax.axis_index("blk_2")
    upper = blk * 5 // 4
    at = blk % 4 * 10
    left = [occ_ref[upper], occ_ref[jnp.minimum(upper + 1, OCC - 1)]]
    row = lax.broadcasted_iota(jnp.int32, (PAIRS, 1), 0)
    column = jnp.zeros((PAIRS, 1), jnp.int32)
    irreps = []
    for m in range(PAIRS):
        later = at + m >= OCC
        right = occ_ref[at + m - jnp.where(later, OCC, 0)]
        irreps.append(jnp.bitwise_xor(jnp.where(later, left[1], left[0]), right))
        column = jnp.where(row == m, irreps[m], column)
    return irreps, column


def count_rows(irreps, need):
    for g in range(IRREPS):
        tiles = jnp.int32(0)
        for irrep in irreps:
            tiles += jnp.where(irrep == g, 1, 0)
        need[g] = (tiles + NARROW - 1) // NARROW


def send_kernel(t_ref, cd_ref, occ_ref, out_ref, choose, need):
    irreps, ranks = places(cd_ref)
    fill_chooser(choose, ranks, 0)
    count_rows(irreps, need)
    pairs, row_irrep = my_pairs(occ_ref)
    packed = pack(t_ref[...], row_irrep, column_irreps(irreps), choose)
    lane = lax.broadcasted_iota(jnp.int32, (1, PAIRS), 1)
    first = jnp.zeros((1, PAIRS), jnp.int32)
    count = jnp.zeros((1, PAIRS), jnp.int32)
    row = jnp.int32(0)
    for m in range(PAIRS):
        rows = need[pairs[m]]
        first = jnp.where(lane == m, row, first)
        count = jnp.where(lane == m, rows, count)
        row += rows
    place = lax.broadcasted_iota(jnp.int32, (ROWS, PAIRS), 0)
    width = NARROW * TW
    spread = None
    for part in range(PARTS):
        at = jnp.where(count > part, first + part, -1)
        move = jnp.where(place == at, 1.0, 0.0).astype(jnp.bfloat16)
        moved = jnp.dot(
            move, packed[:, part * width : (part + 1) * width], preferred_element_type=jnp.float32
        )
        spread = moved if spread is None else spread + moved
    spread = spread.astype(jnp.bfloat16)
    for s in range(SOURCES):
        out_ref[s] = spread


def send_full_kernel(turn, t_ref, cd_ref, occ_ref, out_ref, choose):
    irreps, ranks = places(cd_ref)
    fill_chooser(choose, ranks, turn)
    _, row_irrep = my_pairs(occ_ref)
    packed = pack(t_ref[...], row_irrep, column_irreps(irreps), choose)
    for s in range(SOURCES):
        out_ref[s, :PAIRS, :] = packed
        out_ref[s, PAIRS:, :] = jnp.zeros((FULL - PAIRS, WIDE * TW), jnp.bfloat16)


def pack_rows_kernel(turn, v_ref, ab_ref, cd_ref, out_ref, choose):
    irreps, ranks = places(cd_ref)
    fill_chooser(choose, ranks, turn)
    row = lax.broadcasted_iota(jnp.int32, (4 * TW, 1), 0) // TW
    row_irrep = jnp.zeros((4 * TW, 1), jnp.int32)
    for i in range(4):
        row_irrep = jnp.where(row == i, ab_ref[i], row_irrep)
    out_ref[...] = pack(v_ref[...], row_irrep, column_irreps(irreps), choose)


def tables_kernel(cd_ref, occ_ref, list_ref, code_ref, kept_ref, orbitals, count, need):
    core = lax.axis_index("blk_2")
    for g in range(IRREPS):
        orbitals[g] = 0

    @pl.loop(0, OCC)
    def _(i):
        g = occ_ref[i]
        orbitals[g] = orbitals[g] + 1

    start = jnp.int32(0)
    most = jnp.int32(0)
    for g in range(IRREPS):
        pairs = jnp.int32(0)
        for h in range(IRREPS):
            pairs += orbitals[h] * orbitals[g ^ h]
        kept_ref[g] = start
        count[g] = start
        start += pairs
        most = jnp.maximum(most, pairs)
    irreps, ranks = places(cd_ref)
    widest = ranks[0]
    for rank in ranks[1:]:
        widest = jnp.maximum(widest, rank)
    count_rows(irreps, need)
    kept_ref[8] = start
    kept_ref[9] = jnp.where(widest < WIDE, 0, 1)
    kept_ref[10] = most
    for k in range(11, KEPT):
        kept_ref[k] = 0

    @pl.loop(0, 8)
    def _(part):
        half = SOURCES * ROWS
        base = [part * 2 * ROWS + jnp.bitwise_xor(other, core) * half for other in range(2)]
        longest = jnp.int32(0)
        row = None
        for i in range(5):
            left = occ_ref[part * 5 + i]
            for j in range(OCC):
                pair = i * OCC + j
                source, m = divmod(pair, PAIRS)
                if m == 0:
                    row = base[source % 2] + source // 2 * ROWS
                    end = row + ROWS
                irrep = jnp.bitwise_xor(left, occ_ref[j])
                at = count[irrep]
                count[irrep] = at + 1
                list_ref[at] = jnp.minimum(row, end - 1)
                code_ref[part * 200 + pair] = at * IRREPS + irrep
                row += need[irrep]
                if m == PAIRS - 1:
                    longest = jnp.maximum(longest, row - end)
        kept_ref[9] = jnp.where(longest > 0, 1, kept_ref[9])

    for k in range(IJ, CODES):
        code_ref[k] = NOWHERE

    @pl.loop(0, (LIST - IJ) // 16)
    def _(k):
        for u in range(16):
            list_ref[IJ + k * 16 + u] = 0


def full_list_kernel(occ_ref, kept_ref, list_ref, count):
    core = lax.axis_index("blk_2")
    for g in range(IRREPS):
        count[g] = kept_ref[g]

    @pl.loop(0, OCC)
    def _(i):
        left = occ_ref[i]

        @pl.loop(0, OCC)
        def _(j):
            pair = i * OCC + j
            irrep = jnp.bitwise_xor(left, occ_ref[j])
            at = count[irrep]
            count[irrep] = at + 1
            source = pair // PAIRS
            chip = jnp.bitwise_xor(source & 1, core) * SOURCES + (source >> 1)
            list_ref[at] = chip * FULL + pair - source * PAIRS

    @pl.loop(IJ, LIST)
    def _(k):
        list_ref[k] = 0


def product_kernel(full, round_ref, *refs):
    turns = 2 if full else 1
    half_rows = SOURCES * (FULL if full else ROWS)
    halves, weights = refs[: 2 * turns], refs[2 * turns : 3 * turns]
    ab_ref, list_ref, kept_ref, out_ref, left_product, right_product, dense, both = refs[3 * turns :]
    products = (left_product, right_product)
    wire = dense.shape[0]
    cols = wire - 1

    def times(held, weight):
        return lax.dot_general(held, weight, NT, preferred_element_type=jnp.float32)

    for half in range(2):
        if full:
            total = times(halves[half][...], weights[0][...])
            total += times(halves[2 + half][...], weights[1][...])
        else:
            held = halves[half][...].astype(jnp.float32)
            rows = [held] + [pltpu.roll(held, half_rows - part, 0) for part in range(1, PARTS)]
            joined = jnp.concatenate([r.astype(jnp.bfloat16) for r in rows], axis=1)
            total = times(joined, weights[0][...])
        for q in range(2):
            at = slice(half * half_rows, (half + 1) * half_rows)
            products[q][at, :] = total[:, q * 128 : (q + 1) * 128]
    lower = lax.broadcasted_iota(jnp.int32, (1, 128), 1) < TW
    skip = round_ref[0] * cols
    for q in range(2):
        product = products[q]
        dense[...] = jnp.zeros_like(dense)
        irreps = [ab_ref[2 * q + i] for i in range(2)]
        starts = [jnp.minimum(kept_ref[g] + skip, IJ) for g in irreps]
        counts = [kept_ref[g + 1] - kept_ref[g] - skip for g in irreps]
        most = jnp.clip(jnp.maximum(counts[0], counts[1]), 0, cols)

        @pl.loop(0, (most + 7) // 8)
        def _(block):
            base = block * 8
            for u in range(8):
                at = [list_ref[start + base + u] for start in starts]
                rows = [product[pl.ds(a, 1), :] for a in at]
                dense[pl.ds(base + u, 1), :] = jnp.where(lower, rows[0], rows[1])

        both[q * 128 : (q + 1) * 128, :] = dense[...].T
    largest = jnp.max(jnp.max(jnp.abs(both[...]), axis=1, keepdims=True), axis=0, keepdims=True)
    power = 14.0 - jnp.floor(jnp.log2(jnp.maximum(largest, 1e-30)))
    scaled = both[...] * jnp.exp2(power)
    lane = lax.broadcasted_iota(jnp.int32, (4 * TW, wire), 1)
    out_ref[...] = jnp.where(lane == cols, power, scaled).reshape(32, 8, wire)


def finish_kernel(round_ref, got_ref, ab_ref, kept_ref, code_ref, out_ref):
    irrep = ab_ref[lax.axis_index("panel") // 8]
    wire = got_ref.shape[2]
    cols = wire - 1
    total = None
    for s in range(32):
        got = got_ref[s]
        got = got * jnp.exp2(-got[:, cols:])
        total = got if total is None else total + got
    first = kept_ref[irrep] + round_ref[0] * cols
    for block in range(CODES // 128):
        code = jnp.broadcast_to(code_ref[:, block * 128 : (block + 1) * 128], (8, 128))
        place = jnp.where(code % IRREPS == irrep, code // IRREPS - first, -1)
        place = jnp.where(place < cols, place, -1)
        lane = place & 127
        found = jnp.zeros((8, 128), jnp.float32)
        for k in range(wire // 128):
            moved = jnp.take_along_axis(total[:, k * 128 : (k + 1) * 128], lane, axis=1)
            found = jnp.where(place >> 7 == k, moved, found)
        held = min(128, IJ - block * 128)
        out_ref[:, block * 128 : block * 128 + held] = found[:, :held]


def shaped(shape, dtype):
    return jax.ShapeDtypeStruct(shape, dtype)


def body(integrals, amplitudes, ab_irrep, cd_irrep, occ_irrep):
    bf16, f32, i32 = jnp.bfloat16, jnp.float32, jnp.int32
    width = WIDE * TW
    chooser = pltpu.VMEM((16 * TW, width), bf16)
    numbers = pltpu.SMEM((IRREPS,), i32)

    def both_cores(sent):
        mine = lax.all_to_all(sent, CHIPS, split_axis=0, concat_axis=0, tiled=True)
        mine = mine.reshape(sent.shape[0] * sent.shape[1], sent.shape[2])
        return [mine, lax.ppermute(mine, "blk_2", [(0, 1), (1, 0)])]

    def gathered_full(turn):
        sent = pl.pallas_call(
            functools.partial(send_full_kernel, turn),
            out_shape=shaped((SOURCES, FULL, width), bf16),
            in_specs=[VMEM, SMEM, SMEM],
            out_specs=VMEM,
            scratch_shapes=[chooser],
            compiler_params=GRANT,
        )(amplitudes, cd_irrep, occ_irrep)
        return both_cores(sent)

    def weights(turn):
        return pl.pallas_call(
            functools.partial(pack_rows_kernel, turn),
            out_shape=shaped((4 * TW, width), bf16),
            in_specs=[VMEM, SMEM, SMEM],
            out_specs=VMEM,
            scratch_shapes=[chooser],
            compiler_params=GRANT,
        )(integrals, ab_irrep, cd_irrep)

    sent = pl.pallas_call(
        send_kernel,
        out_shape=shaped((SOURCES, ROWS, NARROW * TW), bf16),
        in_specs=[VMEM, SMEM, SMEM],
        out_specs=VMEM,
        scratch_shapes=[chooser, numbers],
        compiler_params=GRANT,
        name="send",
    )(amplitudes, cd_irrep, occ_irrep)
    halves = both_cores(sent)

    pair_list, code, kept = pl.pallas_call(
        tables_kernel,
        out_shape=[shaped((LIST,), i32), shaped((CODES,), i32), shaped((KEPT,), i32)],
        in_specs=[SMEM, SMEM],
        out_specs=[SMEM] * 3,
        scratch_shapes=[numbers] * 3,
        compiler_params=GRANT,
        name="tables",
    )(cd_irrep, occ_irrep)
    code = code.reshape(1, CODES)
    zero = jnp.zeros((1,), i32)
    first_weights = weights(0)

    def products(full, wire, which, operands, pairs):
        rows = 2 * SOURCES * (FULL if full else ROWS)
        return pl.pallas_call(
            functools.partial(product_kernel, full),
            out_shape=pltpu.VMEM((32, 8, wire), f32),
            in_specs=[SMEM] + [VMEM] * len(operands) + [SMEM] * 3,
            out_specs=VMEM,
            scratch_shapes=[
                pltpu.VMEM((rows, 128), f32),
                pltpu.VMEM((rows, 128), f32),
                pltpu.VMEM((wire, 128), f32),
                pltpu.VMEM((4 * TW, wire), f32),
            ],
            compiler_params=LARGE,
        )(which, *operands, ab_irrep, pairs, kept)

    def full_products(wire, which):
        pairs = pl.pallas_call(
            full_list_kernel,
            out_shape=shaped((LIST,), i32),
            in_specs=[SMEM] * 2,
            out_specs=SMEM,
            scratch_shapes=[numbers],
            compiler_params=GRANT,
            name="full_list",
        )(occ_irrep, kept)
        operands = [*gathered_full(0), *gathered_full(1), first_weights, weights(1)]
        return products(True, wire, which, operands, pairs)

    general, most = kept[9] > 0, kept[10]

    def reduced(wire, which):
        partial = lax.cond(
            general,
            lambda: full_products(wire, which),
            lambda: products(False, wire, which, [*halves, first_weights], pair_list),
        ).astype(jnp.float16)
        arrived = lax.all_to_all(partial, "panel", split_axis=0, concat_axis=0, tiled=True)
        return pl.pallas_call(
            finish_kernel,
            out_shape=shaped((8, IJ), f32),
            in_specs=[SMEM, VMEM, SMEM, SMEM, VMEM],
            out_specs=VMEM,
            compiler_params=GRANT,
            name="finish",
        )(which, arrived.astype(f32), ab_irrep, kept, code)

    def all_rounds():
        cols = WIRES[-1] - 1

        def add_round(number, total):
            which = jnp.full((1,), number, i32)
            return total + reduced(WIRES[-1], which)

        return lax.fori_loop(0, (most + cols - 1) // cols, add_round, jnp.zeros((8, IJ), f32))

    branches = [functools.partial(reduced, wire, zero) for wire in WIRES]
    chosen = sum((most >= wire).astype(i32) for wire in WIRES)
    return lax.switch(chosen, [*branches, all_rounds])


def solution(mesh):
    split = Mesh(
        mesh.devices.reshape(2, 8, 2, mesh.shape["panel"]), ("blk_0", "blk_1", "blk_2", "panel")
    )
    return jax.shard_map(
        body,
        mesh=split,
        in_specs=(P(BLK, "panel"), P(BLK, "panel"), P(BLK), P("panel"), P()),
        out_specs=P(BLK_PANEL, None),
        check_vma=False,
    )
```

```python
import functools

import jax
import jax.numpy as jnp
from jax import lax
from jax.experimental import pallas as pl
from jax.experimental.pallas import tpu as pltpu
from jax.sharding import Mesh
from jax.sharding import PartitionSpec as P


TW = 64
IRREPS = 8
OCC = 40
IJ = 1600
BLK = ("blk_0", "blk_1", "blk_2")
BLK_PANEL = ("blk_0", "blk_1", "blk_2", "panel")
CHIPS = ("blk_0", "blk_1")

PAIRS = 50
SOURCES = 16
WIDE = 8
NARROW = 2
PARTS = WIDE // NARROW
ROWS = 144
FULL = 56
WIRES = (256, 384, 512)
LIST = 1408
KEPT = 16

SMEM = pl.BlockSpec(memory_space=pltpu.SMEM)
VMEM = pl.BlockSpec(memory_space=pltpu.VMEM)
NT = (((1,), (1,)), ((), ()))
GRANT = pltpu.CompilerParams(vmem_limit_bytes=24 << 20)
LARGE = pltpu.CompilerParams(vmem_limit_bytes=40 << 20)


def places(cd_ref):
    irreps = [cd_ref[t] for t in range(16)]
    ranks = []
    for t in range(16):
        rank = jnp.int32(0)
        for earlier in range(t):
            rank += jnp.where(irreps[earlier] == irreps[t], 1, 0)
        ranks.append(rank)
    return irreps, ranks


def fill_chooser(choose, ranks, turn):
    width = WIDE * TW
    row = lax.broadcasted_iota(jnp.int32, (TW, width), 0)
    col = lax.broadcasted_iota(jnp.int32, (TW, width), 1)
    place = jnp.where(col % TW == row, col // TW + turn * WIDE, -1)
    for t in range(16):
        hit = jnp.where(place == ranks[t], 1.0, 0.0)
        choose[t * TW : (t + 1) * TW, :] = hit.astype(jnp.bfloat16)


def column_irreps(irreps):
    lane = lax.broadcasted_iota(jnp.int32, (1, 16 * TW), 1) // TW
    found = jnp.zeros((1, 16 * TW), jnp.int32)
    for t in range(16):
        found = jnp.where(lane == t, irreps[t], found)
    return found


def pack(values, row_irrep, col_irrep, choose):
    kept = jnp.where(row_irrep == col_irrep, values.astype(jnp.float32), 0.0)
    return jnp.dot(
        kept.astype(jnp.bfloat16), choose[...], preferred_element_type=jnp.float32
    ).astype(jnp.bfloat16)


def my_pairs(occ_ref):
    blk = lax.axis_index("blk_0") * 16 + lax.axis_index("blk_1") * 2 + lax.axis_index("blk_2")
    upper = blk * 5 // 4
    at = blk % 4 * 10
    left = [occ_ref[upper], occ_ref[jnp.minimum(upper + 1, OCC - 1)]]
    row = lax.broadcasted_iota(jnp.int32, (PAIRS, 1), 0)
    column = jnp.zeros((PAIRS, 1), jnp.int32)
    irreps = []
    for m in range(PAIRS):
        later = at + m >= OCC
        right = occ_ref[at + m - jnp.where(later, OCC, 0)]
        irreps.append(jnp.bitwise_xor(jnp.where(later, left[1], left[0]), right))
        column = jnp.where(row == m, irreps[m], column)
    return irreps, column


def count_rows(irreps, need):
    for g in range(IRREPS):
        tiles = jnp.int32(0)
        for irrep in irreps:
            tiles += jnp.where(irrep == g, 1, 0)
        need[g] = (tiles + NARROW - 1) // NARROW


def send_kernel(t_ref, cd_ref, occ_ref, out_ref, choose, need):
    irreps, ranks = places(cd_ref)
    fill_chooser(choose, ranks, 0)
    count_rows(irreps, need)
    pairs, row_irrep = my_pairs(occ_ref)
    packed = pack(t_ref[...], row_irrep, column_irreps(irreps), choose)
    lane = lax.broadcasted_iota(jnp.int32, (1, PAIRS), 1)
    first = jnp.zeros((1, PAIRS), jnp.int32)
    count = jnp.zeros((1, PAIRS), jnp.int32)
    row = jnp.int32(0)
    for m in range(PAIRS):
        rows = need[pairs[m]]
        first = jnp.where(lane == m, row, first)
        count = jnp.where(lane == m, rows, count)
        row += rows
    place = lax.broadcasted_iota(jnp.int32, (ROWS, PAIRS), 0)
    width = NARROW * TW
    spread = None
    for part in range(PARTS):
        at = jnp.where(count > part, first + part, -1)
        move = jnp.where(place == at, 1.0, 0.0).astype(jnp.bfloat16)
        moved = jnp.dot(
            move, packed[:, part * width : (part + 1) * width], preferred_element_type=jnp.float32
        )
        spread = moved if spread is None else spread + moved
    spread = spread.astype(jnp.bfloat16)
    for s in range(SOURCES):
        out_ref[s] = spread


def send_full_kernel(turn, t_ref, cd_ref, occ_ref, out_ref, choose):
    irreps, ranks = places(cd_ref)
    fill_chooser(choose, ranks, turn)
    _, row_irrep = my_pairs(occ_ref)
    packed = pack(t_ref[...], row_irrep, column_irreps(irreps), choose)
    for s in range(SOURCES):
        out_ref[s, :PAIRS, :] = packed
        out_ref[s, PAIRS:, :] = jnp.zeros((FULL - PAIRS, WIDE * TW), jnp.bfloat16)


def pack_rows_kernel(turn, v_ref, ab_ref, cd_ref, out_ref, choose):
    irreps, ranks = places(cd_ref)
    fill_chooser(choose, ranks, turn)
    row = lax.broadcasted_iota(jnp.int32, (4 * TW, 1), 0) // TW
    row_irrep = jnp.zeros((4 * TW, 1), jnp.int32)
    for i in range(4):
        row_irrep = jnp.where(row == i, ab_ref[i], row_irrep)
    out_ref[...] = pack(v_ref[...], row_irrep, column_irreps(irreps), choose)


def list_kernel(cd_ref, occ_ref, counts_ref, list_ref, kept_ref, count, need):
    core = lax.axis_index("blk_2")
    irreps, _ = places(cd_ref)
    count_rows(irreps, need)
    start = jnp.int32(0)
    for g in range(IRREPS):
        kept_ref[g] = start
        count[g] = start
        start += counts_ref[core * IRREPS + g]
    for k in range(IRREPS, KEPT):
        kept_ref[k] = start

    for mine in range(2):

        @pl.when(core == mine)
        def _():
            @pl.loop(0, 8)
            def _(part):
                for chip in range(2):
                    row = (part * 2 + chip) * ROWS
                    last = row + ROWS - 1
                    for m in range(PAIRS):
                        i, j = divmod((chip * 2 + mine) * PAIRS + m, OCC)
                        if m == 0 or j == 0:
                            left = occ_ref[part * 5 + i]
                        irrep = jnp.bitwise_xor(left, occ_ref[j])
                        at = count[irrep]
                        count[irrep] = at + 1
                        list_ref[at] = jnp.minimum(row, last)
                        row += need[irrep]

    @pl.loop(0, (LIST - IJ // 2) // 16)
    def _(k):
        for u in range(16):
            list_ref[IJ // 2 + k * 16 + u] = 0


def full_list_kernel(occ_ref, kept_ref, list_ref, count):
    core = lax.axis_index("blk_2")
    for g in range(IRREPS):
        count[g] = kept_ref[g]

    @pl.loop(0, OCC)
    def _(i):
        left = occ_ref[i]

        @pl.loop(0, OCC)
        def _(j):
            pair = i * OCC + j
            source = pair // PAIRS

            @pl.when((source & 1) == core)
            def _():
                irrep = jnp.bitwise_xor(left, occ_ref[j])
                at = count[irrep]
                count[irrep] = at + 1
                list_ref[at] = (source >> 1) * FULL + pair - source * PAIRS

    @pl.loop(IJ // 2, LIST)
    def _(k):
        list_ref[k] = 0


def times(held, weight):
    return lax.dot_general(held, weight, NT, preferred_element_type=jnp.float32)


def joined_rows(held_ref):
    held = held_ref[...].astype(jnp.float32)
    count = held.shape[0]
    rows = [held] + [pltpu.roll(held, count - part, 0) for part in range(1, PARTS)]
    return jnp.concatenate([r.astype(jnp.bfloat16) for r in rows], axis=1)


def product_kernel(full, round_ref, *refs):
    turns = 2 if full else 1
    held, weights, refs = refs[:turns], refs[turns : 3 * turns], refs[3 * turns :]
    *ab_refs, list_ref, kept_ref, out_ref = refs[:5]
    *products, dense, both = refs[5:]
    wire = dense.shape[0]
    cols = wire - 1
    rows = [ref[...] for ref in held] if full else [joined_rows(held[0])]
    for core in range(2):
        total = None
        for turn in range(turns):
            part = times(rows[turn], weights[2 * turn + core][...])
            total = part if total is None else total + part
        for q in range(2):
            products[2 * core + q][...] = total[:, q * 128 : (q + 1) * 128]
    lower = lax.broadcasted_iota(jnp.int32, (1, 128), 1) < TW
    skip = round_ref[0] * cols
    for q in range(4):
        product = products[q]
        dense[...] = jnp.zeros_like(dense)
        irreps = [ab_refs[q // 2][2 * (q % 2) + i] for i in range(2)]
        starts = [jnp.minimum(kept_ref[g] + skip, IJ // 2) for g in irreps]
        counts = [kept_ref[g + 1] - kept_ref[g] - skip for g in irreps]
        most = jnp.clip(jnp.maximum(counts[0], counts[1]), 0, cols)

        @pl.loop(0, (most + 7) // 8)
        def _(block):
            base = block * 8
            for u in range(8):
                at = [list_ref[start + base + u] for start in starts]
                picked = [product[pl.ds(a, 1), :] for a in at]
                dense[pl.ds(base + u, 1), :] = jnp.where(lower, picked[0], picked[1])

        both[q * 128 : (q + 1) * 128, :] = dense[...].T
    largest = jnp.max(jnp.max(jnp.abs(both[...]), axis=1, keepdims=True), axis=0, keepdims=True)
    power = 14.0 - jnp.floor(jnp.log2(jnp.maximum(largest, 1e-30)))
    lane = lax.broadcasted_iota(jnp.int32, (4 * TW, wire), 1)
    for core in range(2):
        scaled = both[core * 4 * TW : (core + 1) * 4 * TW, :] * jnp.exp2(power)
        sent = jnp.where(lane == cols, power, scaled).reshape(32, 8, wire)
        out_ref[:, core * 8 : (core + 1) * 8, :] = sent


def sum_kernel(got_ref, mine_ref, partner_ref):
    cols = got_ref.shape[2] - 1
    total = None
    for s in range(32):
        got = got_ref[s]
        got = got * jnp.exp2(-got[:, cols:])
        total = got if total is None else total + got
    mine_ref[...] = total[:8]
    partner_ref[...] = total[8:]


def finish_kernel(round_ref, mine_ref, partner_ref, ab_ref, pairs_ref, out_ref):
    core = lax.axis_index("blk_2")
    irrep = ab_ref[lax.axis_index("panel") // 8]
    wire = mine_ref.shape[1]
    cols = wire - 1
    pairs = pairs_ref[...]
    hits = [pairs == irrep + core * IRREPS, pairs == irrep + (1 - core) * IRREPS]
    count = jnp.where(hits[0], 1, jnp.where(hits[1], 1 << 16, 0))
    row = lax.broadcasted_iota(jnp.int32, pairs.shape, 0)
    lane = lax.broadcasted_iota(jnp.int32, pairs.shape, 1)
    for step in (1, 2, 4, 8, 16, 32, 64):
        count += jnp.where(lane >= step, pltpu.roll(count, step, 1), 0)
    whole = jnp.broadcast_to(count[:, 127:], pairs.shape)
    above = whole
    for step in (1, 2, 4, 8):
        above += jnp.where(row >= step, pltpu.roll(above, step, 0), 0)
    count += above - whole
    skip = round_ref[0] * cols + 1
    places_of = []
    for hit, found in zip(hits, (count & 0xFFFF, count >> 16)):
        place = jnp.where(hit, found - skip, -1)
        places_of.append(jnp.where(place < cols, place, -1))
    sources = [mine_ref[...], partner_ref[...]]
    for block in range(13):
        spread = jnp.zeros((8, 128), jnp.float32)
        for place, source in zip(places_of, sources):
            at = jnp.broadcast_to(place[block : block + 1, :], (8, 128))
            for k in range(wire // 128):
                moved = jnp.take_along_axis(source[:, k * 128 : (k + 1) * 128], at & 127, axis=1)
                spread = jnp.where(at >> 7 == k, moved, spread)
        held = min(128, IJ - block * 128)
        out_ref[:, block * 128 : block * 128 + held] = spread[:, :held]


def shaped(shape, dtype):
    return jax.ShapeDtypeStruct(shape, dtype)


def body(integrals, amplitudes, ab_irrep, cd_irrep, occ_irrep):
    bf16, f32, i32 = jnp.bfloat16, jnp.float32, jnp.int32
    width = WIDE * TW
    chooser = pltpu.VMEM((16 * TW, width), bf16)
    numbers = pltpu.SMEM((IRREPS,), i32)

    def over_chips(sent):
        got = lax.all_to_all(sent, CHIPS, split_axis=0, concat_axis=0, tiled=True)
        return got.reshape(sent.shape[0] * sent.shape[1], sent.shape[2])

    def swapped(array):
        return lax.ppermute(array, "blk_2", [(0, 1), (1, 0)])

    def gathered_full(turn):
        sent = pl.pallas_call(
            functools.partial(send_full_kernel, turn),
            out_shape=shaped((SOURCES, FULL, width), bf16),
            in_specs=[VMEM, SMEM, SMEM],
            out_specs=VMEM,
            scratch_shapes=[chooser],
            compiler_params=GRANT,
        )(amplitudes, cd_irrep, occ_irrep)
        return over_chips(sent)

    def weights(turn):
        mine = pl.pallas_call(
            functools.partial(pack_rows_kernel, turn),
            out_shape=shaped((4 * TW, width), bf16),
            in_specs=[VMEM, SMEM, SMEM],
            out_specs=VMEM,
            scratch_shapes=[chooser],
            compiler_params=GRANT,
        )(integrals, ab_irrep, cd_irrep)
        return [mine, swapped(mine)]

    sent = pl.pallas_call(
        send_kernel,
        out_shape=shaped((SOURCES, ROWS, NARROW * TW), bf16),
        in_specs=[VMEM, SMEM, SMEM],
        out_specs=VMEM,
        scratch_shapes=[chooser, numbers],
        compiler_params=GRANT,
        name="send",
    )(amplitudes, cd_irrep, occ_irrep)
    held = over_chips(sent)

    irrep = jnp.bitwise_xor(occ_irrep[:, None], occ_irrep[None, :]).reshape(32, PAIRS)
    kinds = irrep + jnp.arange(32, dtype=i32)[:, None] % 2 * IRREPS
    numbered = jnp.arange(2 * IRREPS, dtype=i32)
    counts = jnp.sum((kinds == numbered[:, None, None]).astype(i32), axis=(1, 2))
    tiles = jnp.sum((cd_irrep == numbered[:IRREPS, None]).astype(i32), axis=1)
    need = (tiles + NARROW - 1) // NARROW
    alike = irrep == numbered[:IRREPS, None, None]
    rows = jnp.sum(jnp.where(alike, need[:, None, None], 0), axis=(0, 2))
    general = jnp.logical_or(jnp.max(rows) > ROWS, jnp.max(tiles) > WIDE)
    most = jnp.max(counts)
    pairs = jnp.pad(kinds.reshape(IJ), (0, 2048 - IJ), constant_values=2 * IRREPS)
    pairs = pairs.reshape(16, 128)

    first_weights = weights(0)
    irreps = [ab_irrep, swapped(ab_irrep)]

    pair_list, kept = pl.pallas_call(
        list_kernel,
        out_shape=[shaped((LIST,), i32), shaped((KEPT,), i32)],
        in_specs=[SMEM] * 3,
        out_specs=[SMEM] * 2,
        scratch_shapes=[numbers] * 2,
        compiler_params=GRANT,
        name="list",
    )(cd_irrep, occ_irrep, counts)

    def products(full, wire, which, operands, rows_list):
        rows = SOURCES * (FULL if full else ROWS)
        return pl.pallas_call(
            functools.partial(product_kernel, full),
            out_shape=pltpu.VMEM((32, 16, wire), f32),
            in_specs=[SMEM] + [VMEM] * len(operands) + [SMEM] * 4,
            out_specs=VMEM,
            scratch_shapes=[pltpu.VMEM((rows, 128), f32)] * 4
            + [pltpu.VMEM((wire, 128), f32), pltpu.VMEM((8 * TW, wire), f32)],
            compiler_params=LARGE,
        )(which, *operands, *irreps, rows_list, kept)

    def full_products(wire, which):
        rows_list = pl.pallas_call(
            full_list_kernel,
            out_shape=shaped((LIST,), i32),
            in_specs=[SMEM] * 2,
            out_specs=SMEM,
            scratch_shapes=[numbers],
            compiler_params=GRANT,
            name="full_list",
        )(occ_irrep, kept)
        operands = [gathered_full(0), gathered_full(1), *first_weights, *weights(1)]
        return products(True, wire, which, operands, rows_list)

    def reduced(wire, which):
        partial = lax.cond(
            general,
            lambda: full_products(wire, which),
            lambda: products(False, wire, which, [held, *first_weights], pair_list),
        ).astype(jnp.float16)
        arrived = lax.all_to_all(partial, "panel", split_axis=0, concat_axis=0, tiled=True)
        mine, partners = pl.pallas_call(
            sum_kernel,
            out_shape=[shaped((8, wire), f32)] * 2,
            in_specs=[VMEM],
            out_specs=[VMEM] * 2,
            compiler_params=GRANT,
            name="sum",
        )(arrived.astype(f32))
        return pl.pallas_call(
            finish_kernel,
            out_shape=shaped((8, IJ), f32),
            in_specs=[SMEM, VMEM, VMEM, SMEM, VMEM],
            out_specs=VMEM,
            compiler_params=GRANT,
            name="finish",
        )(which, mine, swapped(partners), ab_irrep, pairs)

    zero = jnp.zeros((1,), i32)

    def all_rounds():
        cols = WIRES[-1] - 1

        def add_round(number, total):
            which = jnp.full((1,), number, i32)
            return total + reduced(WIRES[-1], which)

        return lax.fori_loop(0, (most + cols - 1) // cols, add_round, jnp.zeros((8, IJ), f32))

    branches = [functools.partial(reduced, wire, zero) for wire in WIRES]
    chosen = sum((most >= wire).astype(i32) for wire in WIRES)
    return lax.switch(chosen, [*branches, all_rounds])


def solution(mesh):
    split = Mesh(
        mesh.devices.reshape(2, 8, 2, mesh.shape["panel"]), ("blk_0", "blk_1", "blk_2", "panel")
    )
    return jax.shard_map(
        body,
        mesh=split,
        in_specs=(P(BLK, "panel"), P(BLK, "panel"), P(BLK), P("panel"), P()),
        out_specs=P(BLK_PANEL, None),
        check_vma=False,
    )
```

```python
import functools

import jax
import jax.numpy as jnp
import numpy as np
from jax import lax
from jax.experimental import pallas as pl
from jax.experimental.pallas import tpu as pltpu
from jax.sharding import Mesh
from jax.sharding import PartitionSpec as P


TW = 64
IRREPS = 8
OCC = 40
IJ = 1600
BLK = ("blk_0", "blk_1", "blk_2")
BLK_PANEL = ("blk_0", "blk_1", "blk_2", "panel")
CHIPS = ("blk_0", "blk_1")

PAIRS = 50
SOURCES = 16
WIDE = 8
NARROW = 2
PARTS = WIDE // NARROW
ROWS = 144
FULL = 56
WIRES = (256, 384)
LONG = 512
KEPT = 24
LIST = KEPT + 1384

SMEM = pl.BlockSpec(memory_space=pltpu.SMEM)
VMEM = pl.BlockSpec(memory_space=pltpu.VMEM)
NT = (((1,), (1,)), ((), ()))
GRANT = pltpu.CompilerParams(vmem_limit_bytes=24 << 20)
LARGE = pltpu.CompilerParams(vmem_limit_bytes=40 << 20)


def places(cd_ref):
    irreps = [cd_ref[t] for t in range(16)]
    ranks = []
    for t in range(16):
        rank = jnp.int32(0)
        for earlier in range(t):
            rank += jnp.where(irreps[earlier] == irreps[t], 1, 0)
        ranks.append(rank)
    return irreps, ranks


def fill_chooser(choose, ranks, turn):
    width = WIDE * TW
    row = lax.broadcasted_iota(jnp.int32, (TW, width), 0)
    col = lax.broadcasted_iota(jnp.int32, (TW, width), 1)
    place = jnp.where(col % TW == row, col // TW + turn * WIDE, -1)
    for t in range(16):
        hit = jnp.where(place == ranks[t], 1.0, 0.0)
        choose[t * TW : (t + 1) * TW, :] = hit.astype(jnp.bfloat16)


def column_irreps(irreps):
    lane = lax.broadcasted_iota(jnp.int32, (1, 16 * TW), 1) // TW
    found = jnp.zeros((1, 16 * TW), jnp.int32)
    for t in range(16):
        found = jnp.where(lane == t, irreps[t], found)
    return found


def pack(values, row_irrep, col_irrep, choose):
    kept = jnp.where(row_irrep == col_irrep, values.astype(jnp.float32), 0.0)
    return jnp.dot(
        kept.astype(jnp.bfloat16), choose[...], preferred_element_type=jnp.float32
    ).astype(jnp.bfloat16)


def my_pairs(occ_ref):
    blk = lax.axis_index("blk_0") * 16 + lax.axis_index("blk_1") * 2 + lax.axis_index("blk_2")
    upper = blk * 5 // 4
    at = blk % 4 * 10
    left = [occ_ref[upper], occ_ref[jnp.minimum(upper + 1, OCC - 1)]]
    row = lax.broadcasted_iota(jnp.int32, (PAIRS, 1), 0)
    column = jnp.zeros((PAIRS, 1), jnp.int32)
    irreps = []
    for m in range(PAIRS):
        later = at + m >= OCC
        right = occ_ref[at + m - jnp.where(later, OCC, 0)]
        irreps.append(jnp.bitwise_xor(jnp.where(later, left[1], left[0]), right))
        column = jnp.where(row == m, irreps[m], column)
    return irreps, column


def count_rows(irreps, need):
    for g in range(IRREPS):
        tiles = jnp.int32(0)
        for irrep in irreps:
            tiles += jnp.where(irrep == g, 1, 0)
        need[g] = (tiles + NARROW - 1) // NARROW


def send_kernel(t_ref, cd_ref, occ_ref, out_ref, choose, need):
    irreps, ranks = places(cd_ref)
    fill_chooser(choose, ranks, 0)
    count_rows(irreps, need)
    pairs, row_irrep = my_pairs(occ_ref)
    packed = pack(t_ref[...], row_irrep, column_irreps(irreps), choose)
    lane = lax.broadcasted_iota(jnp.int32, (1, PAIRS), 1)
    first = jnp.zeros((1, PAIRS), jnp.int32)
    count = jnp.zeros((1, PAIRS), jnp.int32)
    row = jnp.int32(0)
    for m in range(PAIRS):
        rows = need[pairs[m]]
        first = jnp.where(lane == m, row, first)
        count = jnp.where(lane == m, rows, count)
        row += rows
    place = lax.broadcasted_iota(jnp.int32, (ROWS, PAIRS), 0)
    width = NARROW * TW
    spread = None
    for part in range(PARTS):
        at = jnp.where(count > part, first + part, -1)
        move = jnp.where(place == at, 1.0, 0.0).astype(jnp.bfloat16)
        moved = jnp.dot(
            move, packed[:, part * width : (part + 1) * width], preferred_element_type=jnp.float32
        )
        spread = moved if spread is None else spread + moved
    spread = spread.astype(jnp.bfloat16)
    for s in range(SOURCES):
        out_ref[s] = spread


def send_full_kernel(turn, t_ref, cd_ref, occ_ref, out_ref, choose):
    irreps, ranks = places(cd_ref)
    fill_chooser(choose, ranks, turn)
    _, row_irrep = my_pairs(occ_ref)
    packed = pack(t_ref[...], row_irrep, column_irreps(irreps), choose)
    for s in range(SOURCES):
        out_ref[s, :PAIRS, :] = packed
        out_ref[s, PAIRS:, :] = jnp.zeros((FULL - PAIRS, WIDE * TW), jnp.bfloat16)


def pack_rows_kernel(turn, first, v_ref, ab_ref, cd_ref, out_ref, tiles_ref, choose):
    irreps, ranks = places(cd_ref)
    fill_chooser(choose, ranks, turn)
    row = lax.broadcasted_iota(jnp.int32, (4 * TW, 1), 0) // TW
    row_irrep = jnp.zeros((4 * TW, 1), jnp.int32)
    for i in range(4):
        row_irrep = jnp.where(row == i, ab_ref[first + i], row_irrep)
        tiles_ref[i] = ab_ref[first + i]
    out_ref[...] = pack(v_ref[...], row_irrep, column_irreps(irreps), choose)


def list_kernel(cd_ref, occ_ref, counts_ref, rows_ref, ab_ref, theirs_ref, list_ref, chosen_ref, count, need):
    core = lax.axis_index("blk_2")
    irreps, _ = places(cd_ref)
    count_rows(irreps, need)
    start = jnp.int32(KEPT)
    for g in range(IRREPS):
        list_ref[g] = start
        count[g] = start
        start += counts_ref[core * IRREPS + g]
    for k in range(IRREPS, 16):
        list_ref[k] = start
    for k in range(4):
        list_ref[16 + k] = ab_ref[k]
        list_ref[20 + k] = theirs_ref[k]
    tiles, longest, most = jnp.int32(0), jnp.int32(0), jnp.int32(0)
    for g in range(IRREPS):
        tiles = jnp.maximum(tiles, need[g])
    for k in range(32):
        longest = jnp.maximum(longest, rows_ref[k])
    for k in range(2 * IRREPS):
        most = jnp.maximum(most, counts_ref[k])
    chosen = jnp.int32(0)
    for wire in WIRES:
        chosen += jnp.where(most >= wire, 1, 0)
    chosen_ref[0] = chosen
    chosen_ref[1] = jnp.where(jnp.logical_or(tiles > PARTS, longest > ROWS), 1, 0)
    chosen_ref[2] = most
    chosen_ref[3] = 0

    for mine in range(2):

        @pl.when(core == mine)
        def _():
            @pl.loop(0, 8)
            def _(part):
                for chip in range(2):
                    row = (part * 2 + chip) * ROWS
                    last = row + ROWS - 1
                    for m in range(PAIRS):
                        i, j = divmod((chip * 2 + mine) * PAIRS + m, OCC)
                        if m == 0 or j == 0:
                            left = occ_ref[part * 5 + i]
                        irrep = jnp.bitwise_xor(left, occ_ref[j])
                        at = count[irrep]
                        count[irrep] = at + 1
                        list_ref[at] = jnp.minimum(row, last)
                        row += need[irrep]

    @pl.loop(0, (LIST - KEPT - IJ // 2) // 8)
    def _(k):
        for u in range(8):
            list_ref[KEPT + IJ // 2 + k * 8 + u] = 0


def full_list_kernel(occ_ref, starts_ref, list_ref, count):
    core = lax.axis_index("blk_2")
    for g in range(IRREPS):
        count[g] = starts_ref[g]
    for k in range(KEPT):
        list_ref[k] = starts_ref[k]

    @pl.loop(0, OCC)
    def _(i):
        left = occ_ref[i]

        @pl.loop(0, OCC)
        def _(j):
            pair = i * OCC + j
            source = pair // PAIRS

            @pl.when((source & 1) == core)
            def _():
                irrep = jnp.bitwise_xor(left, occ_ref[j])
                at = count[irrep]
                count[irrep] = at + 1
                list_ref[at] = (source >> 1) * FULL + pair - source * PAIRS

    @pl.loop(KEPT + IJ // 2, LIST)
    def _(k):
        list_ref[k] = 0


def times(held, weight):
    return lax.dot_general(held, weight, NT, preferred_element_type=jnp.float32)


def joined_rows(held_ref):
    held = held_ref[...].astype(jnp.float32)
    count = held.shape[0]
    rows = [held] + [pltpu.roll(held, count - part, 0) for part in range(1, PARTS)]
    return jnp.concatenate([r.astype(jnp.bfloat16) for r in rows], axis=1)


def product_kernel(full, round_ref, *refs):
    turns = 2 if full else 1
    held, weights, refs = refs[:turns], refs[turns : 3 * turns], refs[3 * turns :]
    list_ref, out_ref, *products, dense, both = refs
    wire = dense.shape[0]
    cols = wire - 1
    rows = [ref[...] for ref in held] if full else [joined_rows(held[0])]
    for core in range(2):
        total = None
        for turn in range(turns):
            part = times(rows[turn], weights[2 * turn + core][...])
            total = part if total is None else total + part
        for q in range(2):
            products[2 * core + q][...] = total[:, q * 128 : (q + 1) * 128]
    lower = lax.broadcasted_iota(jnp.int32, (1, 128), 1) < TW
    skip = round_ref[0] * cols
    for q in range(4):
        product = products[q]
        dense[...] = jnp.zeros_like(dense)
        irreps = [list_ref[16 + 2 * q + i] for i in range(2)]
        starts = [jnp.minimum(list_ref[g] + skip, KEPT + IJ // 2) for g in irreps]
        counts = [list_ref[g + 1] - list_ref[g] - skip for g in irreps]
        most = jnp.clip(jnp.maximum(counts[0], counts[1]), 0, cols)

        @pl.loop(0, (most + 7) // 8)
        def _(block):
            base = block * 8
            for u in range(8):
                at = [list_ref[start + base + u] for start in starts]
                picked = [product[pl.ds(a, 1), :] for a in at]
                dense[pl.ds(base + u, 1), :] = jnp.where(lower, picked[0], picked[1])

        both[q * 128 : (q + 1) * 128, :] = dense[...].T
    largest = jnp.max(jnp.max(jnp.abs(both[...]), axis=1, keepdims=True), axis=0, keepdims=True)
    power = 14.0 - jnp.floor(jnp.log2(jnp.maximum(largest, 1e-30)))
    lane = lax.broadcasted_iota(jnp.int32, (4 * TW, wire), 1)
    for core in range(2):
        scaled = both[core * 4 * TW : (core + 1) * 4 * TW, :] * jnp.exp2(power)
        sent = jnp.where(lane == cols, power, scaled).reshape(32, 8, wire)
        out_ref[:, core * 8 : (core + 1) * 8, :] = sent


def sum_kernel(got_ref, mine_ref, partner_ref):
    cols = got_ref.shape[2] - 1
    total = None
    for s in range(32):
        got = got_ref[s]
        got = got * jnp.exp2(-got[:, cols:])
        total = got if total is None else total + got
    mine_ref[...] = total[:8]
    partner_ref[...] = total[8:]


def places_kernel(cols, round_ref, list_ref, pairs_ref, *place_refs):
    core = lax.axis_index("blk_2")
    irrep = list_ref[16 + lax.axis_index("panel") // 8]
    pairs = pairs_ref[...]
    hits = [pairs == irrep + core * IRREPS, pairs == irrep + (1 - core) * IRREPS]
    count = jnp.where(hits[0], 1, jnp.where(hits[1], 1 << 16, 0))
    row = lax.broadcasted_iota(jnp.int32, pairs.shape, 0)
    lane = lax.broadcasted_iota(jnp.int32, pairs.shape, 1)
    for step in (1, 2, 4, 8, 16, 32, 64):
        count += jnp.where(lane >= step, pltpu.roll(count, step, 1), 0)
    whole = jnp.broadcast_to(count[:, 127:], pairs.shape)
    above = whole
    for step in (1, 2, 4, 8):
        above += jnp.where(row >= step, pltpu.roll(above, step, 0), 0)
    count += above - whole
    skip = round_ref[0] * cols + 1
    for hit, found, place_ref in zip(hits, (count & 0xFFFF, count >> 16), place_refs):
        place = jnp.where(hit, found - skip, -1)
        place_ref[...] = jnp.where(place < cols, place, -1)


def finish_kernel(mine_ref, partner_ref, mine_place_ref, partner_place_ref, out_ref):
    wire = mine_ref.shape[1]
    sources = [mine_ref[...], partner_ref[...]]
    for block in range(13):
        spread = jnp.zeros((8, 128), jnp.float32)
        for place_ref, source in zip((mine_place_ref, partner_place_ref), sources):
            at = jnp.broadcast_to(place_ref[block : block + 1, :], (8, 128))
            for k in range(wire // 128):
                moved = jnp.take_along_axis(source[:, k * 128 : (k + 1) * 128], at & 127, axis=1)
                spread = jnp.where(at >> 7 == k, moved, spread)
        held = min(128, IJ - block * 128)
        out_ref[:, block * 128 : block * 128 + held] = spread[:, :held]


def shaped(shape, dtype):
    return jax.ShapeDtypeStruct(shape, dtype)


def body(integrals, amplitudes, ab_irrep, cd_irrep, occ_irrep):
    bf16, f32, i32 = jnp.bfloat16, jnp.float32, jnp.int32
    width = WIDE * TW
    chooser = pltpu.VMEM((16 * TW, width), bf16)
    numbers = pltpu.SMEM((IRREPS,), i32)

    def over_chips(sent):
        got = lax.all_to_all(sent, CHIPS, split_axis=0, concat_axis=0, tiled=True)
        return got.reshape(sent.shape[0] * sent.shape[1], sent.shape[2])

    def swapped(array):
        return lax.ppermute(array, "blk_2", [(0, 1), (1, 0)])

    def gathered_full(turn):
        sent = pl.pallas_call(
            functools.partial(send_full_kernel, turn),
            out_shape=shaped((SOURCES, FULL, width), bf16),
            in_specs=[VMEM, SMEM, SMEM],
            out_specs=VMEM,
            scratch_shapes=[chooser],
            compiler_params=GRANT,
        )(amplitudes, cd_irrep, occ_irrep)
        return over_chips(sent)

    def weights(turn, first, irreps):
        mine, tiles = pl.pallas_call(
            functools.partial(pack_rows_kernel, turn, first),
            out_shape=[shaped((4 * TW, width), bf16), shaped((4,), i32)],
            in_specs=[VMEM, SMEM, SMEM],
            out_specs=[VMEM, SMEM],
            scratch_shapes=[chooser],
            compiler_params=GRANT,
        )(integrals, irreps, cd_irrep)
        return [mine, swapped(mine)], tiles

    sent = pl.pallas_call(
        send_kernel,
        out_shape=shaped((SOURCES, ROWS, NARROW * TW), bf16),
        in_specs=[VMEM, SMEM, SMEM],
        out_specs=VMEM,
        scratch_shapes=[chooser, numbers],
        compiler_params=GRANT,
        name="send",
    )(amplitudes, cd_irrep, occ_irrep)
    held = over_chips(sent)

    number = np.arange(16 * 128, dtype=np.int32).reshape(16, 128)
    real, source = number < IJ, number // PAIRS

    def orbital_irrep(which):
        orbital = lax.broadcasted_iota(i32, (OCC, 16, 128), 0)
        hit = orbital == jnp.asarray(which)[None]
        return jnp.sum(jnp.where(hit, occ_irrep[:, None, None], 0), axis=0)

    irrep = jnp.bitwise_xor(orbital_irrep(number // OCC), orbital_irrep(number % OCC))
    kinds = jnp.asarray(np.where(real, source % 2 * IRREPS, 4 * IRREPS), dtype=i32)
    pairs = irrep + kinds
    numbered = np.arange(2 * IRREPS, dtype=np.int32)
    counts = jnp.sum((pairs == numbered[:, None, None]).astype(i32), axis=(1, 2))
    tiles = jnp.sum((cd_irrep == numbered[:IRREPS, None]).astype(i32), axis=1)
    need = (tiles + NARROW - 1) // NARROW
    alike = irrep == numbered[:IRREPS, None, None]
    taken = jnp.sum(jnp.where(alike, need[:, None, None], 0), axis=0)
    theirs = jnp.asarray(source)[None] == lax.broadcasted_iota(i32, (32, 16, 128), 0)
    rows = jnp.sum(jnp.where(theirs, taken, 0), axis=(1, 2))

    first_weights, my_irrep = weights(0, 0, ab_irrep)
    their_irrep = swapped(my_irrep)

    pair_list, choices = pl.pallas_call(
        list_kernel,
        out_shape=[shaped((LIST,), i32), shaped((4,), i32)],
        in_specs=[SMEM] * 6,
        out_specs=[SMEM] * 2,
        scratch_shapes=[numbers] * 2,
        compiler_params=GRANT,
        name="list",
    )(cd_irrep, occ_irrep, counts, rows, ab_irrep, their_irrep)
    chosen, general, most = choices[0], choices[1] > 0, choices[2]

    def products(full, wire, which, operands, rows_list):
        rows = SOURCES * (FULL if full else ROWS)
        return pl.pallas_call(
            functools.partial(product_kernel, full),
            out_shape=pltpu.VMEM((32, 16, wire), f32),
            in_specs=[SMEM] + [VMEM] * len(operands) + [SMEM],
            out_specs=VMEM,
            scratch_shapes=[pltpu.VMEM((rows, 128), f32)] * 4
            + [pltpu.VMEM((wire, 128), f32), pltpu.VMEM((8 * TW, wire), f32)],
            compiler_params=LARGE,
        )(which, *operands, rows_list)

    def full_products(wire, which):
        rows_list = pl.pallas_call(
            full_list_kernel,
            out_shape=shaped((LIST,), i32),
            in_specs=[SMEM] * 2,
            out_specs=SMEM,
            scratch_shapes=[numbers],
            compiler_params=GRANT,
            name="full_list",
        )(occ_irrep, pair_list)
        operands = [gathered_full(0), gathered_full(1), *first_weights, *weights(1, 16, pair_list)[0]]
        return products(True, wire, which, operands, rows_list)

    def reduced(wire, which):
        partial = lax.cond(
            general,
            lambda: full_products(wire, which),
            lambda: products(False, wire, which, [held, *first_weights], pair_list),
        ).astype(jnp.float16)
        arrived = lax.all_to_all(partial, "panel", split_axis=0, concat_axis=0, tiled=True)
        mine, partners = pl.pallas_call(
            sum_kernel,
            out_shape=[shaped((8, wire), f32)] * 2,
            in_specs=[VMEM],
            out_specs=[VMEM] * 2,
            compiler_params=GRANT,
            name="sum",
        )(arrived.astype(f32))
        spots = pl.pallas_call(
            functools.partial(places_kernel, wire - 1),
            out_shape=[shaped((16, 128), i32)] * 2,
            in_specs=[SMEM, SMEM, VMEM],
            out_specs=[VMEM] * 2,
            compiler_params=GRANT,
            name="places",
        )(which, pair_list, pairs)
        theirs = swapped(partners)
        return pl.pallas_call(
            finish_kernel,
            out_shape=shaped((8, IJ), f32),
            in_specs=[VMEM] * 4,
            out_specs=VMEM,
            compiler_params=GRANT,
            name="finish",
        )(mine, theirs, *spots)

    zero = jnp.zeros((1,), i32)

    def all_rounds():
        cols = LONG - 1

        def add_round(number, total):
            which = jnp.full((1,), number, i32)
            return total + reduced(LONG, which)

        return lax.fori_loop(0, (most + cols - 1) // cols, add_round, jnp.zeros((8, IJ), f32))

    branches = [functools.partial(reduced, wire, zero) for wire in WIRES]
    return lax.switch(chosen, [*branches, all_rounds])


def solution(mesh):
    split = Mesh(
        mesh.devices.reshape(2, 8, 2, mesh.shape["panel"]), ("blk_0", "blk_1", "blk_2", "panel")
    )
    return jax.shard_map(
        body,
        mesh=split,
        in_specs=(P(BLK, "panel"), P(BLK, "panel"), P(BLK), P("panel"), P()),
        out_specs=P(BLK_PANEL, None),
        check_vma=False,
    )
```

```python
import functools

import jax
import jax.numpy as jnp
import numpy as np
from jax import lax
from jax.experimental import pallas as pl
from jax.experimental.pallas import tpu as pltpu
from jax.sharding import Mesh
from jax.sharding import PartitionSpec as P


TW = 64
IRREPS = 8
OCC = 40
IJ = 1600
BLK = ("blk_0", "blk_1", "blk_2")
BLK_PANEL = ("blk_0", "blk_1", "blk_2", "panel")
CHIPS = ("blk_0", "blk_1")

PAIRS = 50
SOURCES = 16
WIDE = 8
NARROW = 2
PARTS = WIDE // NARROW
ROWS = 144
FULL = 56
WIRES = (256, 384)
LONG = 512
KEPT = 24
LIST = KEPT + 1384

SMEM = pl.BlockSpec(memory_space=pltpu.SMEM)
VMEM = pl.BlockSpec(memory_space=pltpu.VMEM)
NT = (((1,), (1,)), ((), ()))
GRANT = pltpu.CompilerParams(vmem_limit_bytes=24 << 20)
LARGE = pltpu.CompilerParams(vmem_limit_bytes=40 << 20)


def places(cd_ref):
    irreps = [cd_ref[t] for t in range(16)]
    ranks = []
    for t in range(16):
        rank = jnp.int32(0)
        for earlier in range(t):
            rank += jnp.where(irreps[earlier] == irreps[t], 1, 0)
        ranks.append(rank)
    return irreps, ranks


def fill_chooser(choose, ranks, turn):
    width = WIDE * TW
    row = lax.broadcasted_iota(jnp.int32, (TW, width), 0)
    col = lax.broadcasted_iota(jnp.int32, (TW, width), 1)
    place = jnp.where(col % TW == row, col // TW + turn * WIDE, -1)
    for t in range(16):
        hit = jnp.where(place == ranks[t], 1.0, 0.0)
        choose[t * TW : (t + 1) * TW, :] = hit.astype(jnp.bfloat16)


def column_irreps(irreps):
    lane = lax.broadcasted_iota(jnp.int32, (1, 16 * TW), 1) // TW
    found = jnp.zeros((1, 16 * TW), jnp.int32)
    for t in range(16):
        found = jnp.where(lane == t, irreps[t], found)
    return found


def pack(values, row_irrep, col_irrep, choose):
    kept = jnp.where(row_irrep == col_irrep, values.astype(jnp.float32), 0.0)
    return jnp.dot(
        kept.astype(jnp.bfloat16), choose[...], preferred_element_type=jnp.float32
    ).astype(jnp.bfloat16)


def my_pairs(occ_ref):
    blk = lax.axis_index("blk_0") * 16 + lax.axis_index("blk_1") * 2 + lax.axis_index("blk_2")
    upper = blk * 5 // 4
    at = blk % 4 * 10
    left = [occ_ref[upper], occ_ref[jnp.minimum(upper + 1, OCC - 1)]]
    row = lax.broadcasted_iota(jnp.int32, (PAIRS, 1), 0)
    column = jnp.zeros((PAIRS, 1), jnp.int32)
    irreps = []
    for m in range(PAIRS):
        later = at + m >= OCC
        right = occ_ref[at + m - jnp.where(later, OCC, 0)]
        irreps.append(jnp.bitwise_xor(jnp.where(later, left[1], left[0]), right))
        column = jnp.where(row == m, irreps[m], column)
    return irreps, column


def count_rows(irreps, need):
    for g in range(IRREPS):
        tiles = jnp.int32(0)
        for irrep in irreps:
            tiles += jnp.where(irrep == g, 1, 0)
        need[g] = (tiles + NARROW - 1) // NARROW


def send_kernel(t_ref, cd_ref, occ_ref, out_ref, choose, need):
    irreps, ranks = places(cd_ref)
    fill_chooser(choose, ranks, 0)
    count_rows(irreps, need)
    pairs, row_irrep = my_pairs(occ_ref)
    packed = pack(t_ref[...], row_irrep, column_irreps(irreps), choose)
    lane = lax.broadcasted_iota(jnp.int32, (1, PAIRS), 1)
    first = jnp.zeros((1, PAIRS), jnp.int32)
    count = jnp.zeros((1, PAIRS), jnp.int32)
    row = jnp.int32(0)
    for m in range(PAIRS):
        rows = need[pairs[m]]
        first = jnp.where(lane == m, row, first)
        count = jnp.where(lane == m, rows, count)
        row += rows
    place = lax.broadcasted_iota(jnp.int32, (ROWS, PAIRS), 0)
    width = NARROW * TW
    spread = None
    for part in range(PARTS):
        at = jnp.where(count > part, first + part, -1)
        move = jnp.where(place == at, 1.0, 0.0).astype(jnp.bfloat16)
        moved = jnp.dot(
            move, packed[:, part * width : (part + 1) * width], preferred_element_type=jnp.float32
        )
        spread = moved if spread is None else spread + moved
    spread = spread.astype(jnp.bfloat16)
    for s in range(SOURCES):
        out_ref[s] = spread


def send_full_kernel(turn, t_ref, cd_ref, occ_ref, out_ref, choose):
    irreps, ranks = places(cd_ref)
    fill_chooser(choose, ranks, turn)
    _, row_irrep = my_pairs(occ_ref)
    packed = pack(t_ref[...], row_irrep, column_irreps(irreps), choose)
    for s in range(SOURCES):
        out_ref[s, :PAIRS, :] = packed
        out_ref[s, PAIRS:, :] = jnp.zeros((FULL - PAIRS, WIDE * TW), jnp.bfloat16)


def pack_rows_kernel(turn, first, v_ref, ab_ref, cd_ref, out_ref, choose):
    irreps, ranks = places(cd_ref)
    fill_chooser(choose, ranks, turn)
    row = lax.broadcasted_iota(jnp.int32, (4 * TW, 1), 0) // TW
    row_irrep = jnp.zeros((4 * TW, 1), jnp.int32)
    for i in range(4):
        row_irrep = jnp.where(row == i, ab_ref[first + i], row_irrep)
    lane = lax.broadcasted_iota(jnp.int32, (8, WIDE * TW), 1) // 128
    told = jnp.zeros((8, WIDE * TW), jnp.int32)
    for i in range(4):
        told = jnp.where(lane == i, ab_ref[first + i], told)
    out_ref[4 * TW :, :] = told.astype(jnp.float32).astype(jnp.bfloat16)
    out_ref[: 4 * TW, :] = pack(v_ref[...], row_irrep, column_irreps(irreps), choose)


def list_kernel(cd_ref, occ_ref, counts_ref, rows_ref, ab_ref, list_ref, chosen_ref, count, need):
    core = lax.axis_index("blk_2")
    irreps, _ = places(cd_ref)
    count_rows(irreps, need)
    start = jnp.int32(KEPT)
    for g in range(IRREPS):
        list_ref[g] = start
        count[g] = start
        start += counts_ref[core * IRREPS + g]
    for k in range(IRREPS, 16):
        list_ref[k] = start
    for k in range(4):
        list_ref[16 + k] = ab_ref[k]
        list_ref[20 + k] = 0
    tiles, longest, most = jnp.int32(0), jnp.int32(0), jnp.int32(0)
    for g in range(IRREPS):
        tiles = jnp.maximum(tiles, need[g])
    for k in range(32):
        longest = jnp.maximum(longest, rows_ref[k])
    for k in range(2 * IRREPS):
        most = jnp.maximum(most, counts_ref[k])
    chosen = jnp.int32(0)
    for wire in WIRES:
        chosen += jnp.where(most >= wire, 1, 0)
    chosen_ref[0] = chosen
    chosen_ref[1] = jnp.where(jnp.logical_or(tiles > PARTS, longest > ROWS), 1, 0)
    chosen_ref[2] = most
    chosen_ref[3] = 0

    for mine in range(2):

        @pl.when(core == mine)
        def _():
            @pl.loop(0, 8)
            def _(part):
                for chip in range(2):
                    row = (part * 2 + chip) * ROWS
                    last = row + ROWS - 1
                    for m in range(PAIRS):
                        i, j = divmod((chip * 2 + mine) * PAIRS + m, OCC)
                        if m == 0 or j == 0:
                            left = occ_ref[part * 5 + i]
                        irrep = jnp.bitwise_xor(left, occ_ref[j])
                        at = count[irrep]
                        count[irrep] = at + 1
                        list_ref[at] = jnp.minimum(row, last)
                        row += need[irrep]

    @pl.loop(0, (LIST - KEPT - IJ // 2) // 8)
    def _(k):
        for u in range(8):
            list_ref[KEPT + IJ // 2 + k * 8 + u] = 0


def full_list_kernel(occ_ref, starts_ref, list_ref, count):
    core = lax.axis_index("blk_2")
    for g in range(IRREPS):
        count[g] = starts_ref[g]
    for k in range(KEPT):
        list_ref[k] = starts_ref[k]

    @pl.loop(0, OCC)
    def _(i):
        left = occ_ref[i]

        @pl.loop(0, OCC)
        def _(j):
            pair = i * OCC + j
            source = pair // PAIRS

            @pl.when((source & 1) == core)
            def _():
                irrep = jnp.bitwise_xor(left, occ_ref[j])
                at = count[irrep]
                count[irrep] = at + 1
                list_ref[at] = (source >> 1) * FULL + pair - source * PAIRS

    @pl.loop(KEPT + IJ // 2, LIST)
    def _(k):
        list_ref[k] = 0


def times(held, weight):
    return lax.dot_general(held, weight, NT, preferred_element_type=jnp.float32)


def joined_rows(held_ref):
    held = held_ref[...].astype(jnp.float32)
    count = held.shape[0]
    rows = [held] + [pltpu.roll(held, count - part, 0) for part in range(1, PARTS)]
    return jnp.concatenate([r.astype(jnp.bfloat16) for r in rows], axis=1)


def product_kernel(full, round_ref, *refs):
    turns = 2 if full else 1
    held, weights, refs = refs[:turns], refs[turns : 3 * turns], refs[3 * turns :]
    list_ref, out_ref, *products, dense, both = refs
    wire = dense.shape[0]
    cols = wire - 1
    rows = [ref[...] for ref in held] if full else [joined_rows(held[0])]
    for core in range(2):
        total = None
        for turn in range(turns):
            part = times(rows[turn], weights[2 * turn + core][: 4 * TW, :])
            total = part if total is None else total + part
        for q in range(2):
            products[2 * core + q][...] = total[:, q * 128 : (q + 1) * 128]
    lower = lax.broadcasted_iota(jnp.int32, (1, 128), 1) < TW
    skip = round_ref[0] * cols
    told = weights[1][4 * TW :, :].astype(jnp.float32)
    tile_irreps = [list_ref[16 + i] for i in range(4)]
    tile_irreps += [jnp.max(told[:, i * 128 : (i + 1) * 128]).astype(jnp.int32) for i in range(4)]
    for q in range(4):
        product = products[q]
        dense[...] = jnp.zeros_like(dense)
        irreps = tile_irreps[2 * q : 2 * q + 2]
        starts = [jnp.minimum(list_ref[g] + skip, KEPT + IJ // 2) for g in irreps]
        counts = [list_ref[g + 1] - list_ref[g] - skip for g in irreps]
        most = jnp.clip(jnp.maximum(counts[0], counts[1]), 0, cols)

        @pl.loop(0, (most + 7) // 8)
        def _(block):
            base = block * 8
            for u in range(8):
                at = [list_ref[start + base + u] for start in starts]
                picked = [product[pl.ds(a, 1), :] for a in at]
                dense[pl.ds(base + u, 1), :] = jnp.where(lower, picked[0], picked[1])

        both[q * 128 : (q + 1) * 128, :] = dense[...].T
    largest = jnp.max(jnp.max(jnp.abs(both[...]), axis=1, keepdims=True), axis=0, keepdims=True)
    power = 14.0 - jnp.floor(jnp.log2(jnp.maximum(largest, 1e-30)))
    lane = lax.broadcasted_iota(jnp.int32, (4 * TW, wire), 1)
    for core in range(2):
        scaled = both[core * 4 * TW : (core + 1) * 4 * TW, :] * jnp.exp2(power)
        sent = jnp.where(lane == cols, power, scaled).reshape(32, 8, wire)
        out_ref[:, core * 8 : (core + 1) * 8, :] = sent


def sum_kernel(got_ref, mine_ref, partner_ref):
    cols = got_ref.shape[2] - 1
    total = None
    for s in range(32):
        got = got_ref[s]
        got = got * jnp.exp2(-got[:, cols:])
        total = got if total is None else total + got
    mine_ref[...] = total[:8]
    partner_ref[...] = total[8:]


def places_kernel(cols, round_ref, list_ref, pairs_ref, *place_refs):
    core = lax.axis_index("blk_2")
    irrep = list_ref[16 + lax.axis_index("panel") // 8]
    pairs = pairs_ref[...]
    hits = [pairs == irrep + core * IRREPS, pairs == irrep + (1 - core) * IRREPS]
    count = jnp.where(hits[0], 1, jnp.where(hits[1], 1 << 16, 0))
    row = lax.broadcasted_iota(jnp.int32, pairs.shape, 0)
    lane = lax.broadcasted_iota(jnp.int32, pairs.shape, 1)
    for step in (1, 2, 4, 8, 16, 32, 64):
        count += jnp.where(lane >= step, pltpu.roll(count, step, 1), 0)
    whole = jnp.broadcast_to(count[:, 127:], pairs.shape)
    above = whole
    for step in (1, 2, 4, 8):
        above += jnp.where(row >= step, pltpu.roll(above, step, 0), 0)
    count += above - whole
    skip = round_ref[0] * cols + 1
    for hit, found, place_ref in zip(hits, (count & 0xFFFF, count >> 16), place_refs):
        place = jnp.where(hit, found - skip, -1)
        place_ref[...] = jnp.where(place < cols, place, -1)


def finish_kernel(mine_ref, partner_ref, mine_place_ref, partner_place_ref, out_ref):
    wire = mine_ref.shape[1]
    sources = [mine_ref[...], partner_ref[...]]
    for block in range(13):
        spread = jnp.zeros((8, 128), jnp.float32)
        for place_ref, source in zip((mine_place_ref, partner_place_ref), sources):
            at = jnp.broadcast_to(place_ref[block : block + 1, :], (8, 128))
            for k in range(wire // 128):
                moved = jnp.take_along_axis(source[:, k * 128 : (k + 1) * 128], at & 127, axis=1)
                spread = jnp.where(at >> 7 == k, moved, spread)
        held = min(128, IJ - block * 128)
        out_ref[:, block * 128 : block * 128 + held] = spread[:, :held]


def shaped(shape, dtype):
    return jax.ShapeDtypeStruct(shape, dtype)


def body(integrals, amplitudes, ab_irrep, cd_irrep, occ_irrep):
    bf16, f32, i32 = jnp.bfloat16, jnp.float32, jnp.int32
    width = WIDE * TW
    chooser = pltpu.VMEM((16 * TW, width), bf16)
    numbers = pltpu.SMEM((IRREPS,), i32)

    def over_chips(sent):
        got = lax.all_to_all(sent, CHIPS, split_axis=0, concat_axis=0, tiled=True)
        return got.reshape(sent.shape[0] * sent.shape[1], sent.shape[2])

    def swapped(array):
        return lax.ppermute(array, "blk_2", [(0, 1), (1, 0)])

    def gathered_full(turn):
        sent = pl.pallas_call(
            functools.partial(send_full_kernel, turn),
            out_shape=shaped((SOURCES, FULL, width), bf16),
            in_specs=[VMEM, SMEM, SMEM],
            out_specs=VMEM,
            scratch_shapes=[chooser],
            compiler_params=GRANT,
        )(amplitudes, cd_irrep, occ_irrep)
        return over_chips(sent)

    def weights(turn, first, irreps):
        mine = pl.pallas_call(
            functools.partial(pack_rows_kernel, turn, first),
            out_shape=shaped((4 * TW + 8, width), bf16),
            in_specs=[VMEM, SMEM, SMEM],
            out_specs=VMEM,
            scratch_shapes=[chooser],
            compiler_params=GRANT,
        )(integrals, irreps, cd_irrep)
        return [mine, swapped(mine)]

    sent = pl.pallas_call(
        send_kernel,
        out_shape=shaped((SOURCES, ROWS, NARROW * TW), bf16),
        in_specs=[VMEM, SMEM, SMEM],
        out_specs=VMEM,
        scratch_shapes=[chooser, numbers],
        compiler_params=GRANT,
        name="send",
    )(amplitudes, cd_irrep, occ_irrep)
    held = over_chips(sent)

    number = np.arange(16 * 128, dtype=np.int32).reshape(16, 128)
    real, source = number < IJ, number // PAIRS

    def orbital_irrep(which):
        orbital = lax.broadcasted_iota(i32, (OCC, 16, 128), 0)
        hit = orbital == jnp.asarray(which)[None]
        return jnp.sum(jnp.where(hit, occ_irrep[:, None, None], 0), axis=0)

    irrep = jnp.bitwise_xor(orbital_irrep(number // OCC), orbital_irrep(number % OCC))
    kinds = jnp.asarray(np.where(real, source % 2 * IRREPS, 4 * IRREPS), dtype=i32)
    pairs = irrep + kinds
    numbered = np.arange(2 * IRREPS, dtype=np.int32)
    counts = jnp.sum((pairs == numbered[:, None, None]).astype(i32), axis=(1, 2))
    tiles = jnp.sum((cd_irrep == numbered[:IRREPS, None]).astype(i32), axis=1)
    need = (tiles + NARROW - 1) // NARROW
    alike = irrep == numbered[:IRREPS, None, None]
    taken = jnp.sum(jnp.where(alike, need[:, None, None], 0), axis=0)
    theirs = jnp.asarray(source)[None] == lax.broadcasted_iota(i32, (32, 16, 128), 0)
    rows = jnp.sum(jnp.where(theirs, taken, 0), axis=(1, 2))

    first_weights = weights(0, 0, ab_irrep)

    pair_list, choices = pl.pallas_call(
        list_kernel,
        out_shape=[shaped((LIST,), i32), shaped((4,), i32)],
        in_specs=[SMEM] * 5,
        out_specs=[SMEM] * 2,
        scratch_shapes=[numbers] * 2,
        compiler_params=GRANT,
        name="list",
    )(cd_irrep, occ_irrep, counts, rows, ab_irrep)
    chosen, general, most = choices[0], choices[1] > 0, choices[2]

    def products(full, wire, which, operands, rows_list):
        rows = SOURCES * (FULL if full else ROWS)
        return pl.pallas_call(
            functools.partial(product_kernel, full),
            out_shape=pltpu.VMEM((32, 16, wire), f32),
            in_specs=[SMEM] + [VMEM] * len(operands) + [SMEM],
            out_specs=VMEM,
            scratch_shapes=[pltpu.VMEM((rows, 128), f32)] * 4
            + [pltpu.VMEM((wire, 128), f32), pltpu.VMEM((8 * TW, wire), f32)],
            compiler_params=LARGE,
        )(which, *operands, rows_list)

    def full_products(wire, which):
        rows_list = pl.pallas_call(
            full_list_kernel,
            out_shape=shaped((LIST,), i32),
            in_specs=[SMEM] * 2,
            out_specs=SMEM,
            scratch_shapes=[numbers],
            compiler_params=GRANT,
            name="full_list",
        )(occ_irrep, pair_list)
        operands = [gathered_full(0), gathered_full(1), *first_weights, *weights(1, 16, pair_list)]
        return products(True, wire, which, operands, rows_list)

    def reduced(wire, which):
        partial = lax.cond(
            general,
            lambda: full_products(wire, which),
            lambda: products(False, wire, which, [held, *first_weights], pair_list),
        ).astype(jnp.float16)
        arrived = lax.all_to_all(partial, "panel", split_axis=0, concat_axis=0, tiled=True)
        mine, partners = pl.pallas_call(
            sum_kernel,
            out_shape=[shaped((8, wire), f32)] * 2,
            in_specs=[VMEM],
            out_specs=[VMEM] * 2,
            compiler_params=GRANT,
            name="sum",
        )(arrived.astype(f32))
        spots = pl.pallas_call(
            functools.partial(places_kernel, wire - 1),
            out_shape=[shaped((16, 128), i32)] * 2,
            in_specs=[SMEM, SMEM, VMEM],
            out_specs=[VMEM] * 2,
            compiler_params=GRANT,
            name="places",
        )(which, pair_list, pairs)
        theirs = swapped(partners)
        return pl.pallas_call(
            finish_kernel,
            out_shape=shaped((8, IJ), f32),
            in_specs=[VMEM] * 4,
            out_specs=VMEM,
            compiler_params=GRANT,
            name="finish",
        )(mine, theirs, *spots)

    zero = jnp.zeros((1,), i32)

    def all_rounds():
        cols = LONG - 1

        def add_round(number, total):
            which = jnp.full((1,), number, i32)
            return total + reduced(LONG, which)

        return lax.fori_loop(0, (most + cols - 1) // cols, add_round, jnp.zeros((8, IJ), f32))

    branches = [functools.partial(reduced, wire, zero) for wire in WIRES]
    return lax.switch(chosen, [*branches, all_rounds])


def solution(mesh):
    split = Mesh(
        mesh.devices.reshape(2, 8, 2, mesh.shape["panel"]), ("blk_0", "blk_1", "blk_2", "panel")
    )
    return jax.shard_map(
        body,
        mesh=split,
        in_specs=(P(BLK, "panel"), P(BLK, "panel"), P(BLK), P("panel"), P()),
        out_specs=P(BLK_PANEL, None),
        check_vma=False,
    )
```

```python
import functools

import jax
import jax.numpy as jnp
import numpy as np
from jax import lax
from jax.experimental import pallas as pl
from jax.experimental.pallas import tpu as pltpu
from jax.sharding import Mesh
from jax.sharding import PartitionSpec as P


TW = 64
IRREPS = 8
OCC = 40
IJ = 1600
BLK = ("blk_0", "blk_1", "blk_2")
BLK_PANEL = ("blk_0", "blk_1", "blk_2", "panel")
CHIPS = ("blk_0", "blk_1")

PAIRS = 50
SOURCES = 16
WIDE = 8
NARROW = 2
PARTS = WIDE // NARROW
ROWS = 144
FULL = 56
WIRES = (256, 384)
LONG = 512
KEPT = 24
LIST = KEPT + 1384

SMEM = pl.BlockSpec(memory_space=pltpu.SMEM)
VMEM = pl.BlockSpec(memory_space=pltpu.VMEM)
NT = (((1,), (1,)), ((), ()))
GRANT = pltpu.CompilerParams(vmem_limit_bytes=24 << 20)
LARGE = pltpu.CompilerParams(vmem_limit_bytes=40 << 20)


def places(cd_ref):
    irreps = [cd_ref[t] for t in range(16)]
    ranks = []
    for t in range(16):
        rank = jnp.int32(0)
        for earlier in range(t):
            rank += jnp.where(irreps[earlier] == irreps[t], 1, 0)
        ranks.append(rank)
    return irreps, ranks


def fill_chooser(choose, ranks, turn):
    width = WIDE * TW
    row = lax.broadcasted_iota(jnp.int32, (TW, width), 0)
    col = lax.broadcasted_iota(jnp.int32, (TW, width), 1)
    place = jnp.where(col % TW == row, col // TW + turn * WIDE, -1)
    for t in range(16):
        hit = jnp.where(place == ranks[t], 1.0, 0.0)
        choose[t * TW : (t + 1) * TW, :] = hit.astype(jnp.bfloat16)


def column_irreps(irreps):
    lane = lax.broadcasted_iota(jnp.int32, (1, 16 * TW), 1) // TW
    found = jnp.zeros((1, 16 * TW), jnp.int32)
    for t in range(16):
        found = jnp.where(lane == t, irreps[t], found)
    return found


def pack(values, row_irrep, col_irrep, choose):
    kept = jnp.where(row_irrep == col_irrep, values.astype(jnp.float32), 0.0)
    return jnp.dot(
        kept.astype(jnp.bfloat16), choose[...], preferred_element_type=jnp.float32
    ).astype(jnp.bfloat16)


def my_pairs(occ_ref):
    blk = lax.axis_index("blk_0") * 16 + lax.axis_index("blk_1") * 2 + lax.axis_index("blk_2")
    upper = blk * 5 // 4
    at = blk % 4 * 10
    left = [occ_ref[upper], occ_ref[jnp.minimum(upper + 1, OCC - 1)]]
    row = lax.broadcasted_iota(jnp.int32, (PAIRS, 1), 0)
    column = jnp.zeros((PAIRS, 1), jnp.int32)
    irreps = []
    for m in range(PAIRS):
        later = at + m >= OCC
        right = occ_ref[at + m - jnp.where(later, OCC, 0)]
        irreps.append(jnp.bitwise_xor(jnp.where(later, left[1], left[0]), right))
        column = jnp.where(row == m, irreps[m], column)
    return irreps, column


def count_rows(irreps, need):
    for g in range(IRREPS):
        tiles = jnp.int32(0)
        for irrep in irreps:
            tiles += jnp.where(irrep == g, 1, 0)
        need[g] = (tiles + NARROW - 1) // NARROW


def send_kernel(t_ref, cd_ref, occ_ref, out_ref, choose, need):
    irreps, ranks = places(cd_ref)
    fill_chooser(choose, ranks, 0)
    count_rows(irreps, need)
    pairs, row_irrep = my_pairs(occ_ref)
    packed = pack(t_ref[...], row_irrep, column_irreps(irreps), choose)
    lane = lax.broadcasted_iota(jnp.int32, (1, PAIRS), 1)
    first = jnp.zeros((1, PAIRS), jnp.int32)
    count = jnp.zeros((1, PAIRS), jnp.int32)
    row = jnp.int32(0)
    for m in range(PAIRS):
        rows = need[pairs[m]]
        first = jnp.where(lane == m, row, first)
        count = jnp.where(lane == m, rows, count)
        row += rows
    place = lax.broadcasted_iota(jnp.int32, (ROWS, PAIRS), 0)
    width = NARROW * TW
    spread = None
    for part in range(PARTS):
        at = jnp.where(count > part, first + part, -1)
        move = jnp.where(place == at, 1.0, 0.0).astype(jnp.bfloat16)
        moved = jnp.dot(
            move, packed[:, part * width : (part + 1) * width], preferred_element_type=jnp.float32
        )
        spread = moved if spread is None else spread + moved
    spread = spread.astype(jnp.bfloat16)
    for s in range(SOURCES):
        out_ref[s] = spread


def send_full_kernel(turn, t_ref, cd_ref, occ_ref, out_ref, choose):
    irreps, ranks = places(cd_ref)
    fill_chooser(choose, ranks, turn)
    _, row_irrep = my_pairs(occ_ref)
    packed = pack(t_ref[...], row_irrep, column_irreps(irreps), choose)
    for s in range(SOURCES):
        out_ref[s, :PAIRS, :] = packed
        out_ref[s, PAIRS:, :] = jnp.zeros((FULL - PAIRS, WIDE * TW), jnp.bfloat16)


def pack_rows_kernel(turn, first, v_ref, ab_ref, cd_ref, out_ref, choose):
    irreps, ranks = places(cd_ref)
    fill_chooser(choose, ranks, turn)
    row = lax.broadcasted_iota(jnp.int32, (4 * TW, 1), 0) // TW
    row_irrep = jnp.zeros((4 * TW, 1), jnp.int32)
    for i in range(4):
        row_irrep = jnp.where(row == i, ab_ref[first + i], row_irrep)
    lane = lax.broadcasted_iota(jnp.int32, (8, WIDE * TW), 1) // 128
    told = jnp.zeros((8, WIDE * TW), jnp.int32)
    for i in range(4):
        told = jnp.where(lane == i, ab_ref[first + i], told)
    out_ref[4 * TW :, :] = told.astype(jnp.float32).astype(jnp.bfloat16)
    out_ref[: 4 * TW, :] = pack(v_ref[...], row_irrep, column_irreps(irreps), choose)


def list_kernel(cd_ref, occ_ref, counts_ref, rows_ref, ab_ref, list_ref, chosen_ref, count, need):
    core = lax.axis_index("blk_2")
    irreps, _ = places(cd_ref)
    count_rows(irreps, need)
    start = jnp.int32(KEPT)
    for g in range(IRREPS):
        list_ref[g] = start
        count[g] = start
        start += counts_ref[core * IRREPS + g]
    for k in range(IRREPS, 16):
        list_ref[k] = start
    for k in range(4):
        list_ref[16 + k] = ab_ref[k]
        list_ref[20 + k] = 0
    tiles, longest, most = jnp.int32(0), jnp.int32(0), jnp.int32(0)
    for g in range(IRREPS):
        tiles = jnp.maximum(tiles, need[g])
    for k in range(32):
        longest = jnp.maximum(longest, rows_ref[k])
    for k in range(2 * IRREPS):
        most = jnp.maximum(most, counts_ref[k])
    chosen = jnp.int32(0)
    for wire in WIRES:
        chosen += jnp.where(most >= wire, 1, 0)
    chosen_ref[0] = chosen
    chosen_ref[1] = jnp.where(jnp.logical_or(tiles > PARTS, longest > ROWS), 1, 0)
    chosen_ref[2] = most
    chosen_ref[3] = 0

    for mine in range(2):

        @pl.when(core == mine)
        def _():
            @pl.loop(0, 8)
            def _(part):
                for chip in range(2):
                    row = (part * 2 + chip) * ROWS
                    last = row + ROWS - 1
                    for m in range(PAIRS):
                        i, j = divmod((chip * 2 + mine) * PAIRS + m, OCC)
                        if m == 0 or j == 0:
                            left = occ_ref[part * 5 + i]
                        irrep = jnp.bitwise_xor(left, occ_ref[j])
                        at = count[irrep]
                        count[irrep] = at + 1
                        list_ref[at] = jnp.minimum(row, last)
                        row += need[irrep]

    @pl.loop(0, (LIST - KEPT - IJ // 2) // 8)
    def _(k):
        for u in range(8):
            list_ref[KEPT + IJ // 2 + k * 8 + u] = 0


def full_list_kernel(occ_ref, starts_ref, list_ref, count):
    core = lax.axis_index("blk_2")
    for g in range(IRREPS):
        count[g] = starts_ref[g]
    for k in range(KEPT):
        list_ref[k] = starts_ref[k]

    @pl.loop(0, OCC)
    def _(i):
        left = occ_ref[i]

        @pl.loop(0, OCC)
        def _(j):
            pair = i * OCC + j
            source = pair // PAIRS

            @pl.when((source & 1) == core)
            def _():
                irrep = jnp.bitwise_xor(left, occ_ref[j])
                at = count[irrep]
                count[irrep] = at + 1
                list_ref[at] = (source >> 1) * FULL + pair - source * PAIRS

    @pl.loop(KEPT + IJ // 2, LIST)
    def _(k):
        list_ref[k] = 0


def times(held, weight):
    return lax.dot_general(held, weight, NT, preferred_element_type=jnp.float32)


def joined_rows(held_ref):
    held = held_ref[...].astype(jnp.float32)
    count = held.shape[0]
    rows = [held] + [pltpu.roll(held, count - part, 0) for part in range(1, PARTS)]
    return jnp.concatenate([r.astype(jnp.bfloat16) for r in rows], axis=1)


def product_kernel(full, round_ref, *refs):
    turns = 2 if full else 1
    held, weights, refs = refs[:turns], refs[turns : 3 * turns], refs[3 * turns :]
    list_ref, out_ref, *products, dense, both = refs
    wire = dense.shape[0]
    cols = wire - 1
    rows = [ref[...] for ref in held] if full else [joined_rows(held[0])]
    for core in range(2):
        total = None
        for turn in range(turns):
            part = times(rows[turn], weights[2 * turn + core][: 4 * TW, :])
            total = part if total is None else total + part
        for q in range(2):
            products[2 * core + q][...] = total[:, q * 128 : (q + 1) * 128]
    lower = lax.broadcasted_iota(jnp.int32, (1, 128), 1) < TW
    skip = round_ref[0] * cols
    told = weights[1][4 * TW :, :].astype(jnp.float32)
    tile_irreps = [list_ref[16 + i] for i in range(4)]
    tile_irreps += [jnp.max(told[:, i * 128 : (i + 1) * 128]).astype(jnp.int32) for i in range(4)]
    for q in range(4):
        product = products[q]
        dense[...] = jnp.zeros_like(dense)
        irreps = tile_irreps[2 * q : 2 * q + 2]
        starts = [jnp.minimum(list_ref[g] + skip, KEPT + IJ // 2) for g in irreps]
        counts = [list_ref[g + 1] - list_ref[g] - skip for g in irreps]
        most = jnp.clip(jnp.maximum(counts[0], counts[1]), 0, cols)

        @pl.loop(0, (most + 15) // 16)
        def _(block):
            base = block * 16
            for u in range(16):
                at = [list_ref[start + base + u] for start in starts]
                picked = [product[pl.ds(a, 1), :] for a in at]
                dense[pl.ds(base + u, 1), :] = jnp.where(lower, picked[0], picked[1])

        both[q * 128 : (q + 1) * 128, :] = dense[...].T
    largest = jnp.max(jnp.max(jnp.abs(both[...]), axis=1, keepdims=True), axis=0, keepdims=True)
    power = 14.0 - jnp.floor(jnp.log2(jnp.maximum(largest, 1e-30)))
    lane = lax.broadcasted_iota(jnp.int32, (4 * TW, wire), 1)
    for core in range(2):
        scaled = both[core * 4 * TW : (core + 1) * 4 * TW, :] * jnp.exp2(power)
        sent = jnp.where(lane == cols, power, scaled).reshape(32, 8, wire)
        out_ref[:, core * 8 : (core + 1) * 8, :] = sent


def sum_kernel(got_ref, mine_ref, partner_ref):
    cols = got_ref.shape[2] - 1
    total = None
    for s in range(32):
        got = got_ref[s]
        got = got * jnp.exp2(-got[:, cols:])
        total = got if total is None else total + got
    mine_ref[...] = total[:8]
    partner_ref[...] = total[8:]


def places_kernel(cols, round_ref, list_ref, pairs_ref, *place_refs):
    core = lax.axis_index("blk_2")
    irrep = list_ref[16 + lax.axis_index("panel") // 8]
    pairs = pairs_ref[...]
    hits = [pairs == irrep + core * IRREPS, pairs == irrep + (1 - core) * IRREPS]
    count = jnp.where(hits[0], 1, jnp.where(hits[1], 1 << 16, 0))
    row = lax.broadcasted_iota(jnp.int32, pairs.shape, 0)
    lane = lax.broadcasted_iota(jnp.int32, pairs.shape, 1)
    for step in (1, 2, 4, 8, 16, 32, 64):
        count += jnp.where(lane >= step, pltpu.roll(count, step, 1), 0)
    whole = jnp.broadcast_to(count[:, 127:], pairs.shape)
    above = whole
    for step in (1, 2, 4, 8):
        above += jnp.where(row >= step, pltpu.roll(above, step, 0), 0)
    count += above - whole
    skip = round_ref[0] * cols + 1
    for hit, found, place_ref in zip(hits, (count & 0xFFFF, count >> 16), place_refs):
        place = jnp.where(hit, found - skip, -1)
        place_ref[...] = jnp.where(place < cols, place, -1)


def finish_kernel(mine_ref, partner_ref, mine_place_ref, partner_place_ref, out_ref):
    wire = mine_ref.shape[1]
    sources = [mine_ref[...], partner_ref[...]]
    for block in range(13):
        spread = jnp.zeros((8, 128), jnp.float32)
        for place_ref, source in zip((mine_place_ref, partner_place_ref), sources):
            at = jnp.broadcast_to(place_ref[block : block + 1, :], (8, 128))
            for k in range(wire // 128):
                moved = jnp.take_along_axis(source[:, k * 128 : (k + 1) * 128], at & 127, axis=1)
                spread = jnp.where(at >> 7 == k, moved, spread)
        held = min(128, IJ - block * 128)
        out_ref[:, block * 128 : block * 128 + held] = spread[:, :held]


def shaped(shape, dtype):
    return jax.ShapeDtypeStruct(shape, dtype)


def body(integrals, amplitudes, ab_irrep, cd_irrep, occ_irrep):
    bf16, f32, i32 = jnp.bfloat16, jnp.float32, jnp.int32
    width = WIDE * TW
    chooser = pltpu.VMEM((16 * TW, width), bf16)
    numbers = pltpu.SMEM((IRREPS,), i32)

    def over_chips(sent):
        got = lax.all_to_all(sent, CHIPS, split_axis=0, concat_axis=0, tiled=True)
        return got.reshape(sent.shape[0] * sent.shape[1], sent.shape[2])

    def swapped(array):
        return lax.ppermute(array, "blk_2", [(0, 1), (1, 0)])

    def gathered_full(turn):
        sent = pl.pallas_call(
            functools.partial(send_full_kernel, turn),
            out_shape=shaped((SOURCES, FULL, width), bf16),
            in_specs=[VMEM, SMEM, SMEM],
            out_specs=VMEM,
            scratch_shapes=[chooser],
            compiler_params=GRANT,
        )(amplitudes, cd_irrep, occ_irrep)
        return over_chips(sent)

    def weights(turn, first, irreps):
        mine = pl.pallas_call(
            functools.partial(pack_rows_kernel, turn, first),
            out_shape=shaped((4 * TW + 8, width), bf16),
            in_specs=[VMEM, SMEM, SMEM],
            out_specs=VMEM,
            scratch_shapes=[chooser],
            compiler_params=GRANT,
        )(integrals, irreps, cd_irrep)
        return [mine, swapped(mine)]

    sent = pl.pallas_call(
        send_kernel,
        out_shape=shaped((SOURCES, ROWS, NARROW * TW), bf16),
        in_specs=[VMEM, SMEM, SMEM],
        out_specs=VMEM,
        scratch_shapes=[chooser, numbers],
        compiler_params=GRANT,
        name="send",
    )(amplitudes, cd_irrep, occ_irrep)
    held = over_chips(sent)

    number = np.arange(16 * 128, dtype=np.int32).reshape(16, 128)
    real, source = number < IJ, number // PAIRS

    def orbital_irrep(which):
        orbital = lax.broadcasted_iota(i32, (OCC, 16, 128), 0)
        hit = orbital == jnp.asarray(which)[None]
        return jnp.sum(jnp.where(hit, occ_irrep[:, None, None], 0), axis=0)

    irrep = jnp.bitwise_xor(orbital_irrep(number // OCC), orbital_irrep(number % OCC))
    kinds = jnp.asarray(np.where(real, source % 2 * IRREPS, 4 * IRREPS), dtype=i32)
    pairs = irrep + kinds
    numbered = np.arange(2 * IRREPS, dtype=np.int32)
    counts = jnp.sum((pairs == numbered[:, None, None]).astype(i32), axis=(1, 2))
    tiles = jnp.sum((cd_irrep == numbered[:IRREPS, None]).astype(i32), axis=1)
    need = (tiles + NARROW - 1) // NARROW
    alike = irrep == numbered[:IRREPS, None, None]
    taken = jnp.sum(jnp.where(alike, need[:, None, None], 0), axis=0)
    theirs = jnp.asarray(source)[None] == lax.broadcasted_iota(i32, (32, 16, 128), 0)
    rows = jnp.sum(jnp.where(theirs, taken, 0), axis=(1, 2))

    first_weights = weights(0, 0, ab_irrep)

    pair_list, choices = pl.pallas_call(
        list_kernel,
        out_shape=[shaped((LIST,), i32), shaped((4,), i32)],
        in_specs=[SMEM] * 5,
        out_specs=[SMEM] * 2,
        scratch_shapes=[numbers] * 2,
        compiler_params=GRANT,
        name="list",
    )(cd_irrep, occ_irrep, counts, rows, ab_irrep)
    chosen, general, most = choices[0], choices[1] > 0, choices[2]

    def products(full, wire, which, operands, rows_list):
        rows = SOURCES * (FULL if full else ROWS)
        return pl.pallas_call(
            functools.partial(product_kernel, full),
            out_shape=pltpu.VMEM((32, 16, wire), f32),
            in_specs=[SMEM] + [VMEM] * len(operands) + [SMEM],
            out_specs=VMEM,
            scratch_shapes=[pltpu.VMEM((rows, 128), f32)] * 4
            + [pltpu.VMEM((wire, 128), f32), pltpu.VMEM((8 * TW, wire), f32)],
            compiler_params=LARGE,
        )(which, *operands, rows_list)

    def full_products(wire, which):
        rows_list = pl.pallas_call(
            full_list_kernel,
            out_shape=shaped((LIST,), i32),
            in_specs=[SMEM] * 2,
            out_specs=SMEM,
            scratch_shapes=[numbers],
            compiler_params=GRANT,
            name="full_list",
        )(occ_irrep, pair_list)
        operands = [gathered_full(0), gathered_full(1), *first_weights, *weights(1, 16, pair_list)]
        return products(True, wire, which, operands, rows_list)

    def reduced(wire, which):
        partial = lax.cond(
            general,
            lambda: full_products(wire, which),
            lambda: products(False, wire, which, [held, *first_weights], pair_list),
        ).astype(jnp.float16)
        arrived = lax.all_to_all(partial, "panel", split_axis=0, concat_axis=0, tiled=True)
        mine, partners = pl.pallas_call(
            sum_kernel,
            out_shape=[shaped((8, wire), f32)] * 2,
            in_specs=[VMEM],
            out_specs=[VMEM] * 2,
            compiler_params=GRANT,
            name="sum",
        )(arrived.astype(f32))
        spots = pl.pallas_call(
            functools.partial(places_kernel, wire - 1),
            out_shape=[shaped((16, 128), i32)] * 2,
            in_specs=[SMEM, SMEM, VMEM],
            out_specs=[VMEM] * 2,
            compiler_params=GRANT,
            name="places",
        )(which, pair_list, pairs)
        theirs = swapped(partners)
        return pl.pallas_call(
            finish_kernel,
            out_shape=shaped((8, IJ), f32),
            in_specs=[VMEM] * 4,
            out_specs=VMEM,
            compiler_params=GRANT,
            name="finish",
        )(mine, theirs, *spots)

    zero = jnp.zeros((1,), i32)

    def all_rounds():
        cols = LONG - 1

        def add_round(number, total):
            which = jnp.full((1,), number, i32)
            return total + reduced(LONG, which)

        return lax.fori_loop(0, (most + cols - 1) // cols, add_round, jnp.zeros((8, IJ), f32))

    branches = [functools.partial(reduced, wire, zero) for wire in WIRES]
    return lax.switch(chosen, [*branches, all_rounds])


def solution(mesh):
    split = Mesh(
        mesh.devices.reshape(2, 8, 2, mesh.shape["panel"]), ("blk_0", "blk_1", "blk_2", "panel")
    )
    return jax.shard_map(
        body,
        mesh=split,
        in_specs=(P(BLK, "panel"), P(BLK, "panel"), P(BLK), P("panel"), P()),
        out_specs=P(BLK_PANEL, None),
        check_vma=False,
    )
```

```python
import functools

import jax
import jax.numpy as jnp
import numpy as np
from jax import lax
from jax.experimental import pallas as pl
from jax.experimental.pallas import tpu as pltpu
from jax.sharding import Mesh
from jax.sharding import PartitionSpec as P


TW = 64
IRREPS = 8
OCC = 40
IJ = 1600
BLK = ("blk_0", "blk_1", "blk_2")
BLK_PANEL = ("blk_0", "blk_1", "blk_2", "panel")
CHIPS = ("blk_0", "blk_1")

PAIRS = 50
SOURCES = 16
WIDE = 8
NARROW = 2
PARTS = WIDE // NARROW
ROWS = 144
FULL = 56
WIRES = (256, 384)
LONG = 512
KEPT = 24
LIST = KEPT + 1384

SMEM = pl.BlockSpec(memory_space=pltpu.SMEM)
VMEM = pl.BlockSpec(memory_space=pltpu.VMEM)
NT = (((1,), (1,)), ((), ()))
GRANT = pltpu.CompilerParams(vmem_limit_bytes=24 << 20)
LARGE = pltpu.CompilerParams(vmem_limit_bytes=40 << 20)


def places(cd_ref):
    irreps = [cd_ref[t] for t in range(16)]
    ranks = []
    for t in range(16):
        rank = jnp.int32(0)
        for earlier in range(t):
            rank += jnp.where(irreps[earlier] == irreps[t], 1, 0)
        ranks.append(rank)
    return irreps, ranks


def fill_chooser(choose, ranks, turn):
    width = WIDE * TW
    row = lax.broadcasted_iota(jnp.int32, (TW, width), 0)
    col = lax.broadcasted_iota(jnp.int32, (TW, width), 1)
    place = jnp.where(col % TW == row, col // TW + turn * WIDE, -1)
    for t in range(16):
        hit = jnp.where(place == ranks[t], 1.0, 0.0)
        choose[t * TW : (t + 1) * TW, :] = hit.astype(jnp.bfloat16)


def column_irreps(irreps):
    lane = lax.broadcasted_iota(jnp.int32, (1, 16 * TW), 1) // TW
    found = jnp.zeros((1, 16 * TW), jnp.int32)
    for t in range(16):
        found = jnp.where(lane == t, irreps[t], found)
    return found


def pack(values, row_irrep, col_irrep, choose):
    kept = jnp.where(row_irrep == col_irrep, values.astype(jnp.float32), 0.0)
    return jnp.dot(
        kept.astype(jnp.bfloat16), choose[...], preferred_element_type=jnp.float32
    ).astype(jnp.bfloat16)


def my_pairs(occ_ref):
    blk = lax.axis_index("blk_0") * 16 + lax.axis_index("blk_1") * 2 + lax.axis_index("blk_2")
    upper = blk * 5 // 4
    at = blk % 4 * 10
    left = [occ_ref[upper], occ_ref[jnp.minimum(upper + 1, OCC - 1)]]
    row = lax.broadcasted_iota(jnp.int32, (PAIRS, 1), 0)
    column = jnp.zeros((PAIRS, 1), jnp.int32)
    irreps = []
    for m in range(PAIRS):
        later = at + m >= OCC
        right = occ_ref[at + m - jnp.where(later, OCC, 0)]
        irreps.append(jnp.bitwise_xor(jnp.where(later, left[1], left[0]), right))
        column = jnp.where(row == m, irreps[m], column)
    return irreps, column


def count_rows(irreps, need):
    for g in range(IRREPS):
        tiles = jnp.int32(0)
        for irrep in irreps:
            tiles += jnp.where(irrep == g, 1, 0)
        need[g] = (tiles + NARROW - 1) // NARROW


def send_kernel(t_ref, cd_ref, occ_ref, out_ref, choose, need):
    irreps, ranks = places(cd_ref)
    fill_chooser(choose, ranks, 0)
    count_rows(irreps, need)
    pairs, row_irrep = my_pairs(occ_ref)
    packed = pack(t_ref[...], row_irrep, column_irreps(irreps), choose)
    lane = lax.broadcasted_iota(jnp.int32, (1, PAIRS), 1)
    first = jnp.zeros((1, PAIRS), jnp.int32)
    count = jnp.zeros((1, PAIRS), jnp.int32)
    row = jnp.int32(0)
    for m in range(PAIRS):
        rows = need[pairs[m]]
        first = jnp.where(lane == m, row, first)
        count = jnp.where(lane == m, rows, count)
        row += rows
    place = lax.broadcasted_iota(jnp.int32, (ROWS, PAIRS), 0)
    width = NARROW * TW
    spread = None
    for part in range(PARTS):
        at = jnp.where(count > part, first + part, -1)
        move = jnp.where(place == at, 1.0, 0.0).astype(jnp.bfloat16)
        moved = jnp.dot(
            move, packed[:, part * width : (part + 1) * width], preferred_element_type=jnp.float32
        )
        spread = moved if spread is None else spread + moved
    spread = spread.astype(jnp.bfloat16)
    for s in range(SOURCES):
        out_ref[s] = spread


def send_full_kernel(turn, t_ref, cd_ref, occ_ref, out_ref, choose):
    irreps, ranks = places(cd_ref)
    fill_chooser(choose, ranks, turn)
    _, row_irrep = my_pairs(occ_ref)
    packed = pack(t_ref[...], row_irrep, column_irreps(irreps), choose)
    for s in range(SOURCES):
        out_ref[s, :PAIRS, :] = packed
        out_ref[s, PAIRS:, :] = jnp.zeros((FULL - PAIRS, WIDE * TW), jnp.bfloat16)


def pack_rows_kernel(turn, first, v_ref, ab_ref, cd_ref, out_ref, choose):
    irreps, ranks = places(cd_ref)
    fill_chooser(choose, ranks, turn)
    row = lax.broadcasted_iota(jnp.int32, (4 * TW, 1), 0) // TW
    row_irrep = jnp.zeros((4 * TW, 1), jnp.int32)
    for i in range(4):
        row_irrep = jnp.where(row == i, ab_ref[first + i], row_irrep)
    lane = lax.broadcasted_iota(jnp.int32, (8, WIDE * TW), 1) // 128
    told = jnp.zeros((8, WIDE * TW), jnp.int32)
    for i in range(4):
        told = jnp.where(lane == i, ab_ref[first + i], told)
    out_ref[4 * TW :, :] = told.astype(jnp.float32).astype(jnp.bfloat16)
    out_ref[: 4 * TW, :] = pack(v_ref[...], row_irrep, column_irreps(irreps), choose)


def list_kernel(cd_ref, occ_ref, counts_ref, rows_ref, ab_ref, list_ref, chosen_ref, count, need):
    core = lax.axis_index("blk_2")
    irreps, _ = places(cd_ref)
    count_rows(irreps, need)
    start = jnp.int32(KEPT)
    for g in range(IRREPS):
        list_ref[g] = start
        count[g] = start
        start += counts_ref[core * IRREPS + g]
    for k in range(IRREPS, 16):
        list_ref[k] = start
    for k in range(4):
        list_ref[16 + k] = ab_ref[k]
        list_ref[20 + k] = 0
    tiles, longest, most = jnp.int32(0), jnp.int32(0), jnp.int32(0)
    for g in range(IRREPS):
        tiles = jnp.maximum(tiles, need[g])
    for k in range(32):
        longest = jnp.maximum(longest, rows_ref[k])
    for k in range(2 * IRREPS):
        most = jnp.maximum(most, counts_ref[k])
    chosen = jnp.int32(0)
    for wire in WIRES:
        chosen += jnp.where(most >= wire, 1, 0)
    chosen_ref[0] = chosen
    chosen_ref[1] = jnp.where(jnp.logical_or(tiles > PARTS, longest > ROWS), 1, 0)
    chosen_ref[2] = most
    chosen_ref[3] = 0

    for mine in range(2):

        @pl.when(core == mine)
        def _():
            @pl.loop(0, 8)
            def _(part):
                for chip in range(2):
                    row = (part * 2 + chip) * ROWS
                    last = row + ROWS - 1
                    for m in range(PAIRS):
                        i, j = divmod((chip * 2 + mine) * PAIRS + m, OCC)
                        if m == 0 or j == 0:
                            left = occ_ref[part * 5 + i]
                        irrep = jnp.bitwise_xor(left, occ_ref[j])
                        at = count[irrep]
                        count[irrep] = at + 1
                        list_ref[at] = jnp.minimum(row, last)
                        row += need[irrep]

    @pl.loop(0, (LIST - KEPT - IJ // 2) // 8)
    def _(k):
        for u in range(8):
            list_ref[KEPT + IJ // 2 + k * 8 + u] = 0


def full_list_kernel(occ_ref, starts_ref, list_ref, count):
    core = lax.axis_index("blk_2")
    for g in range(IRREPS):
        count[g] = starts_ref[g]
    for k in range(KEPT):
        list_ref[k] = starts_ref[k]

    @pl.loop(0, OCC)
    def _(i):
        left = occ_ref[i]

        @pl.loop(0, OCC)
        def _(j):
            pair = i * OCC + j
            source = pair // PAIRS

            @pl.when((source & 1) == core)
            def _():
                irrep = jnp.bitwise_xor(left, occ_ref[j])
                at = count[irrep]
                count[irrep] = at + 1
                list_ref[at] = (source >> 1) * FULL + pair - source * PAIRS

    @pl.loop(KEPT + IJ // 2, LIST)
    def _(k):
        list_ref[k] = 0


def times(held, weight):
    return lax.dot_general(held, weight, NT, preferred_element_type=jnp.float32)


def joined_rows(held_ref):
    held = held_ref[...].astype(jnp.float32)
    count = held.shape[0]
    rows = [held] + [pltpu.roll(held, count - part, 0) for part in range(1, PARTS)]
    return jnp.concatenate([r.astype(jnp.bfloat16) for r in rows], axis=1)


def product_kernel(full, round_ref, *refs):
    turns = 2 if full else 1
    held, weights, refs = refs[:turns], refs[turns : 3 * turns], refs[3 * turns :]
    list_ref, out_ref, *products, dense, both = refs
    wire = dense.shape[0]
    cols = wire - 1
    rows = [ref[...] for ref in held] if full else [joined_rows(held[0])]
    for core in range(2):
        total = None
        for turn in range(turns):
            part = times(rows[turn], weights[2 * turn + core][: 4 * TW, :])
            total = part if total is None else total + part
        for q in range(2):
            products[2 * core + q][...] = total[:, q * 128 : (q + 1) * 128]
    lower = lax.broadcasted_iota(jnp.int32, (1, 128), 1) < TW
    skip = round_ref[0] * cols
    told = weights[1][4 * TW :, :].astype(jnp.float32)
    tile_irreps = [list_ref[16 + i] for i in range(4)]
    tile_irreps += [jnp.max(told[:, i * 128 : (i + 1) * 128]).astype(jnp.int32) for i in range(4)]
    for q in range(4):
        product = products[q]
        dense[...] = jnp.zeros_like(dense)
        irreps = tile_irreps[2 * q : 2 * q + 2]
        starts = [jnp.minimum(list_ref[g] + skip, KEPT + IJ // 2) for g in irreps]
        counts = [list_ref[g + 1] - list_ref[g] - skip for g in irreps]
        most = jnp.clip(jnp.maximum(counts[0], counts[1]), 0, cols)

        @pl.loop(0, (most + 7) // 8)
        def _(block):
            base = block * 8
            for u in range(8):
                at = [list_ref[start + base + u] for start in starts]
                picked = [product[pl.ds(a, 1), :] for a in at]
                dense[pl.ds(base + u, 1), :] = jnp.where(lower, picked[0], picked[1])

        both[q * 128 : (q + 1) * 128, :] = dense[...].T
    largest = jnp.max(jnp.max(jnp.abs(both[...]), axis=1, keepdims=True), axis=0, keepdims=True)
    power = 14.0 - jnp.floor(jnp.log2(jnp.maximum(largest, 1e-30)))
    lane = lax.broadcasted_iota(jnp.int32, (4 * TW, wire), 1)
    for core in range(2):
        scaled = both[core * 4 * TW : (core + 1) * 4 * TW, :] * jnp.exp2(power)
        sent = jnp.where(lane == cols, power, scaled).reshape(32, 8, wire)
        out_ref[:, core * 8 : (core + 1) * 8, :] = sent


def sum_kernel(got_ref, mine_ref, partner_ref):
    cols = got_ref.shape[2] - 1
    total = None
    for s in range(32):
        got = got_ref[s]
        got = got * jnp.exp2(-got[:, cols:])
        total = got if total is None else total + got
    mine_ref[...] = total[:8]
    partner_ref[...] = total[8:]


def places_kernel(cols, round_ref, list_ref, pairs_ref, *place_refs):
    core = lax.axis_index("blk_2")
    irrep = list_ref[16 + lax.axis_index("panel") // 8]
    pairs = pairs_ref[...]
    hits = [pairs == irrep + core * IRREPS, pairs == irrep + (1 - core) * IRREPS]
    count = jnp.where(hits[0], 1, jnp.where(hits[1], 1 << 16, 0))
    row = lax.broadcasted_iota(jnp.int32, pairs.shape, 0)
    lane = lax.broadcasted_iota(jnp.int32, pairs.shape, 1)
    for step in (1, 2, 4, 8, 16, 32, 64):
        count += jnp.where(lane >= step, pltpu.roll(count, step, 1), 0)
    whole = jnp.broadcast_to(count[:, 127:], pairs.shape)
    above = whole
    for step in (1, 2, 4, 8):
        above += jnp.where(row >= step, pltpu.roll(above, step, 0), 0)
    count += above - whole
    skip = round_ref[0] * cols + 1
    for hit, found, place_ref in zip(hits, (count & 0xFFFF, count >> 16), place_refs):
        place = jnp.where(hit, found - skip, -1)
        place_ref[...] = jnp.where(place < cols, place, -1)


def finish_kernel(mine_ref, partner_ref, mine_place_ref, partner_place_ref, out_ref):
    wire = mine_ref.shape[1]
    sources = [mine_ref[...], partner_ref[...]]
    for block in range(13):
        spread = jnp.zeros((8, 128), jnp.float32)
        for place_ref, source in zip((mine_place_ref, partner_place_ref), sources):
            at = jnp.broadcast_to(place_ref[block : block + 1, :], (8, 128))
            for k in range(wire // 128):
                moved = jnp.take_along_axis(source[:, k * 128 : (k + 1) * 128], at & 127, axis=1)
                spread = jnp.where(at >> 7 == k, moved, spread)
        held = min(128, IJ - block * 128)
        out_ref[:, block * 128 : block * 128 + held] = spread[:, :held]


def shaped(shape, dtype):
    return jax.ShapeDtypeStruct(shape, dtype)


def body(integrals, amplitudes, ab_irrep, cd_irrep, occ_irrep):
    bf16, f32, i32 = jnp.bfloat16, jnp.float32, jnp.int32
    width = WIDE * TW
    chooser = pltpu.VMEM((16 * TW, width), bf16)
    numbers = pltpu.SMEM((IRREPS,), i32)

    def over_chips(sent):
        got = lax.all_to_all(sent, CHIPS, split_axis=0, concat_axis=0, tiled=True)
        return got.reshape(sent.shape[0] * sent.shape[1], sent.shape[2])

    def swapped(array):
        return lax.ppermute(array, "blk_2", [(0, 1), (1, 0)])

    def gathered_full(turn):
        sent = pl.pallas_call(
            functools.partial(send_full_kernel, turn),
            out_shape=shaped((SOURCES, FULL, width), bf16),
            in_specs=[VMEM, SMEM, SMEM],
            out_specs=VMEM,
            scratch_shapes=[chooser],
            compiler_params=GRANT,
        )(amplitudes, cd_irrep, occ_irrep)
        return over_chips(sent)

    def weights(turn, first, irreps):
        mine = pl.pallas_call(
            functools.partial(pack_rows_kernel, turn, first),
            out_shape=shaped((4 * TW + 8, width), bf16),
            in_specs=[VMEM, SMEM, SMEM],
            out_specs=VMEM,
            scratch_shapes=[chooser],
            compiler_params=GRANT,
        )(integrals, irreps, cd_irrep)
        return [mine, swapped(mine)]

    sent = pl.pallas_call(
        send_kernel,
        out_shape=shaped((SOURCES, ROWS, NARROW * TW), bf16),
        in_specs=[VMEM, SMEM, SMEM],
        out_specs=VMEM,
        scratch_shapes=[chooser, numbers],
        compiler_params=GRANT,
        name="send",
    )(amplitudes, cd_irrep, occ_irrep)
    held = over_chips(sent)

    number = np.arange(16 * 128, dtype=np.int32).reshape(16, 128)
    real, source = number < IJ, number // PAIRS

    def orbital_irrep(which):
        orbital = lax.broadcasted_iota(i32, (OCC, 16, 128), 0)
        hit = orbital == jnp.asarray(which)[None]
        return jnp.sum(jnp.where(hit, occ_irrep[:, None, None], 0), axis=0)

    irrep = jnp.bitwise_xor(orbital_irrep(number // OCC), orbital_irrep(number % OCC))
    kinds = jnp.asarray(np.where(real, source % 2 * IRREPS, 4 * IRREPS), dtype=i32)
    pairs = irrep + kinds
    numbered = np.arange(2 * IRREPS, dtype=np.int32)
    counts = jnp.sum((pairs == numbered[:, None, None]).astype(i32), axis=(1, 2))
    tiles = jnp.sum((cd_irrep == numbered[:IRREPS, None]).astype(i32), axis=1)
    need = (tiles + NARROW - 1) // NARROW
    alike = irrep == numbered[:IRREPS, None, None]
    taken = jnp.sum(jnp.where(alike, need[:, None, None], 0), axis=0)
    theirs = jnp.asarray(source)[None] == lax.broadcasted_iota(i32, (32, 16, 128), 0)
    rows = jnp.sum(jnp.where(theirs, taken, 0), axis=(1, 2))

    first_weights = weights(0, 0, ab_irrep)

    pair_list, choices = pl.pallas_call(
        list_kernel,
        out_shape=[shaped((LIST,), i32), shaped((4,), i32)],
        in_specs=[SMEM] * 5,
        out_specs=[SMEM] * 2,
        scratch_shapes=[numbers] * 2,
        compiler_params=GRANT,
        name="list",
    )(cd_irrep, occ_irrep, counts, rows, ab_irrep)
    chosen, general, most = choices[0], choices[1] > 0, choices[2]

    def products(full, wire, which, operands, rows_list):
        rows = SOURCES * (FULL if full else ROWS)
        return pl.pallas_call(
            functools.partial(product_kernel, full),
            out_shape=pltpu.VMEM((32, 16, wire), f32),
            in_specs=[SMEM] + [VMEM] * len(operands) + [SMEM],
            out_specs=VMEM,
            scratch_shapes=[pltpu.VMEM((rows, 128), f32)] * 4
            + [pltpu.VMEM((wire, 128), f32), pltpu.VMEM((8 * TW, wire), f32)],
            compiler_params=LARGE,
        )(which, *operands, rows_list)

    def full_products(wire, which):
        rows_list = pl.pallas_call(
            full_list_kernel,
            out_shape=shaped((LIST,), i32),
            in_specs=[SMEM] * 2,
            out_specs=SMEM,
            scratch_shapes=[numbers],
            compiler_params=GRANT,
            name="full_list",
        )(occ_irrep, pair_list)
        operands = [gathered_full(0), gathered_full(1), *first_weights, *weights(1, 16, pair_list)]
        return products(True, wire, which, operands, rows_list)

    def places_of(cols, which):
        return pl.pallas_call(
            functools.partial(places_kernel, cols),
            out_shape=[shaped((16, 128), i32)] * 2,
            in_specs=[SMEM, SMEM, VMEM],
            out_specs=[VMEM] * 2,
            compiler_params=GRANT,
            name="places",
        )(which, pair_list, pairs)

    zero = jnp.zeros((1,), i32)
    first_spots = places_of(IJ, zero)

    def reduced(wire, which, spots=None):
        partial = lax.cond(
            general,
            lambda: full_products(wire, which),
            lambda: products(False, wire, which, [held, *first_weights], pair_list),
        ).astype(jnp.float16)
        arrived = lax.all_to_all(partial, "panel", split_axis=0, concat_axis=0, tiled=True)
        mine, partners = pl.pallas_call(
            sum_kernel,
            out_shape=[shaped((8, wire), f32)] * 2,
            in_specs=[VMEM],
            out_specs=[VMEM] * 2,
            compiler_params=GRANT,
            name="sum",
        )(arrived.astype(f32))
        if spots is None:
            spots = places_of(wire - 1, which)
        theirs = swapped(partners)
        return pl.pallas_call(
            finish_kernel,
            out_shape=shaped((8, IJ), f32),
            in_specs=[VMEM] * 4,
            out_specs=VMEM,
            compiler_params=GRANT,
            name="finish",
        )(mine, theirs, *spots)

    def all_rounds():
        cols = LONG - 1

        def add_round(number, total):
            which = jnp.full((1,), number, i32)
            return total + reduced(LONG, which)

        return lax.fori_loop(0, (most + cols - 1) // cols, add_round, jnp.zeros((8, IJ), f32))

    branches = [functools.partial(reduced, wire, zero, first_spots) for wire in WIRES]
    return lax.switch(chosen, [*branches, all_rounds])


def solution(mesh):
    split = Mesh(
        mesh.devices.reshape(2, 8, 2, mesh.shape["panel"]), ("blk_0", "blk_1", "blk_2", "panel")
    )
    return jax.shard_map(
        body,
        mesh=split,
        in_specs=(P(BLK, "panel"), P(BLK, "panel"), P(BLK), P("panel"), P()),
        out_specs=P(BLK_PANEL, None),
        check_vma=False,
    )
```

```python
import functools

import jax
import jax.numpy as jnp
import numpy as np
from jax import lax
from jax.experimental import pallas as pl
from jax.experimental.pallas import tpu as pltpu
from jax.sharding import Mesh
from jax.sharding import PartitionSpec as P


TW = 64
IRREPS = 8
OCC = 40
IJ = 1600
BLK = ("blk_0", "blk_1", "blk_2")
BLK_PANEL = ("blk_0", "blk_1", "blk_2", "panel")
CHIPS = ("blk_0", "blk_1")

PAIRS = 50
SOURCES = 16
WIDE = 8
NARROW = 2
PARTS = WIDE // NARROW
ROWS = 144
FULL = 56
WIRES = (256, 384)
LONG = 512
KEPT = 24
LIST = KEPT + 1384

SMEM = pl.BlockSpec(memory_space=pltpu.SMEM)
VMEM = pl.BlockSpec(memory_space=pltpu.VMEM)
NT = (((1,), (1,)), ((), ()))
GRANT = pltpu.CompilerParams(vmem_limit_bytes=24 << 20)
LARGE = pltpu.CompilerParams(vmem_limit_bytes=40 << 20)


def places(cd_ref):
    irreps = [cd_ref[t] for t in range(16)]
    ranks = []
    for t in range(16):
        rank = jnp.int32(0)
        for earlier in range(t):
            rank += jnp.where(irreps[earlier] == irreps[t], 1, 0)
        ranks.append(rank)
    return irreps, ranks


def fill_chooser(choose, ranks, turn):
    width = WIDE * TW
    row = lax.broadcasted_iota(jnp.int32, (TW, width), 0)
    col = lax.broadcasted_iota(jnp.int32, (TW, width), 1)
    place = jnp.where(col % TW == row, col // TW + turn * WIDE, -1)
    for t in range(16):
        hit = jnp.where(place == ranks[t], 1.0, 0.0)
        choose[t * TW : (t + 1) * TW, :] = hit.astype(jnp.bfloat16)


def column_irreps(irreps):
    lane = lax.broadcasted_iota(jnp.int32, (1, 16 * TW), 1) // TW
    found = jnp.zeros((1, 16 * TW), jnp.int32)
    for t in range(16):
        found = jnp.where(lane == t, irreps[t], found)
    return found


def pack(values, row_irrep, col_irrep, choose):
    kept = jnp.where(row_irrep == col_irrep, values.astype(jnp.float32), 0.0)
    return jnp.dot(
        kept.astype(jnp.bfloat16), choose[...], preferred_element_type=jnp.float32
    ).astype(jnp.bfloat16)


def my_pairs(occ_ref):
    blk = lax.axis_index("blk_0") * 16 + lax.axis_index("blk_1") * 2 + lax.axis_index("blk_2")
    upper = blk * 5 // 4
    at = blk % 4 * 10
    left = [occ_ref[upper], occ_ref[jnp.minimum(upper + 1, OCC - 1)]]
    row = lax.broadcasted_iota(jnp.int32, (PAIRS, 1), 0)
    column = jnp.zeros((PAIRS, 1), jnp.int32)
    irreps = []
    for m in range(PAIRS):
        later = at + m >= OCC
        right = occ_ref[at + m - jnp.where(later, OCC, 0)]
        irreps.append(jnp.bitwise_xor(jnp.where(later, left[1], left[0]), right))
        column = jnp.where(row == m, irreps[m], column)
    return irreps, column


def count_rows(irreps, need):
    for g in range(IRREPS):
        tiles = jnp.int32(0)
        for irrep in irreps:
            tiles += jnp.where(irrep == g, 1, 0)
        need[g] = (tiles + NARROW - 1) // NARROW


def send_kernel(t_ref, cd_ref, occ_ref, out_ref, choose, need):
    irreps, ranks = places(cd_ref)
    fill_chooser(choose, ranks, 0)
    count_rows(irreps, need)
    pairs, row_irrep = my_pairs(occ_ref)
    packed = pack(t_ref[...], row_irrep, column_irreps(irreps), choose)
    lane = lax.broadcasted_iota(jnp.int32, (1, PAIRS), 1)
    first = jnp.zeros((1, PAIRS), jnp.int32)
    count = jnp.zeros((1, PAIRS), jnp.int32)
    row = jnp.int32(0)
    for m in range(PAIRS):
        rows = need[pairs[m]]
        first = jnp.where(lane == m, row, first)
        count = jnp.where(lane == m, rows, count)
        row += rows
    place = lax.broadcasted_iota(jnp.int32, (ROWS, PAIRS), 0)
    width = NARROW * TW
    spread = None
    for part in range(PARTS):
        at = jnp.where(count > part, first + part, -1)
        move = jnp.where(place == at, 1.0, 0.0).astype(jnp.bfloat16)
        moved = jnp.dot(
            move, packed[:, part * width : (part + 1) * width], preferred_element_type=jnp.float32
        )
        spread = moved if spread is None else spread + moved
    spread = spread.astype(jnp.bfloat16)
    for s in range(SOURCES):
        out_ref[s] = spread


def send_full_kernel(turn, t_ref, cd_ref, occ_ref, out_ref, choose):
    irreps, ranks = places(cd_ref)
    fill_chooser(choose, ranks, turn)
    _, row_irrep = my_pairs(occ_ref)
    packed = pack(t_ref[...], row_irrep, column_irreps(irreps), choose)
    for s in range(SOURCES):
        out_ref[s, :PAIRS, :] = packed
        out_ref[s, PAIRS:, :] = jnp.zeros((FULL - PAIRS, WIDE * TW), jnp.bfloat16)


def pack_rows_kernel(turn, first, v_ref, ab_ref, cd_ref, out_ref, choose):
    irreps, ranks = places(cd_ref)
    fill_chooser(choose, ranks, turn)
    row = lax.broadcasted_iota(jnp.int32, (4 * TW, 1), 0) // TW
    row_irrep = jnp.zeros((4 * TW, 1), jnp.int32)
    for i in range(4):
        row_irrep = jnp.where(row == i, ab_ref[first + i], row_irrep)
    lane = lax.broadcasted_iota(jnp.int32, (8, WIDE * TW), 1) // 128
    told = jnp.zeros((8, WIDE * TW), jnp.int32)
    for i in range(4):
        told = jnp.where(lane == i, ab_ref[first + i], told)
    out_ref[4 * TW :, :] = told.astype(jnp.float32).astype(jnp.bfloat16)
    out_ref[: 4 * TW, :] = pack(v_ref[...], row_irrep, column_irreps(irreps), choose)


def list_kernel(cd_ref, occ_ref, counts_ref, rows_ref, ab_ref, list_ref, chosen_ref, count, need):
    core = lax.axis_index("blk_2")
    irreps, _ = places(cd_ref)
    count_rows(irreps, need)
    start = jnp.int32(KEPT)
    for g in range(IRREPS):
        list_ref[g] = start
        count[g] = start
        start += counts_ref[core * IRREPS + g]
    for k in range(IRREPS, 16):
        list_ref[k] = start
    for k in range(4):
        list_ref[16 + k] = ab_ref[k]
        list_ref[20 + k] = 0
    tiles, longest, most = jnp.int32(0), jnp.int32(0), jnp.int32(0)
    for g in range(IRREPS):
        tiles = jnp.maximum(tiles, need[g])
    for k in range(32):
        longest = jnp.maximum(longest, rows_ref[k])
    for k in range(2 * IRREPS):
        most = jnp.maximum(most, counts_ref[k])
    chosen = jnp.int32(0)
    for wire in WIRES:
        chosen += jnp.where(most >= wire, 1, 0)
    chosen_ref[0] = chosen
    chosen_ref[1] = jnp.where(jnp.logical_or(tiles > PARTS, longest > ROWS), 1, 0)
    chosen_ref[2] = most
    chosen_ref[3] = 0

    for mine in range(2):

        @pl.when(core == mine)
        def _():
            @pl.loop(0, 8)
            def _(part):
                for chip in range(2):
                    row = (part * 2 + chip) * ROWS
                    last = row + ROWS - 1
                    for m in range(PAIRS):
                        i, j = divmod((chip * 2 + mine) * PAIRS + m, OCC)
                        if m == 0 or j == 0:
                            left = occ_ref[part * 5 + i]
                        irrep = jnp.bitwise_xor(left, occ_ref[j])
                        at = count[irrep]
                        count[irrep] = at + 1
                        list_ref[at] = jnp.minimum(row, last)
                        row += need[irrep]

    @pl.loop(0, (LIST - KEPT - IJ // 2) // 8)
    def _(k):
        for u in range(8):
            list_ref[KEPT + IJ // 2 + k * 8 + u] = 0


def full_list_kernel(occ_ref, starts_ref, list_ref, count):
    core = lax.axis_index("blk_2")
    for g in range(IRREPS):
        count[g] = starts_ref[g]
    for k in range(KEPT):
        list_ref[k] = starts_ref[k]

    @pl.loop(0, OCC)
    def _(i):
        left = occ_ref[i]

        @pl.loop(0, OCC)
        def _(j):
            pair = i * OCC + j
            source = pair // PAIRS

            @pl.when((source & 1) == core)
            def _():
                irrep = jnp.bitwise_xor(left, occ_ref[j])
                at = count[irrep]
                count[irrep] = at + 1
                list_ref[at] = (source >> 1) * FULL + pair - source * PAIRS

    @pl.loop(KEPT + IJ // 2, LIST)
    def _(k):
        list_ref[k] = 0


def times(held, weight):
    return lax.dot_general(held, weight, NT, preferred_element_type=jnp.float32)


def joined_rows(held_ref):
    held = held_ref[...].astype(jnp.float32)
    count = held.shape[0]
    rows = [held] + [pltpu.roll(held, count - part, 0) for part in range(1, PARTS)]
    return jnp.concatenate([r.astype(jnp.bfloat16) for r in rows], axis=1)


def product_kernel(full, round_ref, *refs):
    turns = 2 if full else 1
    held, weights, refs = refs[:turns], refs[turns : 3 * turns], refs[3 * turns :]
    list_ref, out_ref, *products, dense, both = refs
    wire = dense.shape[0]
    cols = wire - 1
    rows = [ref[...] for ref in held] if full else [joined_rows(held[0])]
    total = None
    for turn in range(turns):
        both_cores = [weights[2 * turn + core][: 4 * TW, :] for core in range(2)]
        part = times(rows[turn], jnp.concatenate(both_cores, axis=0))
        total = part if total is None else total + part
    for q in range(4):
        products[q][...] = total[:, q * 128 : (q + 1) * 128]
    lower = lax.broadcasted_iota(jnp.int32, (1, 128), 1) < TW
    skip = round_ref[0] * cols
    told = weights[1][4 * TW :, :].astype(jnp.float32)
    tile_irreps = [list_ref[16 + i] for i in range(4)]
    tile_irreps += [jnp.max(told[:, i * 128 : (i + 1) * 128]).astype(jnp.int32) for i in range(4)]
    for q in range(4):
        product = products[q]
        dense[...] = jnp.zeros_like(dense)
        irreps = tile_irreps[2 * q : 2 * q + 2]
        starts = [jnp.minimum(list_ref[g] + skip, KEPT + IJ // 2) for g in irreps]
        counts = [list_ref[g + 1] - list_ref[g] - skip for g in irreps]
        most = jnp.clip(jnp.maximum(counts[0], counts[1]), 0, cols)

        @pl.loop(0, (most + 7) // 8)
        def _(block):
            base = block * 8
            for u in range(8):
                at = [list_ref[start + base + u] for start in starts]
                picked = [product[pl.ds(a, 1), :] for a in at]
                dense[pl.ds(base + u, 1), :] = jnp.where(lower, picked[0], picked[1])

        both[q * 128 : (q + 1) * 128, :] = dense[...].T
    largest = jnp.max(jnp.max(jnp.abs(both[...]), axis=1, keepdims=True), axis=0, keepdims=True)
    power = 14.0 - jnp.floor(jnp.log2(jnp.maximum(largest, 1e-30)))
    lane = lax.broadcasted_iota(jnp.int32, (4 * TW, wire), 1)
    for core in range(2):
        scaled = both[core * 4 * TW : (core + 1) * 4 * TW, :] * jnp.exp2(power)
        sent = jnp.where(lane == cols, power, scaled).reshape(32, 8, wire)
        out_ref[:, core * 8 : (core + 1) * 8, :] = sent


def sum_kernel(got_ref, mine_ref, partner_ref):
    cols = got_ref.shape[2] - 1
    total = None
    for s in range(32):
        got = got_ref[s]
        got = got * jnp.exp2(-got[:, cols:])
        total = got if total is None else total + got
    mine_ref[...] = total[:8]
    partner_ref[...] = total[8:]


def places_kernel(cols, round_ref, list_ref, pairs_ref, *place_refs):
    core = lax.axis_index("blk_2")
    irrep = list_ref[16 + lax.axis_index("panel") // 8]
    pairs = pairs_ref[...]
    hits = [pairs == irrep + core * IRREPS, pairs == irrep + (1 - core) * IRREPS]
    count = jnp.where(hits[0], 1, jnp.where(hits[1], 1 << 16, 0))
    row = lax.broadcasted_iota(jnp.int32, pairs.shape, 0)
    lane = lax.broadcasted_iota(jnp.int32, pairs.shape, 1)
    for step in (1, 2, 4, 8, 16, 32, 64):
        count += jnp.where(lane >= step, pltpu.roll(count, step, 1), 0)
    whole = jnp.broadcast_to(count[:, 127:], pairs.shape)
    above = whole
    for step in (1, 2, 4, 8):
        above += jnp.where(row >= step, pltpu.roll(above, step, 0), 0)
    count += above - whole
    skip = round_ref[0] * cols + 1
    for hit, found, place_ref in zip(hits, (count & 0xFFFF, count >> 16), place_refs):
        place = jnp.where(hit, found - skip, -1)
        place_ref[...] = jnp.where(place < cols, place, -1)


def finish_kernel(mine_ref, partner_ref, mine_place_ref, partner_place_ref, out_ref):
    wire = mine_ref.shape[1]
    sources = [mine_ref[...], partner_ref[...]]
    for block in range(13):
        spread = jnp.zeros((8, 128), jnp.float32)
        for place_ref, source in zip((mine_place_ref, partner_place_ref), sources):
            at = jnp.broadcast_to(place_ref[block : block + 1, :], (8, 128))
            for k in range(wire // 128):
                moved = jnp.take_along_axis(source[:, k * 128 : (k + 1) * 128], at & 127, axis=1)
                spread = jnp.where(at >> 7 == k, moved, spread)
        held = min(128, IJ - block * 128)
        out_ref[:, block * 128 : block * 128 + held] = spread[:, :held]


def shaped(shape, dtype):
    return jax.ShapeDtypeStruct(shape, dtype)


def body(integrals, amplitudes, ab_irrep, cd_irrep, occ_irrep):
    bf16, f32, i32 = jnp.bfloat16, jnp.float32, jnp.int32
    width = WIDE * TW
    chooser = pltpu.VMEM((16 * TW, width), bf16)
    numbers = pltpu.SMEM((IRREPS,), i32)

    def over_chips(sent):
        got = lax.all_to_all(sent, CHIPS, split_axis=0, concat_axis=0, tiled=True)
        return got.reshape(sent.shape[0] * sent.shape[1], sent.shape[2])

    def swapped(array):
        return lax.ppermute(array, "blk_2", [(0, 1), (1, 0)])

    def gathered_full(turn):
        sent = pl.pallas_call(
            functools.partial(send_full_kernel, turn),
            out_shape=shaped((SOURCES, FULL, width), bf16),
            in_specs=[VMEM, SMEM, SMEM],
            out_specs=VMEM,
            scratch_shapes=[chooser],
            compiler_params=GRANT,
        )(amplitudes, cd_irrep, occ_irrep)
        return over_chips(sent)

    def weights(turn, first, irreps):
        mine = pl.pallas_call(
            functools.partial(pack_rows_kernel, turn, first),
            out_shape=shaped((4 * TW + 8, width), bf16),
            in_specs=[VMEM, SMEM, SMEM],
            out_specs=VMEM,
            scratch_shapes=[chooser],
            compiler_params=GRANT,
        )(integrals, irreps, cd_irrep)
        return [mine, swapped(mine)]

    sent = pl.pallas_call(
        send_kernel,
        out_shape=shaped((SOURCES, ROWS, NARROW * TW), bf16),
        in_specs=[VMEM, SMEM, SMEM],
        out_specs=VMEM,
        scratch_shapes=[chooser, numbers],
        compiler_params=GRANT,
        name="send",
    )(amplitudes, cd_irrep, occ_irrep)
    held = over_chips(sent)

    number = np.arange(16 * 128, dtype=np.int32).reshape(16, 128)
    real, source = number < IJ, number // PAIRS

    def orbital_irrep(which):
        orbital = lax.broadcasted_iota(i32, (OCC, 16, 128), 0)
        hit = orbital == jnp.asarray(which)[None]
        return jnp.sum(jnp.where(hit, occ_irrep[:, None, None], 0), axis=0)

    irrep = jnp.bitwise_xor(orbital_irrep(number // OCC), orbital_irrep(number % OCC))
    kinds = jnp.asarray(np.where(real, source % 2 * IRREPS, 4 * IRREPS), dtype=i32)
    pairs = irrep + kinds
    numbered = np.arange(2 * IRREPS, dtype=np.int32)
    counts = jnp.sum((pairs == numbered[:, None, None]).astype(i32), axis=(1, 2))
    tiles = jnp.sum((cd_irrep == numbered[:IRREPS, None]).astype(i32), axis=1)
    need = (tiles + NARROW - 1) // NARROW
    alike = irrep == numbered[:IRREPS, None, None]
    taken = jnp.sum(jnp.where(alike, need[:, None, None], 0), axis=0)
    theirs = jnp.asarray(source)[None] == lax.broadcasted_iota(i32, (32, 16, 128), 0)
    rows = jnp.sum(jnp.where(theirs, taken, 0), axis=(1, 2))

    first_weights = weights(0, 0, ab_irrep)

    pair_list, choices = pl.pallas_call(
        list_kernel,
        out_shape=[shaped((LIST,), i32), shaped((4,), i32)],
        in_specs=[SMEM] * 5,
        out_specs=[SMEM] * 2,
        scratch_shapes=[numbers] * 2,
        compiler_params=GRANT,
        name="list",
    )(cd_irrep, occ_irrep, counts, rows, ab_irrep)
    chosen, general, most = choices[0], choices[1] > 0, choices[2]

    def products(full, wire, which, operands, rows_list):
        rows = SOURCES * (FULL if full else ROWS)
        return pl.pallas_call(
            functools.partial(product_kernel, full),
            out_shape=pltpu.VMEM((32, 16, wire), f32),
            in_specs=[SMEM] + [VMEM] * len(operands) + [SMEM],
            out_specs=VMEM,
            scratch_shapes=[pltpu.VMEM((rows, 128), f32)] * 4
            + [pltpu.VMEM((wire, 128), f32), pltpu.VMEM((8 * TW, wire), f32)],
            compiler_params=LARGE,
        )(which, *operands, rows_list)

    def full_products(wire, which):
        rows_list = pl.pallas_call(
            full_list_kernel,
            out_shape=shaped((LIST,), i32),
            in_specs=[SMEM] * 2,
            out_specs=SMEM,
            scratch_shapes=[numbers],
            compiler_params=GRANT,
            name="full_list",
        )(occ_irrep, pair_list)
        operands = [gathered_full(0), gathered_full(1), *first_weights, *weights(1, 16, pair_list)]
        return products(True, wire, which, operands, rows_list)

    def reduced(wire, which):
        partial = lax.cond(
            general,
            lambda: full_products(wire, which),
            lambda: products(False, wire, which, [held, *first_weights], pair_list),
        ).astype(jnp.float16)
        arrived = lax.all_to_all(partial, "panel", split_axis=0, concat_axis=0, tiled=True)
        mine, partners = pl.pallas_call(
            sum_kernel,
            out_shape=[shaped((8, wire), f32)] * 2,
            in_specs=[VMEM],
            out_specs=[VMEM] * 2,
            compiler_params=GRANT,
            name="sum",
        )(arrived.astype(f32))
        spots = pl.pallas_call(
            functools.partial(places_kernel, wire - 1),
            out_shape=[shaped((16, 128), i32)] * 2,
            in_specs=[SMEM, SMEM, VMEM],
            out_specs=[VMEM] * 2,
            compiler_params=GRANT,
            name="places",
        )(which, pair_list, pairs)
        theirs = swapped(partners)
        return pl.pallas_call(
            finish_kernel,
            out_shape=shaped((8, IJ), f32),
            in_specs=[VMEM] * 4,
            out_specs=VMEM,
            compiler_params=GRANT,
            name="finish",
        )(mine, theirs, *spots)

    zero = jnp.zeros((1,), i32)

    def all_rounds():
        cols = LONG - 1

        def add_round(number, total):
            which = jnp.full((1,), number, i32)
            return total + reduced(LONG, which)

        return lax.fori_loop(0, (most + cols - 1) // cols, add_round, jnp.zeros((8, IJ), f32))

    branches = [functools.partial(reduced, wire, zero) for wire in WIRES]
    return lax.switch(chosen, [*branches, all_rounds])


def solution(mesh):
    split = Mesh(
        mesh.devices.reshape(2, 8, 2, mesh.shape["panel"]), ("blk_0", "blk_1", "blk_2", "panel")
    )
    return jax.shard_map(
        body,
        mesh=split,
        in_specs=(P(BLK, "panel"), P(BLK, "panel"), P(BLK), P("panel"), P()),
        out_specs=P(BLK_PANEL, None),
        check_vma=False,
    )
```
